32 devices in a mesh: tile: 4 (over y, core), tm: 8 (over z, x).
Axes of the slice: x: 2, y: 2, z: 4, core: 2. Of those that a mesh axis runs over, the one named last changes fastest.
Arguments:
- pixels: bfloat16 [192, 16, 64, 256], P(('tile', 'tm')), may hold values from -6 to 6
- slot_tile: int32 [192], replicated, may hold values from -1 to 95, as said below
- w_space: bfloat16 [3, 3, 256, 512], replicated, may hold values from -0.125 to 0.125
- b_space: float32 [512], replicated, may hold values from -3 to 3
- w_time: bfloat16 [3, 512, 512], replicated, may hold values from -0.15625 to 0.15625
- b_time: float32 [512], replicated, may hold values from -3 to 3
- gain: float32 [512], replicated, may hold values from 0.1 to 1.9
Outputs:
- latent: bfloat16 [96, 16, 16, 512], P('tile', 'tm')
The draws below stay inside these ranges and needn't reach their ends.
Inputs may be any that keep to these rules, and one draw needn't show every extreme that they name: `slot_tile`: every tile id 0..95 stands in exactly one slot, -1 marks an empty slot. On each device (the 6 slots of one device in order) the live slots come first; the devices form aligned blocks of four consecutive devices whose live slots number 2 * 3, 3, 3 and 0 in some order. A group is 24 consecutive tile ids (tile id // 24); at most 2 slots of one device hold tiles of one group, and some device holds exactly 2 of one group.
All inputs are finite; a program needn't handle non-finite values.
Results may differ from the reference program's by a relative error of at most 0.0044.
Values may be sent and summed in bfloat16 or wider, within the bound.
A program may use at most 64 MiB of HBM per device.

```python
import jax
import jax.numpy as jnp
from jax import lax

C_IN = 256
C_OUT = 512
TILE_SIDE = 8
TILE_DEV = 3
PIX = 64
CAP = 6
SLOTS = 192
TILES = 96
GROUP_TILES = 24
FRAMES = 16
N_TILE = 4
DEVICES = 32


def draw_slot_tile(key, part):
    key_loads, key_order, key_turn = jax.random.split(key, 3)
    block_count = DEVICES // 4
    pattern = jnp.array([2, 1, 1, 0], jnp.int32) * TILE_DEV
    block_keys = jax.random.split(key_loads, block_count)
    shuffles = jax.vmap(lambda block_key: jax.random.permutation(block_key, 4))(block_keys)
    loads = pattern[shuffles].reshape(DEVICES)
    offsets = jnp.cumsum(loads) - loads
    member_order = jax.random.permutation(key_order, GROUP_TILES).astype(jnp.int32)
    turn = jax.random.randint(key_turn, (), 0, N_TILE)
    slot_pos = jnp.arange(CAP, dtype=jnp.int32)
    sequence = offsets[:, None] + slot_pos[None, :]
    sequence = jnp.minimum(sequence, TILES - 1)
    group_of = (sequence % N_TILE + turn) % N_TILE
    tile_id = group_of * GROUP_TILES + member_order[sequence // N_TILE]
    result = jnp.where(slot_pos[None, :] < loads[:, None], tile_id, -1)
    return result.reshape(SLOTS).astype(jnp.int32)


def block_scale(rng, extent, cuts, low, high):
    level = 1.0
    for dim, blocks in cuts:
        steps = jax.random.uniform(jax.random.fold_in(jax.random.fold_in(rng, 6), dim), (blocks,), jnp.float32, low / len(cuts), high / len(cuts))
        level = level * jnp.repeat(jnp.exp(steps), extent[dim] // blocks).reshape((-1,) + (1,) * (len(extent) - 1 - dim))
    return level


def normal_values(key, extent, scale, reach, pieces=(), kind=jnp.bfloat16):
    level = block_scale(key, extent, pieces, -0.22, 0.18) if pieces else 1.0
    drawn = jax.random.normal(key, extent, jnp.float32) * scale * level
    return jnp.minimum(jnp.maximum(drawn, -reach), reach).astype(kind)


def setup_inputs(seed: int = 0) -> dict:
    streams_of = jax.random.split(jax.random.key(seed), 8)
    return {
        "pixels": normal_values(streams_of[0], (SLOTS, FRAMES, PIX, C_IN), 1.0, 6.0, ((0, 32),)),
        "slot_tile": draw_slot_tile(jax.random.fold_in(streams_of[7], 71), 0),
        "w_space": normal_values(streams_of[2], (3, 3, C_IN, C_OUT), (9 * C_IN) ** -0.5, 0.125),
        "b_space": normal_values(streams_of[3], (C_OUT,), 0.5, 3.0, (), jnp.float32),
        "w_time": normal_values(streams_of[4], (3, C_OUT, C_OUT), (3 * C_OUT) ** -0.5, 0.15625),
        "b_time": normal_values(streams_of[5], (C_OUT,), 0.5, 3.0, (), jnp.float32),
        "gain": jnp.clip(1.0 + 0.18 * jax.random.normal(streams_of[6], (C_OUT,), jnp.float32), 0.1, 1.9),
    }


def conv_space(raw_tiles, w_space, b_space):
    number, frames, pix_count, channels = raw_tiles.shape
    grid = raw_tiles.reshape(number * frames, TILE_SIDE, TILE_SIDE, channels)
    padded = jnp.pad(grid, ((0, 0), (1, 1), (1, 1), (0, 0)))
    half_side = TILE_SIDE // 2
    total = jnp.zeros((number * frames * half_side * half_side, w_space.shape[-1]), jnp.float32)
    for row_tap in range(3):
        for col_tap in range(3):
            patch = padded[:, row_tap:row_tap + TILE_SIDE - 1:2, col_tap:col_tap + TILE_SIDE - 1:2, :]
            total = total + jnp.dot(patch.reshape(-1, channels), w_space[row_tap, col_tap], preferred_element_type=jnp.float32)
    active = jax.nn.silu(total + b_space.astype(jnp.float32))
    return active.astype(jnp.bfloat16).reshape(number, frames, half_side * half_side, -1)

def mix_time(extended, w_time, b_time, gain):
    number, all_frames, positions, channels = extended.shape
    frames = all_frames - 2
    total = jnp.zeros((number * frames * positions, channels), jnp.float32) + b_time.astype(jnp.float32)
    for lag in range(3):
        segment = extended[:, 2 - lag:2 - lag + frames].reshape(-1, channels)
        total = total + jnp.dot(segment, w_time[lag], preferred_element_type=jnp.float32)
    mixed = extended[:, 2:].reshape(-1, channels).astype(jnp.float32) + total
    scale = lax.rsqrt(lax.optimization_barrier(jnp.mean(mixed * mixed, axis=-1, keepdims=True)) + 1e-06)
    return (mixed * scale * gain.astype(jnp.float32)).astype(jnp.bfloat16).reshape(number, frames, positions, channels)

def reference(pixels, slot_tile, w_space, b_space, w_time, b_time, gain):
    slot_count = pixels.shape[0]
    position = jnp.where(slot_tile >= 0, slot_tile, TILES).astype(jnp.int32)
    order = jnp.zeros((TILES + 1,), jnp.int32).at[position].set(jnp.arange(slot_count, dtype=jnp.int32))[:TILES]

    def encode(slot_index):
        raw_tile = lax.dynamic_index_in_dim(pixels, slot_index, 0, keepdims=True)
        spatial = conv_space(raw_tile, w_space, b_space)
        extended = jnp.pad(spatial, ((0, 0), (2, 0), (0, 0), (0, 0)))
        return mix_time(extended, w_time, b_time, gain)[0]
    return lax.map(encode, order)
```

```python
import functools

import jax
import jax.numpy as jnp
from jax import lax
from jax.experimental import pallas as pl
from jax.experimental.pallas import tpu as pltpu
from jax.sharding import PartitionSpec as P

TILE_SIDE = 8
HALF = 4
BASE = 3


def conv_space(raw_tiles, w_space, b_space):
    number, frames, pix_count, channels = raw_tiles.shape
    grid = raw_tiles.reshape(number * frames, TILE_SIDE, TILE_SIDE, channels)
    total = lax.conv_general_dilated(
        grid,
        w_space,
        (2, 2),
        ((1, 1), (1, 1)),
        dimension_numbers=("NHWC", "HWIO", "NHWC"),
        preferred_element_type=jnp.float32,
    )
    active = jax.nn.silu(total + b_space)
    half_side = TILE_SIDE // 2
    return active.astype(jnp.bfloat16).reshape(number, frames, half_side * half_side, -1)


def tables(slot_tile, rows, groups, bucket, group_tiles, my_row):
    table = slot_tile.reshape(rows, -1)
    width = table.shape[1]
    group_of = jnp.where(table >= 0, lax.div(table, group_tiles), groups)
    pos = jnp.arange(width, dtype=jnp.int32)
    earlier = pos[None, :] < pos[:, None]
    same = (group_of[:, :, None] == group_of[:, None, :]) & earlier[None]
    rank = jnp.sum(same.astype(jnp.int32), axis=2)
    target = group_of * bucket + rank
    own_target = lax.dynamic_index_in_dim(target, my_row, 0, keepdims=False)
    own_live = lax.dynamic_index_in_dim(table, my_row, 0, keepdims=False) >= 0
    own_target = jnp.where(own_live, own_target, -1)
    places = jnp.arange(groups * bucket, dtype=jnp.int32)
    send_idx = jnp.sum(
        jnp.where(own_target[None, :] == places[:, None], pos[None, :], 0), axis=1
    )
    wanted = my_row * group_tiles + jnp.arange(group_tiles, dtype=jnp.int32)
    arrived = jnp.arange(rows, dtype=jnp.int32)[:, None] * bucket + rank
    pick_idx = jnp.sum(
        jnp.where(
            table.reshape(-1)[None, :] == wanted[:, None], arrived.reshape(-1)[None, :], 0
        ),
        axis=1,
    )
    return send_idx, pick_idx


def kernel(
    rows, slabs, cap, bucket, group_tiles,
    send_idx, pick_idx, src, w_time, b_time, gain, out,
    got1a, got1b, out2, got2a, got2b, feats, halo, total,
    send1, recv1, send2, recv2, send3, recv3,
):
    frames = 2
    got1, got2 = (got1a, got1b), (got2a, got2b)
    row = lax.axis_index("tile")
    slab = lax.axis_index("tm")
    barrier = pltpu.get_barrier_semaphore()
    for k in range(1, slabs):
        pl.semaphore_signal(barrier, inc=1, device_id={"tm": lax.rem(slab + k, slabs)})
    for k in range(1, rows):
        pl.semaphore_signal(barrier, inc=1, device_id={"tile": lax.rem(row + k, rows)})
    pl.semaphore_wait(barrier, slabs + rows - 2)

    def copy1(f, k):
        to = lax.rem(slab + k, slabs)
        return pltpu.make_async_remote_copy(
            src_ref=src.at[:, to * frames + f],
            dst_ref=got1[f].at[pl.ds(slab * cap, cap)],
            send_sem=send1.at[f, k - 1],
            recv_sem=recv1.at[f, k - 1],
            device_id={"tm": to},
        )

    def copy2(f, k):
        to = lax.rem(row + k, rows)
        return pltpu.make_async_remote_copy(
            src_ref=out2.at[f, pl.ds(to * bucket, bucket)],
            dst_ref=got2[f].at[pl.ds(row * bucket, bucket)],
            send_sem=send2.at[f, k - 1],
            recv_sem=recv2.at[f, k - 1],
            device_id={"tile": to},
        )

    def copy3(f):
        return pltpu.make_async_remote_copy(
            src_ref=feats.at[f],
            dst_ref=halo.at[f],
            send_sem=send3.at[f],
            recv_sem=recv3.at[f],
            device_id={"tm": lax.rem(slab + 1, slabs)},
        )

    for f in range(frames):
        for k in range(1, slabs):
            copy1(f, k).start()
    for f in range(frames):
        got1[f][pl.ds(slab * cap, cap)] = src[:, slab * frames + f]
        for k in range(1, slabs):
            copy1(f, k).wait_recv()

        @pl.loop(0, rows * bucket)
        def _(i):
            out2[f, i] = got1[f][send_idx[i]]

        for k in range(1, rows):
            copy2(f, k).start()

        @pl.loop(0, bucket)
        def _(j):
            got2[f][row * bucket + j] = got1[f][send_idx[row * bucket + j]]

        for k in range(1, rows):
            copy2(f, k).wait_recv()

        @pl.loop(0, group_tiles)
        def _(i):
            feats[f, i] = got2[f][pick_idx[i]]

        @pl.when(slab < slabs - 1)
        def _():
            copy3(f).start()

    part = group_tiles // 2
    height = part * 16

    def flat(value):
        return value.reshape(height, value.shape[-1])

    @pl.loop(0, 2)
    def _(c):
        at = pl.ds(c * part, part)
        own = [flat(feats[0, at]), flat(feats[1, at])]
        for f in range(frames):
            mixed = own[f].astype(jnp.float32) + b_time[...]
            for lag in range(f + 1):
                mixed = mixed + jnp.dot(
                    own[f - lag], w_time[lag], preferred_element_type=jnp.float32
                )
            total[f, c] = mixed

    for f in range(frames):

        @pl.when(slab > 0)
        def _():
            copy3(f).wait_recv()

        @pl.when(slab == 0)
        def _():
            halo[f] = jnp.zeros(halo.shape[1:], halo.dtype)

    @pl.loop(0, 2)
    def _(c):
        at = pl.ds(c * part, part)
        before = [flat(halo[0, at]), flat(halo[1, at])]
        for f in range(frames):
            mixed = total[f, c]
            for lag in range(f + 1, 3):
                mixed = mixed + jnp.dot(
                    before[2 + f - lag], w_time[lag], preferred_element_type=jnp.float32
                )
            scale = lax.rsqrt(jnp.mean(mixed * mixed, axis=-1, keepdims=True) + 1e-06)
            value = (mixed * scale * gain[...]).astype(jnp.bfloat16)
            out[at, f] = value.reshape(part, 16, value.shape[-1])

    for f in range(frames):
        for k in range(1, slabs):
            copy1(f, k).wait_send()
        for k in range(1, rows):
            copy2(f, k).wait_send()

        @pl.when(slab < slabs - 1)
        def _():
            copy3(f).wait_send()


def body(rows, slabs, pixels, slot_tile, w_space, b_space, w_time, b_time, gain):
    cap, all_frames = pixels.shape[:2]
    channels = w_space.shape[-1]
    group_tiles = cap // 2 * slabs
    per_group = (cap + rows - 1) // rows
    bucket = per_group * 3 * (slabs // 4)
    frames = all_frames // slabs
    send_idx, pick_idx = tables(
        slot_tile, rows, rows, bucket, group_tiles, lax.axis_index("tile")
    )
    spatial = conv_space(pixels, w_space, b_space)
    vmem = pl.BlockSpec(memory_space=pltpu.VMEM)
    smem = pl.BlockSpec(memory_space=pltpu.SMEM)
    bf16 = jnp.bfloat16
    dma = pltpu.SemaphoreType.DMA
    return pl.pallas_call(
        functools.partial(kernel, rows, slabs, cap, bucket, group_tiles),
        out_shape=jax.ShapeDtypeStruct((group_tiles, frames, 16, channels), bf16),
        in_specs=[smem, smem, vmem, vmem, vmem, vmem],
        out_specs=vmem,
        scratch_shapes=[
            pltpu.VMEM((slabs * cap, 16, channels), bf16),
            pltpu.VMEM((slabs * cap, 16, channels), bf16),
            pltpu.VMEM((frames, rows * bucket, 16, channels), bf16),
            pltpu.VMEM((rows * bucket, 16, channels), bf16),
            pltpu.VMEM((rows * bucket, 16, channels), bf16),
            pltpu.VMEM((frames, group_tiles, 16, channels), bf16),
            pltpu.VMEM((frames, group_tiles, 16, channels), bf16),
            pltpu.VMEM((frames, 2, group_tiles * 8, channels), jnp.float32),
            dma((frames, slabs - 1)),
            dma((frames, slabs - 1)),
            dma((frames, rows - 1)),
            dma((frames, rows - 1)),
            dma((frames,)),
            dma((frames,)),
        ],
        compiler_params=pltpu.CompilerParams(collective_id=0, has_side_effects=True),
    )(send_idx, pick_idx, spatial, w_time, b_time[None], gain[None])


def index_tables(slot_tile, rows, cap, bucket, group_tiles, row, half):
    slots = slot_tile.shape[0]
    width = HALF * cap
    ids = jnp.arange(slots, dtype=jnp.int32)
    block = lax.div(ids, width)
    group = jnp.where(slot_tile >= 0, lax.div(slot_tile, group_tiles), rows)
    key = block * (rows + 1) + group
    rank = jnp.sum(
        ((key[None, :] == key[:, None]) & (ids[None, :] < ids[:, None])).astype(jnp.int32), axis=1
    )
    arrival = (lax.rem(block, 2) * rows + lax.div(block, 2)) * bucket + rank
    wanted = row * group_tiles + jnp.arange(group_tiles, dtype=jnp.int32)
    pick = jnp.sum(jnp.where(slot_tile[None, :] == wanted[:, None], arrival[None, :], 0), axis=1)
    inside = lax.rem(ids, width)
    dev, pos = lax.div(inside, cap), lax.rem(inside, cap)
    far_place = jnp.where(pos < BASE, dev * BASE + pos, HALF * BASE + pos - BASE)
    places = jnp.arange(2 * rows * bucket, dtype=jnp.int32)
    near = places < rows * bucket
    want_block = row * 2 + jnp.where(near, half, 1 - half)
    want = want_block * (slots * rows) + lax.rem(places, rows * bucket)
    have = jnp.where(slot_tile >= 0, block * (slots * rows) + group * bucket + rank, -1)
    value = jnp.where(block == row * 2 + half, inside, far_place)
    send = jnp.sum(jnp.where(have[None, :] == want[:, None], value[None, :], 0), axis=1)
    live = (block == row * 2 + half) & (pos == BASE) & (slot_tile >= 0)
    full = jnp.sum(jnp.where(live, dev, 0))
    return send, full[None], pick


def encode(
    rows, slabs, cap, bucket, group_tiles,
    send_idx, full, pick_idx, pixels, w_space, b_space, w_time, b_time, gain,
    out,
    pix, ws, wt, plane, patch, spatial, lat,
    near0, near1, far0, far1, relay0, relay1, relay_out, packed, rec0, rec1,
    in_sem, w_sem, send_a, recv_n, recv_f, send_b, recv_r, send_r, send_y, recv_y,
):
    frames = 2
    near, far, relay, rec = (near0, near1), (far0, far1), (relay0, relay1), (rec0, rec1)
    f32, bf16 = jnp.float32, jnp.bfloat16
    row = lax.axis_index("tile")
    slab = lax.axis_index("tm")
    half = lax.div(slab, HALF)
    mine = lax.rem(slab, HALF)
    first = (1 - half) * HALF
    low = half * HALF
    barrier = pltpu.get_barrier_semaphore()
    for k in range(1, slabs):
        pl.semaphore_signal(barrier, inc=1, device_id={"tm": lax.rem(slab + k, slabs)})
    for k in range(1, rows):
        pl.semaphore_signal(barrier, inc=1, device_id={"tile": lax.rem(row + k, rows)})

    def load(s):
        return pltpu.make_async_copy(
            pixels.at[:, pl.ds(s * frames, frames)], pix.at[s], in_sem.at[s]
        )

    start = lax.rem(first + slabs - 1, slabs)
    load(start).start()
    ws_copy = pltpu.make_async_copy(w_space, ws, w_sem.at[0])
    ws_copy.start()
    load(first).start()
    wt_copy = pltpu.make_async_copy(w_time, wt, w_sem.at[1])
    wt_copy.start()

    @pl.loop(1, slabs - 1)
    def _(k):
        load(lax.rem(first + k, slabs)).start()

    count = frames * cap
    side = TILE_SIDE
    out_side = side // 2
    area = out_side * out_side
    height = count * area
    channels = patch.shape[1] // 9
    lanes = plane.shape[-1]
    for piece in range(channels // lanes):
        plane[1, piece, :, 8:16] = jnp.zeros((count, 8, lanes), f32)
    spatial[pl.ds(0, height)] = jnp.zeros((height, spatial.shape[1]), bf16)
    edge = lax.rem(lax.broadcasted_iota(jnp.int32, (area, lanes), 0), out_side) == 0

    def conv(s):
        load(s).wait()

        @pl.loop(0, cap)
        def _(p):
            for f in range(frames):
                image = f * cap + p
                value = pix[s, p, f].astype(f32).reshape(out_side, 2, side, channels)
                for parity in range(2):
                    rows_of = value[:, parity].reshape(out_side * side, channels)
                    for piece in range(channels // lanes):
                        plane[parity, piece, image, 16:48] = rows_of[
                            :, piece * lanes:(piece + 1) * lanes
                        ]
            for f in range(frames):
                image = f * cap + p
                for a in range(3):
                    parity, base = ((1, 8), (0, 16), (1, 16))[a]
                    for b in range(3):
                        for piece in range(channels // lanes):
                            taken = plane[
                                parity, piece, image, pl.ds(base + b - 1, area, stride=2)
                            ]
                            if b == 0:
                                taken = jnp.where(edge, 0.0, taken)
                            at = (3 * a + b) * channels + piece * lanes
                            patch[
                                pl.ds(pl.multiple_of(image * area, area), area),
                                at:at + lanes,
                            ] = taken.astype(bf16)

        total = jnp.dot(patch[...], ws[...], preferred_element_type=f32) + b_space[...]
        active = total / (1.0 + jnp.exp(-total))
        spatial[pl.ds(pl.multiple_of((s + 1) * height, height), height)] = active.astype(bf16)

    def mix(s):
        base = (s + 1) * height
        step = height // frames
        mixed = spatial[pl.ds(pl.multiple_of(base, step), height)].astype(f32) + b_time[...]
        for lag in range(3):
            mixed = mixed + jnp.dot(
                spatial[pl.ds(pl.multiple_of(base - lag * step, step), height)],
                wt[lag],
                preferred_element_type=f32,
            )
        scale = lax.rsqrt(jnp.mean(mixed * mixed, axis=-1, keepdims=True) + 1e-06)
        value = (mixed * scale * gain[...]).astype(bf16)
        lat[s] = value.reshape(frames, cap, area, value.shape[-1])

    def near_copy(f, j):
        s = low + j
        return pltpu.make_async_remote_copy(
            src_ref=lat.at[s, f],
            dst_ref=near[f].at[pl.ds(mine * cap, cap)],
            send_sem=send_a.at[f, s],
            recv_sem=recv_n.at[f, mine],
            device_id={"tm": s},
        )

    def near_wait(f, j):
        return pltpu.make_async_remote_copy(
            src_ref=lat.at[low + j, f],
            dst_ref=near[f].at[pl.ds(j * cap, cap)],
            send_sem=send_a.at[f, low + j],
            recv_sem=recv_n.at[f, j],
            device_id={"tm": low + j},
        )

    def far_copy(f, j):
        s = first + j
        return pltpu.make_async_remote_copy(
            src_ref=lat.at[s, f, pl.ds(0, BASE)],
            dst_ref=far[f].at[pl.ds(mine * BASE, BASE)],
            send_sem=send_a.at[f, s],
            recv_sem=recv_f.at[f, mine],
            device_id={"tm": s},
        )

    def far_wait(f, j):
        return pltpu.make_async_remote_copy(
            src_ref=lat.at[first + j, f, pl.ds(0, BASE)],
            dst_ref=far[f].at[pl.ds(j * BASE, BASE)],
            send_sem=send_a.at[f, first + j],
            recv_sem=recv_f.at[f, j],
            device_id={"tm": first + j},
        )

    def relay_copy(f, j):
        return pltpu.make_async_remote_copy(
            src_ref=lat.at[first + j, f, pl.ds(BASE, BASE)],
            dst_ref=relay[f].at[pl.ds(mine * BASE, BASE)],
            send_sem=send_b.at[f, j],
            recv_sem=recv_r.at[f, mine],
            device_id={"tm": low + j},
        )

    def relay_wait(f, j):
        return pltpu.make_async_remote_copy(
            src_ref=lat.at[first + j, f, pl.ds(BASE, BASE)],
            dst_ref=relay[f].at[pl.ds(j * BASE, BASE)],
            send_sem=send_b.at[f, j],
            recv_sem=recv_r.at[f, j],
            device_id={"tm": low + j},
        )

    def forward(f):
        return pltpu.make_async_remote_copy(
            src_ref=relay_out.at[f],
            dst_ref=far[f].at[pl.ds(HALF * BASE, BASE)],
            send_sem=send_r.at[f],
            recv_sem=recv_f.at[f, HALF],
            device_id={"tm": first + mine},
        )

    def tile_copy(c, f, k):
        to = lax.rem(row + k, rows)
        part = half if c == 0 else 1 - half
        return pltpu.make_async_remote_copy(
            src_ref=packed.at[c, f, pl.ds(to * bucket, bucket)],
            dst_ref=rec[f].at[pl.ds((part * rows + row) * bucket, bucket)],
            send_sem=send_y.at[c, f, k - 1],
            recv_sem=recv_y.at[c, f, k - 1],
            device_id={"tile": to},
        )

    def send_slab(f, k):
        @pl.when(k < HALF)
        def _():
            j = k
            far_copy(f, j).start()

            @pl.when(j != mine)
            def _():
                relay_copy(f, j).start()

            @pl.when(j == mine)
            def _():
                relay[f][pl.ds(mine * BASE, BASE)] = lat[first + mine, f, BASE:cap]

        @pl.when(k >= HALF)
        def _():
            j = k - HALF

            @pl.when(j != mine)
            def _():
                near_copy(f, j).start()

            @pl.when(j == mine)
            def _():
                near[f][pl.ds(mine * cap, cap)] = lat[slab, f]

    def run_relay(f):
        for k in range(1, HALF):
            relay_wait(f, lax.rem(mine + k, HALF)).wait_recv()
        for i in range(BASE):
            relay_out[f, i] = relay[f][full[0] * BASE + i]
        forward(f).start()

    def run_tiles(c, f):
        if c == 0:
            for k in range(1, HALF):
                near_wait(f, lax.rem(mine + k, HALF)).wait_recv()
        else:
            for j in range(HALF):
                far_wait(f, j).wait_recv()
            forward(f).wait_recv()
        source = near[f] if c == 0 else far[f]

        @pl.loop(0, rows * bucket)
        def _(i):
            packed[c, f, i] = source[send_idx[c * rows * bucket + i]]

        for k in range(1, rows):
            tile_copy(c, f, k).start()
        part = half if c == 0 else 1 - half
        rec[f][pl.ds((part * rows + row) * bucket, bucket)] = packed[
            c, f, pl.ds(row * bucket, bucket)
        ]

    ws_copy.wait()
    conv(start)
    pl.semaphore_wait(barrier, slabs + rows - 2)
    wt_copy.wait()

    @pl.loop(0, slabs)
    def _(k):
        s = lax.rem(first + k, slabs)

        @pl.when(k < slabs - 1)
        def _():
            conv(s)

        mix(s)
        send_slab(0, k)

    @pl.loop(0, slabs)
    def _(k):
        send_slab(1, k)

    run_relay(0)
    run_tiles(0, 0)
    run_relay(1)
    run_tiles(1, 0)
    run_tiles(0, 1)
    run_tiles(1, 1)

    for f in range(frames):
        for c in range(2):
            for k in range(1, rows):
                tile_copy(c, f, k).wait_recv()

        @pl.loop(0, group_tiles)
        def _(i):
            out[i, f] = rec[f][pick_idx[i]]

    for f in range(frames):
        for k in range(1, HALF):
            j = lax.rem(mine + k, HALF)
            near_copy(f, j).wait_send()
            relay_copy(f, j).wait_send()
        for j in range(HALF):
            far_copy(f, j).wait_send()
        forward(f).wait_send()
        for c in range(2):
            for k in range(1, rows):
                tile_copy(c, f, k).wait_send()


def body_two_blocks(rows, slabs, pixels, slot_tile, w_space, b_space, w_time, b_time, gain):
    cap, all_frames, pix_count, channels = pixels.shape
    features = w_space.shape[-1]
    frames = all_frames // slabs
    group_tiles = cap // 2 * slabs
    per_group = (cap + rows - 1) // rows
    bucket = per_group * 3
    row = lax.axis_index("tile")
    half = lax.div(lax.axis_index("tm"), HALF)
    send_idx, full, pick_idx = index_tables(
        slot_tile, rows, cap, bucket, group_tiles, row, half
    )
    area = pix_count // 4
    count = frames * cap
    height = count * area
    vmem = pl.BlockSpec(memory_space=pltpu.VMEM)
    smem = pl.BlockSpec(memory_space=pltpu.SMEM)
    hbm = pl.BlockSpec(memory_space=pl.ANY)
    bf16, f32 = jnp.bfloat16, jnp.float32
    dma = pltpu.SemaphoreType.DMA

    def held(*lead):
        return pltpu.VMEM(lead + (area, features), bf16)

    return pl.pallas_call(
        functools.partial(encode, rows, slabs, cap, bucket, group_tiles),
        out_shape=jax.ShapeDtypeStruct((group_tiles, frames, area, features), bf16),
        in_specs=[smem, smem, smem, hbm, hbm, vmem, hbm, vmem, vmem],
        out_specs=vmem,
        scratch_shapes=[
            pltpu.VMEM((slabs, cap, frames, pix_count, channels), bf16),
            pltpu.VMEM((9 * channels, features), bf16),
            pltpu.VMEM((3, features, features), bf16),
            pltpu.VMEM((2, channels // 128, count, 48, 128), f32),
            pltpu.VMEM((height, 9 * channels), bf16),
            pltpu.VMEM(((slabs + 1) * height, features), bf16),
            held(slabs, frames, cap),
            held(HALF * cap), held(HALF * cap),
            held(HALF * BASE + BASE), held(HALF * BASE + BASE),
            held(HALF * BASE), held(HALF * BASE),
            held(frames, BASE),
            held(2, frames, rows * bucket),
            held(2 * rows * bucket), held(2 * rows * bucket),
            dma((slabs,)), dma((2,)),
            dma((frames, slabs)), dma((frames, HALF)), dma((frames, HALF + 1)),
            dma((frames, HALF)), dma((frames, HALF)), dma((frames,)),
            dma((2, frames, rows - 1)), dma((2, frames, rows - 1)),
        ],
        compiler_params=pltpu.CompilerParams(
            collective_id=1, has_side_effects=True, vmem_limit_bytes=48 << 20
        ),
    )(
        send_idx, full, pick_idx, pixels, w_space.reshape(9 * channels, features),
        b_space[None], w_time, b_time[None], gain[None],
    )


def solution(mesh):
    rows, slabs = mesh.shape["tile"], mesh.shape["tm"]
    plan = body_two_blocks if slabs == 2 * HALF else body
    return jax.shard_map(
        functools.partial(plan, rows, slabs),
        mesh=mesh,
        in_specs=(P(("tile", "tm"), None, None, None), P(), P(), P(), P(), P(), P()),
        out_specs=P("tile", "tm", None, None),
        check_vma=False,
    )
```

```python
import functools

import jax
import jax.numpy as jnp
from jax import lax
from jax.experimental import pallas as pl
from jax.experimental.pallas import tpu as pltpu
from jax.sharding import PartitionSpec as P

TILE_SIDE = 8
HALF = 4
BASE = 3


def conv_space(raw_tiles, w_space, b_space):
    number, frames, pix_count, channels = raw_tiles.shape
    grid = raw_tiles.reshape(number * frames, TILE_SIDE, TILE_SIDE, channels)
    total = lax.conv_general_dilated(
        grid,
        w_space,
        (2, 2),
        ((1, 1), (1, 1)),
        dimension_numbers=("NHWC", "HWIO", "NHWC"),
        preferred_element_type=jnp.float32,
    )
    active = jax.nn.silu(total + b_space)
    half_side = TILE_SIDE // 2
    return active.astype(jnp.bfloat16).reshape(number, frames, half_side * half_side, -1)


def tables(slot_tile, rows, groups, bucket, group_tiles, my_row):
    table = slot_tile.reshape(rows, -1)
    width = table.shape[1]
    group_of = jnp.where(table >= 0, lax.div(table, group_tiles), groups)
    pos = jnp.arange(width, dtype=jnp.int32)
    earlier = pos[None, :] < pos[:, None]
    same = (group_of[:, :, None] == group_of[:, None, :]) & earlier[None]
    rank = jnp.sum(same.astype(jnp.int32), axis=2)
    target = group_of * bucket + rank
    own_target = lax.dynamic_index_in_dim(target, my_row, 0, keepdims=False)
    own_live = lax.dynamic_index_in_dim(table, my_row, 0, keepdims=False) >= 0
    own_target = jnp.where(own_live, own_target, -1)
    places = jnp.arange(groups * bucket, dtype=jnp.int32)
    send_idx = jnp.sum(
        jnp.where(own_target[None, :] == places[:, None], pos[None, :], 0), axis=1
    )
    wanted = my_row * group_tiles + jnp.arange(group_tiles, dtype=jnp.int32)
    arrived = jnp.arange(rows, dtype=jnp.int32)[:, None] * bucket + rank
    pick_idx = jnp.sum(
        jnp.where(
            table.reshape(-1)[None, :] == wanted[:, None], arrived.reshape(-1)[None, :], 0
        ),
        axis=1,
    )
    return send_idx, pick_idx


def kernel(
    rows, slabs, cap, bucket, group_tiles,
    send_idx, pick_idx, src, w_time, b_time, gain, out,
    got1a, got1b, out2, got2a, got2b, feats, halo, total,
    send1, recv1, send2, recv2, send3, recv3,
):
    frames = 2
    got1, got2 = (got1a, got1b), (got2a, got2b)
    row = lax.axis_index("tile")
    slab = lax.axis_index("tm")
    barrier = pltpu.get_barrier_semaphore()
    for k in range(1, slabs):
        pl.semaphore_signal(barrier, inc=1, device_id={"tm": lax.rem(slab + k, slabs)})
    for k in range(1, rows):
        pl.semaphore_signal(barrier, inc=1, device_id={"tile": lax.rem(row + k, rows)})
    pl.semaphore_wait(barrier, slabs + rows - 2)

    def copy1(f, k):
        to = lax.rem(slab + k, slabs)
        return pltpu.make_async_remote_copy(
            src_ref=src.at[:, to * frames + f],
            dst_ref=got1[f].at[pl.ds(slab * cap, cap)],
            send_sem=send1.at[f, k - 1],
            recv_sem=recv1.at[f, k - 1],
            device_id={"tm": to},
        )

    def copy2(f, k):
        to = lax.rem(row + k, rows)
        return pltpu.make_async_remote_copy(
            src_ref=out2.at[f, pl.ds(to * bucket, bucket)],
            dst_ref=got2[f].at[pl.ds(row * bucket, bucket)],
            send_sem=send2.at[f, k - 1],
            recv_sem=recv2.at[f, k - 1],
            device_id={"tile": to},
        )

    def copy3(f):
        return pltpu.make_async_remote_copy(
            src_ref=feats.at[f],
            dst_ref=halo.at[f],
            send_sem=send3.at[f],
            recv_sem=recv3.at[f],
            device_id={"tm": lax.rem(slab + 1, slabs)},
        )

    for f in range(frames):
        for k in range(1, slabs):
            copy1(f, k).start()
    for f in range(frames):
        got1[f][pl.ds(slab * cap, cap)] = src[:, slab * frames + f]
        for k in range(1, slabs):
            copy1(f, k).wait_recv()

        @pl.loop(0, rows * bucket)
        def _(i):
            out2[f, i] = got1[f][send_idx[i]]

        for k in range(1, rows):
            copy2(f, k).start()

        @pl.loop(0, bucket)
        def _(j):
            got2[f][row * bucket + j] = got1[f][send_idx[row * bucket + j]]

        for k in range(1, rows):
            copy2(f, k).wait_recv()

        @pl.loop(0, group_tiles)
        def _(i):
            feats[f, i] = got2[f][pick_idx[i]]

        @pl.when(slab < slabs - 1)
        def _():
            copy3(f).start()

    part = group_tiles // 2
    height = part * 16

    def flat(value):
        return value.reshape(height, value.shape[-1])

    @pl.loop(0, 2)
    def _(c):
        at = pl.ds(c * part, part)
        own = [flat(feats[0, at]), flat(feats[1, at])]
        for f in range(frames):
            mixed = own[f].astype(jnp.float32) + b_time[...]
            for lag in range(f + 1):
                mixed = mixed + jnp.dot(
                    own[f - lag], w_time[lag], preferred_element_type=jnp.float32
                )
            total[f, c] = mixed

    for f in range(frames):

        @pl.when(slab > 0)
        def _():
            copy3(f).wait_recv()

        @pl.when(slab == 0)
        def _():
            halo[f] = jnp.zeros(halo.shape[1:], halo.dtype)

    @pl.loop(0, 2)
    def _(c):
        at = pl.ds(c * part, part)
        before = [flat(halo[0, at]), flat(halo[1, at])]
        for f in range(frames):
            mixed = total[f, c]
            for lag in range(f + 1, 3):
                mixed = mixed + jnp.dot(
                    before[2 + f - lag], w_time[lag], preferred_element_type=jnp.float32
                )
            scale = lax.rsqrt(jnp.mean(mixed * mixed, axis=-1, keepdims=True) + 1e-06)
            value = (mixed * scale * gain[...]).astype(jnp.bfloat16)
            out[at, f] = value.reshape(part, 16, value.shape[-1])

    for f in range(frames):
        for k in range(1, slabs):
            copy1(f, k).wait_send()
        for k in range(1, rows):
            copy2(f, k).wait_send()

        @pl.when(slab < slabs - 1)
        def _():
            copy3(f).wait_send()


def body(rows, slabs, pixels, slot_tile, w_space, b_space, w_time, b_time, gain):
    cap, all_frames = pixels.shape[:2]
    channels = w_space.shape[-1]
    group_tiles = cap // 2 * slabs
    per_group = (cap + rows - 1) // rows
    bucket = per_group * 3 * (slabs // 4)
    frames = all_frames // slabs
    send_idx, pick_idx = tables(
        slot_tile, rows, rows, bucket, group_tiles, lax.axis_index("tile")
    )
    spatial = conv_space(pixels, w_space, b_space)
    vmem = pl.BlockSpec(memory_space=pltpu.VMEM)
    smem = pl.BlockSpec(memory_space=pltpu.SMEM)
    bf16 = jnp.bfloat16
    dma = pltpu.SemaphoreType.DMA
    return pl.pallas_call(
        functools.partial(kernel, rows, slabs, cap, bucket, group_tiles),
        out_shape=jax.ShapeDtypeStruct((group_tiles, frames, 16, channels), bf16),
        in_specs=[smem, smem, vmem, vmem, vmem, vmem],
        out_specs=vmem,
        scratch_shapes=[
            pltpu.VMEM((slabs * cap, 16, channels), bf16),
            pltpu.VMEM((slabs * cap, 16, channels), bf16),
            pltpu.VMEM((frames, rows * bucket, 16, channels), bf16),
            pltpu.VMEM((rows * bucket, 16, channels), bf16),
            pltpu.VMEM((rows * bucket, 16, channels), bf16),
            pltpu.VMEM((frames, group_tiles, 16, channels), bf16),
            pltpu.VMEM((frames, group_tiles, 16, channels), bf16),
            pltpu.VMEM((frames, 2, group_tiles * 8, channels), jnp.float32),
            dma((frames, slabs - 1)),
            dma((frames, slabs - 1)),
            dma((frames, rows - 1)),
            dma((frames, rows - 1)),
            dma((frames,)),
            dma((frames,)),
        ],
        compiler_params=pltpu.CompilerParams(collective_id=0, has_side_effects=True),
    )(send_idx, pick_idx, spatial, w_time, b_time[None], gain[None])


def index_row(tiles, rows, cap, bucket, group_tiles, row, half):
    slots = tiles.shape[1]
    width = HALF * cap
    shape = (slots, slots)
    along = lax.broadcasted_iota(jnp.int32, shape, 1)
    down = lax.broadcasted_iota(jnp.int32, shape, 0)
    spread = jnp.broadcast_to(tiles, shape)
    column = jnp.sum(jnp.where(along == down, spread, 0), axis=1, keepdims=True)

    def key_of(ids, tile):
        key = jnp.where(tile < 0, rows, 0)
        for k in range(1, rows):
            key = key + jnp.where(tile >= k * group_tiles, 1, 0)
        block = jnp.zeros_like(ids)
        for k in range(1, slots // width):
            block = block + jnp.where(ids >= k * width, 1, 0)
        return block, key

    ids = lax.broadcasted_iota(jnp.int32, (slots, 1), 0)
    block, group = key_of(ids, column)
    lane = lax.broadcasted_iota(jnp.int32, (1, slots), 1)
    block_r, group_r = key_of(lane, tiles)
    same = (block * (rows + 1) + group) == (block_r * (rows + 1) + group_r)
    rank = jnp.sum(jnp.where(same & (along < down), 1, 0), axis=1, keepdims=True)
    part = block % 2
    arrival = (part * rows + block // 2) * bucket + rank
    inside = ids - block * width
    dev = jnp.zeros_like(ids)
    for k in range(1, HALF):
        dev = dev + jnp.where(inside >= k * cap, 1, 0)
    pos = inside - dev * cap
    far_place = jnp.where(pos < BASE, dev * BASE + pos, HALF * BASE + pos - BASE)
    mine = block == row * 2 + half
    other = block == row * 2 + 1 - half
    live = column >= 0
    value = jnp.where(mine, inside, far_place)
    places = rows * bucket
    target = jnp.where(
        live & (mine | other), group * bucket + rank + jnp.where(other, places, 0), -1
    )
    place = lax.broadcasted_iota(jnp.int32, (1, 128), 1)
    wanted = jnp.where(
        (place >= 2 * places) & (place < 2 * places + group_tiles),
        place - 2 * places + row * group_tiles,
        -2,
    )
    total = jnp.where(target == place, value, 0) + jnp.where(column == wanted, arrival, 0)
    total = total + jnp.where(
        (mine & live & (pos == BASE)) & (place == 2 * places + group_tiles), dev, 0
    )
    limit = jnp.where(
        place < places,
        width,
        jnp.where(
            place < 2 * places,
            (HALF + 1) * BASE,
            jnp.where(place < 2 * places + group_tiles, 2 * places, HALF),
        ),
    )
    return jnp.minimum(jnp.sum(total, axis=0, keepdims=True), limit - 1)


def encode(
    rows, slabs, cap, bucket, group_tiles,
    slot_tile, pixels, w_space, b_space_h, w_time, b_time_h, gain_h,
    out,
    pix, ws, wt, b_space, b_time, gain, tiles, index_v, index, plane, patch, spatial, lat,
    near0, near1, far0, far1, relay0, relay1, relay_out, packed, rec0, rec1,
    in_sem, w_sem, send_a, recv_n, recv_f, send_b, recv_r, send_r, send_y, recv_y,
):
    frames = 2
    near, far, relay, rec = (near0, near1), (far0, far1), (relay0, relay1), (rec0, rec1)
    f32, bf16 = jnp.float32, jnp.bfloat16
    row = lax.axis_index("tile")
    slab = lax.axis_index("tm")
    half = lax.div(slab, HALF)
    mine = lax.rem(slab, HALF)
    first = (1 - half) * HALF
    low = half * HALF
    barrier = pltpu.get_barrier_semaphore()
    for k in range(1, slabs):
        pl.semaphore_signal(barrier, inc=1, device_id={"tm": lax.rem(slab + k, slabs)})
    for k in range(1, rows):
        pl.semaphore_signal(barrier, inc=1, device_id={"tile": lax.rem(row + k, rows)})

    def load(s):
        return pltpu.make_async_copy(
            pixels.at[:, pl.ds(s * frames, frames)], pix.at[s], in_sem.at[s]
        )

    start = lax.rem(first + slabs - 1, slabs)
    load(start).start()
    small = [
        pltpu.make_async_copy(source, target, w_sem.at[2 + i])
        for i, (source, target) in enumerate(
            ((b_space_h, b_space), (b_time_h, b_time), (gain_h, gain), (slot_tile, tiles))
        )
    ]
    for copy in small:
        copy.start()
    ws_copy = pltpu.make_async_copy(w_space, ws, w_sem.at[0])
    ws_copy.start()
    load(first).start()
    wt_copy = pltpu.make_async_copy(w_time, wt, w_sem.at[1])
    wt_copy.start()

    @pl.loop(1, slabs - 1)
    def _(k):
        load(lax.rem(first + k, slabs)).start()

    count = frames * cap
    side = TILE_SIDE
    out_side = side // 2
    area = out_side * out_side
    height = count * area
    channels = patch.shape[1] // 9
    lanes = plane.shape[-1]
    for piece in range(channels // lanes):
        plane[1, piece, :, 8:16] = jnp.zeros((count, 8, lanes), f32)
    spatial[pl.ds(0, height)] = jnp.zeros((height, spatial.shape[1]), bf16)
    edge = lax.rem(lax.broadcasted_iota(jnp.int32, (area, lanes), 0), out_side) == 0

    def conv(s):
        load(s).wait()

        @pl.loop(0, cap)
        def _(p):
            for f in range(frames):
                image = f * cap + p
                value = pix[s, p, f].astype(f32).reshape(out_side, 2, side, channels)
                for parity in range(2):
                    rows_of = value[:, parity].reshape(out_side * side, channels)
                    for piece in range(channels // lanes):
                        plane[parity, piece, image, 16:48] = rows_of[
                            :, piece * lanes:(piece + 1) * lanes
                        ]
            for f in range(frames):
                image = f * cap + p
                for a in range(3):
                    parity, base = ((1, 8), (0, 16), (1, 16))[a]
                    for b in range(3):
                        for piece in range(channels // lanes):
                            taken = plane[
                                parity, piece, image, pl.ds(base + b - 1, area, stride=2)
                            ]
                            if b == 0:
                                taken = jnp.where(edge, 0.0, taken)
                            at = (3 * a + b) * channels + piece * lanes
                            patch[
                                pl.ds(pl.multiple_of(image * area, area), area),
                                at:at + lanes,
                            ] = taken.astype(bf16)

        total = jnp.dot(patch[...], ws[...], preferred_element_type=f32) + b_space[...]
        active = total / (1.0 + jnp.exp(-total))
        spatial[pl.ds(pl.multiple_of((s + 1) * height, height), height)] = active.astype(bf16)

    def mix(s):
        base = (s + 1) * height
        step = height // frames
        mixed = spatial[pl.ds(pl.multiple_of(base, step), height)].astype(f32) + b_time[...]
        for lag in range(3):
            mixed = mixed + jnp.dot(
                spatial[pl.ds(pl.multiple_of(base - lag * step, step), height)],
                wt[lag],
                preferred_element_type=f32,
            )
        scale = lax.rsqrt(jnp.mean(mixed * mixed, axis=-1, keepdims=True) + 1e-06)
        value = (mixed * scale * gain[...]).astype(bf16)
        lat[s] = value.reshape(frames, cap, area, value.shape[-1])

    def near_copy(f, j):
        s = low + j
        return pltpu.make_async_remote_copy(
            src_ref=lat.at[s, f],
            dst_ref=near[f].at[pl.ds(mine * cap, cap)],
            send_sem=send_a.at[f, s],
            recv_sem=recv_n.at[f, mine],
            device_id={"tm": s},
        )

    def near_wait(f, j):
        return pltpu.make_async_remote_copy(
            src_ref=lat.at[low + j, f],
            dst_ref=near[f].at[pl.ds(j * cap, cap)],
            send_sem=send_a.at[f, low + j],
            recv_sem=recv_n.at[f, j],
            device_id={"tm": low + j},
        )

    def far_copy(f, j):
        s = first + j
        return pltpu.make_async_remote_copy(
            src_ref=lat.at[s, f, pl.ds(0, BASE)],
            dst_ref=far[f].at[pl.ds(mine * BASE, BASE)],
            send_sem=send_a.at[f, s],
            recv_sem=recv_f.at[f, mine],
            device_id={"tm": s},
        )

    def far_wait(f, j):
        return pltpu.make_async_remote_copy(
            src_ref=lat.at[first + j, f, pl.ds(0, BASE)],
            dst_ref=far[f].at[pl.ds(j * BASE, BASE)],
            send_sem=send_a.at[f, first + j],
            recv_sem=recv_f.at[f, j],
            device_id={"tm": first + j},
        )

    def relay_copy(f, j):
        return pltpu.make_async_remote_copy(
            src_ref=lat.at[first + j, f, pl.ds(BASE, BASE)],
            dst_ref=relay[f].at[pl.ds(mine * BASE, BASE)],
            send_sem=send_b.at[f, j],
            recv_sem=recv_r.at[f, mine],
            device_id={"tm": low + j},
        )

    def relay_wait(f, j):
        return pltpu.make_async_remote_copy(
            src_ref=lat.at[first + j, f, pl.ds(BASE, BASE)],
            dst_ref=relay[f].at[pl.ds(j * BASE, BASE)],
            send_sem=send_b.at[f, j],
            recv_sem=recv_r.at[f, j],
            device_id={"tm": low + j},
        )

    def forward(f):
        return pltpu.make_async_remote_copy(
            src_ref=relay_out.at[f],
            dst_ref=far[f].at[pl.ds(HALF * BASE, BASE)],
            send_sem=send_r.at[f],
            recv_sem=recv_f.at[f, HALF],
            device_id={"tm": first + mine},
        )

    def tile_copy(c, f, k):
        to = lax.rem(row + k, rows)
        part = half if c == 0 else 1 - half
        return pltpu.make_async_remote_copy(
            src_ref=packed.at[c, f, pl.ds(to * bucket, bucket)],
            dst_ref=rec[f].at[pl.ds((part * rows + row) * bucket, bucket)],
            send_sem=send_y.at[c, f, k - 1],
            recv_sem=recv_y.at[c, f, k - 1],
            device_id={"tile": to},
        )

    def send_slab(f, k):
        @pl.when(k < HALF)
        def _():
            j = k
            far_copy(f, j).start()

            @pl.when(j != mine)
            def _():
                relay_copy(f, j).start()

            @pl.when(j == mine)
            def _():
                relay[f][pl.ds(mine * BASE, BASE)] = lat[first + mine, f, BASE:cap]

        @pl.when(k >= HALF)
        def _():
            j = k - HALF

            @pl.when(j != mine)
            def _():
                near_copy(f, j).start()

            @pl.when(j == mine)
            def _():
                near[f][pl.ds(mine * cap, cap)] = lat[slab, f]

    def run_relay(f):
        for k in range(1, HALF):
            relay_wait(f, lax.rem(mine + k, HALF)).wait_recv()
        for i in range(BASE):
            relay_out[f, i] = relay[f][index[0, full_at] * BASE + i]
        forward(f).start()

    def run_tiles(c, f):
        if c == 0:
            for k in range(1, HALF):
                near_wait(f, lax.rem(mine + k, HALF)).wait_recv()
        else:
            for j in range(HALF):
                far_wait(f, j).wait_recv()
            forward(f).wait_recv()
        source = near[f] if c == 0 else far[f]

        @pl.loop(0, rows * bucket)
        def _(i):
            packed[c, f, i] = source[index[0, c * rows * bucket + i]]

        for k in range(1, rows):
            tile_copy(c, f, k).start()
        part = half if c == 0 else 1 - half
        rec[f][pl.ds((part * rows + row) * bucket, bucket)] = packed[
            c, f, pl.ds(row * bucket, bucket)
        ]

    for copy in small:
        copy.wait()
    ws_copy.wait()
    conv(start)
    pl.semaphore_wait(barrier, slabs + rows - 2)
    wt_copy.wait()

    @pl.loop(0, slabs)
    def _(k):
        s = lax.rem(first + k, slabs)

        @pl.when(k < slabs - 1)
        def _():
            conv(s)

        mix(s)
        send_slab(0, k)

        @pl.when(k >= HALF)
        def _():
            send_slab(1, k)

    @pl.loop(0, HALF)
    def _(k):
        send_slab(1, k)

    index_v[...] = index_row(tiles[...], rows, cap, bucket, group_tiles, row, half)
    index_copy = pltpu.make_async_copy(index_v, index, w_sem.at[6])
    index_copy.start()
    index_copy.wait()
    pick_at = 2 * rows * bucket
    full_at = pick_at + group_tiles

    run_relay(0)
    run_tiles(0, 0)
    run_tiles(1, 0)
    run_tiles(0, 1)
    run_relay(1)
    run_tiles(1, 1)

    for f in range(frames):
        for c in range(2):
            for k in range(1, rows):
                tile_copy(c, f, k).wait_recv()

        @pl.loop(0, group_tiles)
        def _(i):
            out[i, f] = rec[f][index[0, pick_at + i]]

    for f in range(frames):
        for k in range(1, HALF):
            j = lax.rem(mine + k, HALF)
            near_copy(f, j).wait_send()
            relay_copy(f, j).wait_send()
        for j in range(HALF):
            far_copy(f, j).wait_send()
        forward(f).wait_send()
        for c in range(2):
            for k in range(1, rows):
                tile_copy(c, f, k).wait_send()


def body_two_blocks(rows, slabs, pixels, slot_tile, w_space, b_space, w_time, b_time, gain):
    cap, all_frames, pix_count, channels = pixels.shape
    features = w_space.shape[-1]
    frames = all_frames // slabs
    group_tiles = cap // 2 * slabs
    per_group = (cap + rows - 1) // rows
    bucket = per_group * 3
    area = pix_count // 4
    count = frames * cap
    height = count * area
    vmem = pl.BlockSpec(memory_space=pltpu.VMEM)
    hbm = pl.BlockSpec(memory_space=pl.ANY)
    bf16, f32 = jnp.bfloat16, jnp.float32
    dma = pltpu.SemaphoreType.DMA

    def held(*lead):
        return pltpu.VMEM(lead + (area, features), bf16)

    return pl.pallas_call(
        functools.partial(encode, rows, slabs, cap, bucket, group_tiles),
        out_shape=jax.ShapeDtypeStruct((group_tiles, frames, area, features), bf16),
        in_specs=[hbm] * 7,
        out_specs=vmem,
        scratch_shapes=[
            pltpu.VMEM((slabs, cap, frames, pix_count, channels), bf16),
            pltpu.VMEM((9 * channels, features), bf16),
            pltpu.VMEM((3, features, features), bf16),
            pltpu.VMEM((1, features), f32),
            pltpu.VMEM((1, features), f32),
            pltpu.VMEM((1, features), f32),
            pltpu.VMEM((1, slot_tile.shape[0]), jnp.int32),
            pltpu.VMEM((1, 128), jnp.int32),
            pltpu.SMEM((1, 128), jnp.int32),
            pltpu.VMEM((2, channels // 128, count, 48, 128), f32),
            pltpu.VMEM((height, 9 * channels), bf16),
            pltpu.VMEM(((slabs + 1) * height, features), bf16),
            held(slabs, frames, cap),
            held(HALF * cap), held(HALF * cap),
            held(HALF * BASE + BASE), held(HALF * BASE + BASE),
            held(HALF * BASE), held(HALF * BASE),
            held(frames, BASE),
            held(2, frames, rows * bucket),
            held(2 * rows * bucket), held(2 * rows * bucket),
            dma((slabs,)), dma((7,)),
            dma((frames, slabs)), dma((frames, HALF)), dma((frames, HALF + 1)),
            dma((frames, HALF)), dma((frames, HALF)), dma((frames,)),
            dma((2, frames, rows - 1)), dma((2, frames, rows - 1)),
        ],
        compiler_params=pltpu.CompilerParams(
            collective_id=1, has_side_effects=True, vmem_limit_bytes=62 << 20
        ),
    )(
        slot_tile[None], pixels, w_space.reshape(9 * channels, features),
        b_space[None], w_time, b_time[None], gain[None],
    )


def solution(mesh):
    rows, slabs = mesh.shape["tile"], mesh.shape["tm"]
    plan = body_two_blocks if slabs == 2 * HALF else body
    return jax.shard_map(
        functools.partial(plan, rows, slabs),
        mesh=mesh,
        in_specs=(P(("tile", "tm"), None, None, None), P(), P(), P(), P(), P(), P()),
        out_specs=P("tile", "tm", None, None),
        check_vma=False,
    )
```

```python
import functools

import jax
import jax.numpy as jnp
from jax import lax
from jax.experimental import pallas as pl
from jax.experimental.pallas import tpu as pltpu
from jax.sharding import PartitionSpec as P

TILE_SIDE = 8
HALF = 4
BASE = 3


def conv_space(raw_tiles, w_space, b_space):
    number, frames, pix_count, channels = raw_tiles.shape
    grid = raw_tiles.reshape(number * frames, TILE_SIDE, TILE_SIDE, channels)
    total = lax.conv_general_dilated(
        grid,
        w_space,
        (2, 2),
        ((1, 1), (1, 1)),
        dimension_numbers=("NHWC", "HWIO", "NHWC"),
        preferred_element_type=jnp.float32,
    )
    active = jax.nn.silu(total + b_space)
    half_side = TILE_SIDE // 2
    return active.astype(jnp.bfloat16).reshape(number, frames, half_side * half_side, -1)


def tables(slot_tile, rows, groups, bucket, group_tiles, my_row):
    table = slot_tile.reshape(rows, -1)
    width = table.shape[1]
    group_of = jnp.where(table >= 0, lax.div(table, group_tiles), groups)
    pos = jnp.arange(width, dtype=jnp.int32)
    earlier = pos[None, :] < pos[:, None]
    same = (group_of[:, :, None] == group_of[:, None, :]) & earlier[None]
    rank = jnp.sum(same.astype(jnp.int32), axis=2)
    target = group_of * bucket + rank
    own_target = lax.dynamic_index_in_dim(target, my_row, 0, keepdims=False)
    own_live = lax.dynamic_index_in_dim(table, my_row, 0, keepdims=False) >= 0
    own_target = jnp.where(own_live, own_target, -1)
    places = jnp.arange(groups * bucket, dtype=jnp.int32)
    send_idx = jnp.sum(
        jnp.where(own_target[None, :] == places[:, None], pos[None, :], 0), axis=1
    )
    wanted = my_row * group_tiles + jnp.arange(group_tiles, dtype=jnp.int32)
    arrived = jnp.arange(rows, dtype=jnp.int32)[:, None] * bucket + rank
    pick_idx = jnp.sum(
        jnp.where(
            table.reshape(-1)[None, :] == wanted[:, None], arrived.reshape(-1)[None, :], 0
        ),
        axis=1,
    )
    return send_idx, pick_idx


def kernel(
    rows, slabs, cap, bucket, group_tiles,
    send_idx, pick_idx, src, w_time, b_time, gain, out,
    got1a, got1b, out2, got2a, got2b, feats, halo, total,
    send1, recv1, send2, recv2, send3, recv3,
):
    frames = 2
    got1, got2 = (got1a, got1b), (got2a, got2b)
    row = lax.axis_index("tile")
    slab = lax.axis_index("tm")
    barrier = pltpu.get_barrier_semaphore()
    for k in range(1, slabs):
        pl.semaphore_signal(barrier, inc=1, device_id={"tm": lax.rem(slab + k, slabs)})
    for k in range(1, rows):
        pl.semaphore_signal(barrier, inc=1, device_id={"tile": lax.rem(row + k, rows)})
    pl.semaphore_wait(barrier, slabs + rows - 2)

    def copy1(f, k):
        to = lax.rem(slab + k, slabs)
        return pltpu.make_async_remote_copy(
            src_ref=src.at[:, to * frames + f],
            dst_ref=got1[f].at[pl.ds(slab * cap, cap)],
            send_sem=send1.at[f, k - 1],
            recv_sem=recv1.at[f, k - 1],
            device_id={"tm": to},
        )

    def copy2(f, k):
        to = lax.rem(row + k, rows)
        return pltpu.make_async_remote_copy(
            src_ref=out2.at[f, pl.ds(to * bucket, bucket)],
            dst_ref=got2[f].at[pl.ds(row * bucket, bucket)],
            send_sem=send2.at[f, k - 1],
            recv_sem=recv2.at[f, k - 1],
            device_id={"tile": to},
        )

    def copy3(f):
        return pltpu.make_async_remote_copy(
            src_ref=feats.at[f],
            dst_ref=halo.at[f],
            send_sem=send3.at[f],
            recv_sem=recv3.at[f],
            device_id={"tm": lax.rem(slab + 1, slabs)},
        )

    for f in range(frames):
        for k in range(1, slabs):
            copy1(f, k).start()
    for f in range(frames):
        got1[f][pl.ds(slab * cap, cap)] = src[:, slab * frames + f]
        for k in range(1, slabs):
            copy1(f, k).wait_recv()

        @pl.loop(0, rows * bucket)
        def _(i):
            out2[f, i] = got1[f][send_idx[i]]

        for k in range(1, rows):
            copy2(f, k).start()

        @pl.loop(0, bucket)
        def _(j):
            got2[f][row * bucket + j] = got1[f][send_idx[row * bucket + j]]

        for k in range(1, rows):
            copy2(f, k).wait_recv()

        @pl.loop(0, group_tiles)
        def _(i):
            feats[f, i] = got2[f][pick_idx[i]]

        @pl.when(slab < slabs - 1)
        def _():
            copy3(f).start()

    part = group_tiles // 2
    height = part * 16

    def flat(value):
        return value.reshape(height, value.shape[-1])

    @pl.loop(0, 2)
    def _(c):
        at = pl.ds(c * part, part)
        own = [flat(feats[0, at]), flat(feats[1, at])]
        for f in range(frames):
            mixed = own[f].astype(jnp.float32) + b_time[...]
            for lag in range(f + 1):
                mixed = mixed + jnp.dot(
                    own[f - lag], w_time[lag], preferred_element_type=jnp.float32
                )
            total[f, c] = mixed

    for f in range(frames):

        @pl.when(slab > 0)
        def _():
            copy3(f).wait_recv()

        @pl.when(slab == 0)
        def _():
            halo[f] = jnp.zeros(halo.shape[1:], halo.dtype)

    @pl.loop(0, 2)
    def _(c):
        at = pl.ds(c * part, part)
        before = [flat(halo[0, at]), flat(halo[1, at])]
        for f in range(frames):
            mixed = total[f, c]
            for lag in range(f + 1, 3):
                mixed = mixed + jnp.dot(
                    before[2 + f - lag], w_time[lag], preferred_element_type=jnp.float32
                )
            scale = lax.rsqrt(jnp.mean(mixed * mixed, axis=-1, keepdims=True) + 1e-06)
            value = (mixed * scale * gain[...]).astype(jnp.bfloat16)
            out[at, f] = value.reshape(part, 16, value.shape[-1])

    for f in range(frames):
        for k in range(1, slabs):
            copy1(f, k).wait_send()
        for k in range(1, rows):
            copy2(f, k).wait_send()

        @pl.when(slab < slabs - 1)
        def _():
            copy3(f).wait_send()


def body(rows, slabs, pixels, slot_tile, w_space, b_space, w_time, b_time, gain):
    cap, all_frames = pixels.shape[:2]
    channels = w_space.shape[-1]
    group_tiles = cap // 2 * slabs
    per_group = (cap + rows - 1) // rows
    bucket = per_group * 3 * (slabs // 4)
    frames = all_frames // slabs
    send_idx, pick_idx = tables(
        slot_tile, rows, rows, bucket, group_tiles, lax.axis_index("tile")
    )
    spatial = conv_space(pixels, w_space, b_space)
    vmem = pl.BlockSpec(memory_space=pltpu.VMEM)
    smem = pl.BlockSpec(memory_space=pltpu.SMEM)
    bf16 = jnp.bfloat16
    dma = pltpu.SemaphoreType.DMA
    return pl.pallas_call(
        functools.partial(kernel, rows, slabs, cap, bucket, group_tiles),
        out_shape=jax.ShapeDtypeStruct((group_tiles, frames, 16, channels), bf16),
        in_specs=[smem, smem, vmem, vmem, vmem, vmem],
        out_specs=vmem,
        scratch_shapes=[
            pltpu.VMEM((slabs * cap, 16, channels), bf16),
            pltpu.VMEM((slabs * cap, 16, channels), bf16),
            pltpu.VMEM((frames, rows * bucket, 16, channels), bf16),
            pltpu.VMEM((rows * bucket, 16, channels), bf16),
            pltpu.VMEM((rows * bucket, 16, channels), bf16),
            pltpu.VMEM((frames, group_tiles, 16, channels), bf16),
            pltpu.VMEM((frames, group_tiles, 16, channels), bf16),
            pltpu.VMEM((frames, 2, group_tiles * 8, channels), jnp.float32),
            dma((frames, slabs - 1)),
            dma((frames, slabs - 1)),
            dma((frames, rows - 1)),
            dma((frames, rows - 1)),
            dma((frames,)),
            dma((frames,)),
        ],
        compiler_params=pltpu.CompilerParams(collective_id=0, has_side_effects=True),
    )(send_idx, pick_idx, spatial, w_time, b_time[None], gain[None])


def index_row(tiles, rows, cap, bucket, group_tiles, row, half):
    slots = tiles.shape[1]
    width = HALF * cap
    shape = (slots, slots)
    along = lax.broadcasted_iota(jnp.int32, shape, 1)
    down = lax.broadcasted_iota(jnp.int32, shape, 0)
    spread = jnp.broadcast_to(tiles, shape)
    column = jnp.sum(jnp.where(along == down, spread, 0), axis=1, keepdims=True)

    def key_of(ids, tile):
        key = jnp.where(tile < 0, rows, 0)
        for k in range(1, rows):
            key = key + jnp.where(tile >= k * group_tiles, 1, 0)
        block = jnp.zeros_like(ids)
        for k in range(1, slots // width):
            block = block + jnp.where(ids >= k * width, 1, 0)
        return block, key

    ids = lax.broadcasted_iota(jnp.int32, (slots, 1), 0)
    block, group = key_of(ids, column)
    lane = lax.broadcasted_iota(jnp.int32, (1, slots), 1)
    block_r, group_r = key_of(lane, tiles)
    same = (block * (rows + 1) + group) == (block_r * (rows + 1) + group_r)
    rank = jnp.sum(jnp.where(same & (along < down), 1, 0), axis=1, keepdims=True)
    part = block % 2
    arrival = (part * rows + block // 2) * bucket + rank
    inside = ids - block * width
    dev = jnp.zeros_like(ids)
    for k in range(1, HALF):
        dev = dev + jnp.where(inside >= k * cap, 1, 0)
    pos = inside - dev * cap
    came = jnp.where(pos < BASE, dev * BASE + pos, HALF * BASE + pos - BASE)
    mine = block == row * 2 + half
    other = block == row * 2 + 1 - half
    live = column >= 0
    places = rows * bucket
    target = jnp.where(
        live & (mine | other), group * bucket + rank + jnp.where(other, places, 0), -1
    )
    place = lax.broadcasted_iota(jnp.int32, (1, 128), 1)
    wanted = jnp.where(
        (place >= 2 * places) & (place < 2 * places + group_tiles),
        place - 2 * places + row * group_tiles,
        -2,
    )
    total = jnp.where(target == place, came, 0) + jnp.where(column == wanted, arrival, 0)
    full = mine & live & (pos == BASE)
    for at, part_of in ((0, dev // 2), (1, dev % 2)):
        total = total + jnp.where(full & (place == 2 * places + group_tiles + at), part_of, 0)
    limit = jnp.where(
        place < 2 * places,
        (HALF + 1) * BASE,
        jnp.where(place < 2 * places + group_tiles, 2 * places, 2),
    )
    return jnp.minimum(jnp.sum(total, axis=0, keepdims=True), limit - 1)


def encode(
    rows, slabs, cap, bucket, group_tiles,
    slot_tile, pixels, w_space, b_space_h, w_time, b_time_h, gain_h,
    out,
    pix, ws, wt, b_space, b_time, gain, tiles, index_v, index, plane, patch, spatial, lat,
    near, far0, far1, x_near, x_far, z_near, z_far, z_out, forward_out,
    packed_n, packed_f, rec,
    in_sem, w_sem, send_n, recv_n, send_f, recv_f, send_x, recv_x, send_z, recv_z,
    send_r, send_yn, recv_yn, send_yf, recv_yf,
):
    frames = 2
    far = (far0, far1)
    f32, bf16 = jnp.float32, jnp.bfloat16
    row = lax.axis_index("tile")
    slab = lax.axis_index("tm")
    half = lax.div(slab, HALF)
    mine = lax.rem(slab, HALF)
    x = lax.rem(slab, 2)
    zl = lax.div(mine, 2)
    first = (1 - half) * HALF
    low = half * HALF
    x_peer = slab + 1 - 2 * x
    z_peer = slab + 2 - 4 * zl
    barrier = pltpu.get_barrier_semaphore()
    for k in range(1, slabs):
        pl.semaphore_signal(barrier, inc=1, device_id={"tm": lax.rem(slab + k, slabs)})
    for k in range(1, rows):
        pl.semaphore_signal(barrier, inc=1, device_id={"tile": lax.rem(row + k, rows)})

    steps = slabs // 2
    span = 2 * frames
    origin = lax.div(first, 2)

    def load(z):
        return pltpu.make_async_copy(
            pixels.at[:, pl.ds(z * span, span)], pix.at[z], in_sem.at[z]
        )

    start = lax.rem(origin + steps - 1, steps)
    small = [
        pltpu.make_async_copy(source, target, w_sem.at[2 + i])
        for i, (source, target) in enumerate(
            ((slot_tile, tiles), (b_space_h, b_space), (b_time_h, b_time), (gain_h, gain))
        )
    ]
    for copy in small:
        copy.start()
    load(start).start()
    ws_copy = pltpu.make_async_copy(w_space, ws, w_sem.at[0])
    ws_copy.start()
    load(origin).start()
    wt_copy = pltpu.make_async_copy(w_time, wt, w_sem.at[1])
    wt_copy.start()

    @pl.loop(1, steps - 1)
    def _(k):
        load(lax.rem(origin + k, steps)).start()

    count = span * cap
    side = TILE_SIDE
    out_side = side // 2
    area = out_side * out_side
    height = count * area
    step_rows = height // span
    channels = patch.shape[1] // 9
    lanes = plane.shape[-1]
    for piece in range(channels // lanes):
        plane[1, piece, :, 8:16] = jnp.zeros((count, 8, lanes), f32)
    spatial[height - 2 * step_rows:height] = jnp.zeros((2 * step_rows, spatial.shape[1]), bf16)
    edge = lax.rem(lax.broadcasted_iota(jnp.int32, (area, lanes), 0), out_side) == 0

    def conv(z):
        load(z).wait()

        @pl.loop(0, cap)
        def _(p):
            for f in range(span):
                image = f * cap + p
                value = pix[z, p, f].astype(f32).reshape(out_side, 2, side, channels)
                for parity in range(2):
                    rows_of = value[:, parity].reshape(out_side * side, channels)
                    for piece in range(channels // lanes):
                        plane[parity, piece, image, 16:48] = rows_of[
                            :, piece * lanes:(piece + 1) * lanes
                        ]
            for f in range(span):
                image = f * cap + p
                for a in range(3):
                    parity, base = ((1, 8), (0, 16), (1, 16))[a]
                    for b in range(3):
                        for piece in range(channels // lanes):
                            taken = plane[
                                parity, piece, image, pl.ds(base + b - 1, area, stride=2)
                            ]
                            if b == 0:
                                taken = jnp.where(edge, 0.0, taken)
                            at = (3 * a + b) * channels + piece * lanes
                            patch[
                                pl.ds(pl.multiple_of(image * area, area), area),
                                at:at + lanes,
                            ] = taken.astype(bf16)

        total = jnp.dot(patch[...], ws[...], preferred_element_type=f32) + b_space[...]
        active = total / (1.0 + jnp.exp(-total))
        spatial[pl.ds(pl.multiple_of((z + 1) * height, height), height)] = active.astype(bf16)

    def mix(z):
        base = (z + 1) * height
        mixed = spatial[pl.ds(pl.multiple_of(base, step_rows), height)].astype(f32) + b_time[...]
        for lag in range(3):
            mixed = mixed + jnp.dot(
                spatial[pl.ds(pl.multiple_of(base - lag * step_rows, step_rows), height)],
                wt[lag],
                preferred_element_type=f32,
            )
        scale = lax.rsqrt(jnp.mean(mixed * mixed, axis=-1, keepdims=True) + 1e-06)
        value = (mixed * scale * gain[...]).astype(bf16)
        lat[pl.ds(2 * z, 2)] = value.reshape(2, frames, cap, area, value.shape[-1])


    def near_copy(j, source):
        return pltpu.make_async_remote_copy(
            src_ref=lat.at[low + j, :, pl.ds(0, BASE)],
            dst_ref=near.at[:, pl.ds(source * BASE, BASE)],
            send_sem=send_n.at[j],
            recv_sem=recv_n.at[source],
            device_id={"tm": low + j},
        )

    def far_copy(f, j, source):
        return pltpu.make_async_remote_copy(
            src_ref=lat.at[first + j, f, pl.ds(0, BASE)],
            dst_ref=far[f].at[pl.ds(source * BASE, BASE)],
            send_sem=send_f.at[f, j],
            recv_sem=recv_f.at[f, source],
            device_id={"tm": first + j},
        )


    def x_copy(c, place):
        s = (low if c == 0 else first) + 2 * place + 1 - x
        return pltpu.make_async_remote_copy(
            src_ref=lat.at[s, :, pl.ds(BASE, BASE)],
            dst_ref=(x_near if c == 0 else x_far).at[place, x],
            send_sem=send_x.at[c, place],
            recv_sem=recv_x.at[c, place],
            device_id={"tm": x_peer},
        )

    def z_copy(c):
        return pltpu.make_async_remote_copy(
            src_ref=z_out.at[c],
            dst_ref=(z_near if c == 0 else z_far).at[zl],
            send_sem=send_z.at[c],
            recv_sem=recv_z.at[c],
            device_id={"tm": z_peer},
        )

    def forward(f):
        return pltpu.make_async_remote_copy(
            src_ref=forward_out.at[f],
            dst_ref=far[f].at[pl.ds(HALF * BASE, BASE)],
            send_sem=send_r.at[f],
            recv_sem=recv_f.at[f, HALF],
            device_id={"tm": first + mine},
        )

    pick_at = 2 * rows * bucket
    full_at = pick_at + group_tiles

    def merge_x(c):
        source, target, base = (x_near, z_near, low) if c == 0 else (x_far, z_far, first)
        for place in range(2):
            x_copy(c, place).wait_recv()
            source[place, x] = lat[base + 2 * place + x, :, BASE:cap]
        full_x = index[0, full_at + 1]
        z_out[c] = source[1 - zl, full_x]
        target[zl] = source[zl, full_x]
        z_copy(c).start()

    def merge_z_far():
        z_copy(1).wait_recv()
        forward_out[...] = z_far[index[0, full_at]]
        for f in range(frames):
            forward(f).start()

    def merge_z_near():
        z_copy(0).wait_recv()
        near[:, HALF * BASE:] = z_near[index[0, full_at]]


    def tile_near(k):
        to = lax.rem(row + k, rows)
        return pltpu.make_async_remote_copy(
            src_ref=packed_n.at[:, pl.ds(to * bucket, bucket)],
            dst_ref=rec.at[:, pl.ds((half * rows + row) * bucket, bucket)],
            send_sem=send_yn.at[k - 1],
            recv_sem=recv_yn.at[k - 1],
            device_id={"tile": to},
        )

    def tile_far(f, k):
        to = lax.rem(row + k, rows)
        return pltpu.make_async_remote_copy(
            src_ref=packed_f.at[f, pl.ds(to * bucket, bucket)],
            dst_ref=rec.at[f, pl.ds(((1 - half) * rows + row) * bucket, bucket)],
            send_sem=send_yf.at[f, k - 1],
            recv_sem=recv_yf.at[f, k - 1],
            device_id={"tile": to},
        )

    def run_near():
        for k in range(1, HALF):
            near_copy(mine, lax.rem(mine + k, HALF)).wait_recv()
        merge_z_near()

        @pl.loop(0, rows * bucket)
        def _(i):
            for f in range(frames):
                packed_n[f, i] = near[f, index[0, i]]

        for k in range(1, rows):
            tile_near(k).start()
        own = pl.ds(row * bucket, bucket)
        rec[:, pl.ds((half * rows + row) * bucket, bucket)] = packed_n[:, own]

    def run_far(f):
        for j in range(HALF):
            far_copy(f, mine, j).wait_recv()
        forward(f).wait_recv()

        @pl.loop(0, rows * bucket)
        def _(i):
            packed_f[f, i] = far[f][index[0, rows * bucket + i]]

        for k in range(1, rows):
            tile_far(f, k).start()
        own = pl.ds(row * bucket, bucket)
        rec[f, pl.ds(((1 - half) * rows + row) * bucket, bucket)] = packed_f[f, own]

    for copy in small:
        copy.wait()
    index_v[...] = index_row(tiles[...], rows, cap, bucket, group_tiles, row, half)
    index_copy = pltpu.make_async_copy(index_v, index, w_sem.at[6])
    index_copy.start()
    ws_copy.wait()
    conv(start)
    index_copy.wait()
    pl.semaphore_wait(barrier, slabs + rows - 2)
    wt_copy.wait()

    @pl.loop(0, steps)
    def _(k):
        z = lax.rem(origin + k, steps)

        @pl.when(k < steps - 1)
        def _():
            conv(z)

        mix(z)

        @pl.when(k < 2)
        def _():
            x_copy(1, k).start()
            for side_x in range(2):
                far_copy(0, 2 * k + side_x, mine).start()

        @pl.when(k >= 2)
        def _():
            x_copy(0, k - 2).start()
            for side_x in range(2):
                j = 2 * (k - 2) + side_x

                @pl.when(j != mine)
                def _():
                    near_copy(j, mine).start()

                @pl.when(j == mine)
                def _():
                    near[:, pl.ds(mine * BASE, BASE)] = lat[slab, :, 0:BASE]

        @pl.when(k == 1)
        def _():
            merge_x(1)

        @pl.when(k == 2)
        def _():
            merge_z_far()

    for j in range(HALF):
        far_copy(1, j, mine).start()
    merge_x(0)
    run_far(0)
    run_near()
    run_far(1)

    for k in range(1, rows):
        tile_near(k).wait_recv()
        for f in range(frames):
            tile_far(f, k).wait_recv()

    @pl.loop(0, group_tiles)
    def _(i):
        for f in range(frames):
            out[i, f] = rec[f, index[0, pick_at + i]]

    for k in range(1, HALF):
        near_copy(lax.rem(mine + k, HALF), mine).wait_send()
    for c in range(2):
        for place in range(2):
            x_copy(c, place).wait_send()
        z_copy(c).wait_send()
    for f in range(frames):
        for j in range(HALF):
            far_copy(f, j, mine).wait_send()
        forward(f).wait_send()
        for k in range(1, rows):
            tile_far(f, k).wait_send()
    for k in range(1, rows):
        tile_near(k).wait_send()


def body_two_blocks(rows, slabs, pixels, slot_tile, w_space, b_space, w_time, b_time, gain):
    cap, all_frames, pix_count, channels = pixels.shape
    features = w_space.shape[-1]
    frames = all_frames // slabs
    group_tiles = cap // 2 * slabs
    per_group = (cap + rows - 1) // rows
    bucket = per_group * 3
    area = pix_count // 4
    span = 2 * frames
    steps = slabs // 2
    height = span * cap * area
    vmem = pl.BlockSpec(memory_space=pltpu.VMEM)
    hbm = pl.BlockSpec(memory_space=pl.ANY)
    bf16, f32 = jnp.bfloat16, jnp.float32
    dma = pltpu.SemaphoreType.DMA
    arrivals = (HALF + 1) * BASE

    def held(*lead):
        return pltpu.VMEM(lead + (area, features), bf16)

    return pl.pallas_call(
        functools.partial(encode, rows, slabs, cap, bucket, group_tiles),
        out_shape=jax.ShapeDtypeStruct((group_tiles, frames, area, features), bf16),
        in_specs=[hbm] * 7,
        out_specs=vmem,
        scratch_shapes=[
            pltpu.VMEM((steps, cap, span, pix_count, channels), bf16),
            pltpu.VMEM((9 * channels, features), bf16),
            pltpu.VMEM((3, features, features), bf16),
            pltpu.VMEM((1, features), f32),
            pltpu.VMEM((1, features), f32),
            pltpu.VMEM((1, features), f32),
            pltpu.VMEM((1, slot_tile.shape[0]), jnp.int32),
            pltpu.VMEM((1, 128), jnp.int32),
            pltpu.SMEM((1, 128), jnp.int32),
            pltpu.VMEM((2, channels // 128, span * cap, 48, 128), f32),
            pltpu.VMEM((height, 9 * channels), bf16),
            pltpu.VMEM(((steps + 1) * height, features), bf16),
            held(slabs, frames, cap),
            held(frames, arrivals), held(arrivals), held(arrivals),
            held(2, 2, frames, BASE), held(2, 2, frames, BASE),
            held(2, frames, BASE), held(2, frames, BASE), held(2, frames, BASE),
            held(frames, BASE),
            held(frames, rows * bucket), held(frames, rows * bucket),
            held(frames, 2 * rows * bucket),
            dma((steps,)), dma((7,)),
            dma((HALF,)), dma((HALF,)), dma((frames, HALF)), dma((frames, HALF + 1)),
            dma((2, 2)), dma((2, 2)), dma((2,)), dma((2,)), dma((frames,)),
            dma((rows - 1,)), dma((rows - 1,)), dma((frames, rows - 1)), dma((frames, rows - 1)),
        ],
        compiler_params=pltpu.CompilerParams(
            collective_id=1, has_side_effects=True, vmem_limit_bytes=62 << 20
        ),
    )(
        slot_tile[None], pixels, w_space.reshape(9 * channels, features),
        b_space[None], w_time, b_time[None], gain[None],
    )


def solution(mesh):
    rows, slabs = mesh.shape["tile"], mesh.shape["tm"]
    plan = body_two_blocks if slabs == 2 * HALF else body
    return jax.shard_map(
        functools.partial(plan, rows, slabs),
        mesh=mesh,
        in_specs=(P(("tile", "tm"), None, None, None), P(), P(), P(), P(), P(), P()),
        out_specs=P("tile", "tm", None, None),
        check_vma=False,
    )
```

```python
import functools

import jax
import jax.numpy as jnp
from jax import lax
from jax.experimental import pallas as pl
from jax.experimental.pallas import tpu as pltpu
from jax.sharding import PartitionSpec as P

TILE_SIDE = 8
HALF = 4
BASE = 3


def conv_space(raw_tiles, w_space, b_space):
    number, frames, pix_count, channels = raw_tiles.shape
    grid = raw_tiles.reshape(number * frames, TILE_SIDE, TILE_SIDE, channels)
    total = lax.conv_general_dilated(
        grid,
        w_space,
        (2, 2),
        ((1, 1), (1, 1)),
        dimension_numbers=("NHWC", "HWIO", "NHWC"),
        preferred_element_type=jnp.float32,
    )
    active = jax.nn.silu(total + b_space)
    half_side = TILE_SIDE // 2
    return active.astype(jnp.bfloat16).reshape(number, frames, half_side * half_side, -1)


def tables(slot_tile, rows, groups, bucket, group_tiles, my_row):
    table = slot_tile.reshape(rows, -1)
    width = table.shape[1]
    group_of = jnp.where(table >= 0, lax.div(table, group_tiles), groups)
    pos = jnp.arange(width, dtype=jnp.int32)
    earlier = pos[None, :] < pos[:, None]
    same = (group_of[:, :, None] == group_of[:, None, :]) & earlier[None]
    rank = jnp.sum(same.astype(jnp.int32), axis=2)
    target = group_of * bucket + rank
    own_target = lax.dynamic_index_in_dim(target, my_row, 0, keepdims=False)
    own_live = lax.dynamic_index_in_dim(table, my_row, 0, keepdims=False) >= 0
    own_target = jnp.where(own_live, own_target, -1)
    places = jnp.arange(groups * bucket, dtype=jnp.int32)
    send_idx = jnp.sum(
        jnp.where(own_target[None, :] == places[:, None], pos[None, :], 0), axis=1
    )
    wanted = my_row * group_tiles + jnp.arange(group_tiles, dtype=jnp.int32)
    arrived = jnp.arange(rows, dtype=jnp.int32)[:, None] * bucket + rank
    pick_idx = jnp.sum(
        jnp.where(
            table.reshape(-1)[None, :] == wanted[:, None], arrived.reshape(-1)[None, :], 0
        ),
        axis=1,
    )
    return send_idx, pick_idx


def kernel(
    rows, slabs, cap, bucket, group_tiles,
    send_idx, pick_idx, src, w_time, b_time, gain, out,
    got1a, got1b, out2, got2a, got2b, feats, halo, total,
    send1, recv1, send2, recv2, send3, recv3,
):
    frames = 2
    got1, got2 = (got1a, got1b), (got2a, got2b)
    row = lax.axis_index("tile")
    slab = lax.axis_index("tm")
    barrier = pltpu.get_barrier_semaphore()
    for k in range(1, slabs):
        pl.semaphore_signal(barrier, inc=1, device_id={"tm": lax.rem(slab + k, slabs)})
    for k in range(1, rows):
        pl.semaphore_signal(barrier, inc=1, device_id={"tile": lax.rem(row + k, rows)})
    pl.semaphore_wait(barrier, slabs + rows - 2)

    def copy1(f, k):
        to = lax.rem(slab + k, slabs)
        return pltpu.make_async_remote_copy(
            src_ref=src.at[:, to * frames + f],
            dst_ref=got1[f].at[pl.ds(slab * cap, cap)],
            send_sem=send1.at[f, k - 1],
            recv_sem=recv1.at[f, k - 1],
            device_id={"tm": to},
        )

    def copy2(f, k):
        to = lax.rem(row + k, rows)
        return pltpu.make_async_remote_copy(
            src_ref=out2.at[f, pl.ds(to * bucket, bucket)],
            dst_ref=got2[f].at[pl.ds(row * bucket, bucket)],
            send_sem=send2.at[f, k - 1],
            recv_sem=recv2.at[f, k - 1],
            device_id={"tile": to},
        )

    def copy3(f):
        return pltpu.make_async_remote_copy(
            src_ref=feats.at[f],
            dst_ref=halo.at[f],
            send_sem=send3.at[f],
            recv_sem=recv3.at[f],
            device_id={"tm": lax.rem(slab + 1, slabs)},
        )

    for f in range(frames):
        for k in range(1, slabs):
            copy1(f, k).start()
    for f in range(frames):
        got1[f][pl.ds(slab * cap, cap)] = src[:, slab * frames + f]
        for k in range(1, slabs):
            copy1(f, k).wait_recv()

        @pl.loop(0, rows * bucket)
        def _(i):
            out2[f, i] = got1[f][send_idx[i]]

        for k in range(1, rows):
            copy2(f, k).start()

        @pl.loop(0, bucket)
        def _(j):
            got2[f][row * bucket + j] = got1[f][send_idx[row * bucket + j]]

        for k in range(1, rows):
            copy2(f, k).wait_recv()

        @pl.loop(0, group_tiles)
        def _(i):
            feats[f, i] = got2[f][pick_idx[i]]

        @pl.when(slab < slabs - 1)
        def _():
            copy3(f).start()

    part = group_tiles // 2
    height = part * 16

    def flat(value):
        return value.reshape(height, value.shape[-1])

    @pl.loop(0, 2)
    def _(c):
        at = pl.ds(c * part, part)
        own = [flat(feats[0, at]), flat(feats[1, at])]
        for f in range(frames):
            mixed = own[f].astype(jnp.float32) + b_time[...]
            for lag in range(f + 1):
                mixed = mixed + jnp.dot(
                    own[f - lag], w_time[lag], preferred_element_type=jnp.float32
                )
            total[f, c] = mixed

    for f in range(frames):

        @pl.when(slab > 0)
        def _():
            copy3(f).wait_recv()

        @pl.when(slab == 0)
        def _():
            halo[f] = jnp.zeros(halo.shape[1:], halo.dtype)

    @pl.loop(0, 2)
    def _(c):
        at = pl.ds(c * part, part)
        before = [flat(halo[0, at]), flat(halo[1, at])]
        for f in range(frames):
            mixed = total[f, c]
            for lag in range(f + 1, 3):
                mixed = mixed + jnp.dot(
                    before[2 + f - lag], w_time[lag], preferred_element_type=jnp.float32
                )
            scale = lax.rsqrt(jnp.mean(mixed * mixed, axis=-1, keepdims=True) + 1e-06)
            value = (mixed * scale * gain[...]).astype(jnp.bfloat16)
            out[at, f] = value.reshape(part, 16, value.shape[-1])

    for f in range(frames):
        for k in range(1, slabs):
            copy1(f, k).wait_send()
        for k in range(1, rows):
            copy2(f, k).wait_send()

        @pl.when(slab < slabs - 1)
        def _():
            copy3(f).wait_send()


def body(rows, slabs, pixels, slot_tile, w_space, b_space, w_time, b_time, gain):
    cap, all_frames = pixels.shape[:2]
    channels = w_space.shape[-1]
    group_tiles = cap // 2 * slabs
    per_group = (cap + rows - 1) // rows
    bucket = per_group * 3 * (slabs // 4)
    frames = all_frames // slabs
    send_idx, pick_idx = tables(
        slot_tile, rows, rows, bucket, group_tiles, lax.axis_index("tile")
    )
    spatial = conv_space(pixels, w_space, b_space)
    vmem = pl.BlockSpec(memory_space=pltpu.VMEM)
    smem = pl.BlockSpec(memory_space=pltpu.SMEM)
    bf16 = jnp.bfloat16
    dma = pltpu.SemaphoreType.DMA
    return pl.pallas_call(
        functools.partial(kernel, rows, slabs, cap, bucket, group_tiles),
        out_shape=jax.ShapeDtypeStruct((group_tiles, frames, 16, channels), bf16),
        in_specs=[smem, smem, vmem, vmem, vmem, vmem],
        out_specs=vmem,
        scratch_shapes=[
            pltpu.VMEM((slabs * cap, 16, channels), bf16),
            pltpu.VMEM((slabs * cap, 16, channels), bf16),
            pltpu.VMEM((frames, rows * bucket, 16, channels), bf16),
            pltpu.VMEM((rows * bucket, 16, channels), bf16),
            pltpu.VMEM((rows * bucket, 16, channels), bf16),
            pltpu.VMEM((frames, group_tiles, 16, channels), bf16),
            pltpu.VMEM((frames, group_tiles, 16, channels), bf16),
            pltpu.VMEM((frames, 2, group_tiles * 8, channels), jnp.float32),
            dma((frames, slabs - 1)),
            dma((frames, slabs - 1)),
            dma((frames, rows - 1)),
            dma((frames, rows - 1)),
            dma((frames,)),
            dma((frames,)),
        ],
        compiler_params=pltpu.CompilerParams(collective_id=0, has_side_effects=True),
    )(send_idx, pick_idx, spatial, w_time, b_time[None], gain[None])


def index_row(tiles, rows, cap, bucket, group_tiles, row, half):
    slots = tiles.shape[1]
    width = HALF * cap
    shape = (slots, slots)
    along = lax.broadcasted_iota(jnp.int32, shape, 1)
    down = lax.broadcasted_iota(jnp.int32, shape, 0)
    spread = jnp.broadcast_to(tiles, shape)
    column = jnp.sum(jnp.where(along == down, spread, 0), axis=1, keepdims=True)

    def key_of(ids, tile):
        key = jnp.where(tile < 0, rows, 0)
        for k in range(1, rows):
            key = key + jnp.where(tile >= k * group_tiles, 1, 0)
        block = jnp.zeros_like(ids)
        for k in range(1, slots // width):
            block = block + jnp.where(ids >= k * width, 1, 0)
        return block, key

    ids = lax.broadcasted_iota(jnp.int32, (slots, 1), 0)
    block, group = key_of(ids, column)
    lane = lax.broadcasted_iota(jnp.int32, (1, slots), 1)
    block_r, group_r = key_of(lane, tiles)
    same = (block * (rows + 1) + group) == (block_r * (rows + 1) + group_r)
    rank = jnp.sum(jnp.where(same & (along < down), 1, 0), axis=1, keepdims=True)
    part = block % 2
    arrival = (part * rows + block // 2) * bucket + rank
    inside = ids - block * width
    dev = jnp.zeros_like(ids)
    for k in range(1, HALF):
        dev = dev + jnp.where(inside >= k * cap, 1, 0)
    pos = inside - dev * cap
    came = jnp.where(pos < BASE, dev * BASE + pos, HALF * BASE + pos - BASE)
    came = jnp.where(block == row * 2 + half, inside, came)
    mine = block == row * 2 + half
    other = block == row * 2 + 1 - half
    live = column >= 0
    places = rows * bucket
    target = jnp.where(
        live & (mine | other), group * bucket + rank + jnp.where(other, places, 0), -1
    )
    place = lax.broadcasted_iota(jnp.int32, (1, 128), 1)
    wanted = jnp.where(
        (place >= 2 * places) & (place < 2 * places + group_tiles),
        place - 2 * places + row * group_tiles,
        -2,
    )
    total = jnp.where(target == place, came, 0) + jnp.where(column == wanted, arrival, 0)
    full = mine & live & (pos == BASE)
    total = total + jnp.where(full & (place == 2 * places + group_tiles), dev, 0)
    limit = jnp.where(
        place < places,
        width,
        jnp.where(
            place < 2 * places,
            (HALF + 1) * BASE,
            jnp.where(place < 2 * places + group_tiles, 2 * places, HALF),
        ),
    )
    return jnp.minimum(jnp.sum(total, axis=0, keepdims=True), limit - 1)


def encode(
    rows, slabs, cap, bucket, group_tiles,
    slot_tile, pixels, w_space, b_space_h, w_time, b_time_h, gain_h,
    out,
    pix, ws, wt, b_space, b_time, gain, tiles, index_v, index, plane, patch, spatial, lat,
    near0, near1, far0, far1, relay0, relay1, forward_out,
    packed_n, packed_f, rec,
    in_sem, w_sem, send_n, recv_n, send_f, recv_f, send_x, recv_x,
    send_r, send_yn, recv_yn, send_yf, recv_yf,
):
    frames = 2
    near = (near0, near1)
    far, relay = (far0, far1), (relay0, relay1)
    f32, bf16 = jnp.float32, jnp.bfloat16
    row = lax.axis_index("tile")
    slab = lax.axis_index("tm")
    half = lax.div(slab, HALF)
    mine = lax.rem(slab, HALF)
    first = (1 - half) * HALF
    low = half * HALF
    barrier = pltpu.get_barrier_semaphore()
    for k in range(1, slabs):
        pl.semaphore_signal(barrier, inc=1, device_id={"tm": lax.rem(slab + k, slabs)})
    for k in range(1, rows):
        pl.semaphore_signal(barrier, inc=1, device_id={"tile": lax.rem(row + k, rows)})

    steps = slabs // 2
    span = 2 * frames
    origin = lax.div(first, 2)

    def load(z):
        return pltpu.make_async_copy(
            pixels.at[:, pl.ds(z * span, span)], pix.at[z], in_sem.at[z]
        )

    begin = origin

    def conv_at(c):
        return lax.rem(begin + steps - 1 + c, steps)

    def mix_at(k):
        return lax.rem(begin + k, steps)

    small = [
        pltpu.make_async_copy(source, target, w_sem.at[2 + i])
        for i, (source, target) in enumerate(
            ((slot_tile, tiles), (b_space_h, b_space), (b_time_h, b_time), (gain_h, gain))
        )
    ]
    for copy in small:
        copy.start()
    load(conv_at(0)).start()
    ws_copy = pltpu.make_async_copy(w_space, ws, w_sem.at[0])
    ws_copy.start()
    load(conv_at(1)).start()
    wt_copy = pltpu.make_async_copy(w_time, wt, w_sem.at[1])
    wt_copy.start()

    @pl.loop(2, steps)
    def _(c):
        load(conv_at(c)).start()

    count = span * cap
    side = TILE_SIDE
    out_side = side // 2
    area = out_side * out_side
    height = count * area
    step_rows = height // span
    channels = patch.shape[1] // 9
    lanes = plane.shape[-1]
    for piece in range(channels // lanes):
        plane[1, piece, :, 8:16] = jnp.zeros((count, 8, lanes), f32)
    spatial[height - 2 * step_rows:height] = jnp.zeros((2 * step_rows, spatial.shape[1]), bf16)
    edge = lax.rem(lax.broadcasted_iota(jnp.int32, (area, lanes), 0), out_side) == 0

    def conv(z):
        load(z).wait()

        @pl.loop(0, cap)
        def _(p):
            for f in range(span):
                image = f * cap + p
                value = pix[z, p, f].astype(f32).reshape(out_side, 2, side, channels)
                for parity in range(2):
                    rows_of = value[:, parity].reshape(out_side * side, channels)
                    for piece in range(channels // lanes):
                        plane[parity, piece, image, 16:48] = rows_of[
                            :, piece * lanes:(piece + 1) * lanes
                        ]
            for f in range(span):
                image = f * cap + p
                for a in range(3):
                    parity, base = ((1, 8), (0, 16), (1, 16))[a]
                    for b in range(3):
                        for piece in range(channels // lanes):
                            taken = plane[
                                parity, piece, image, pl.ds(base + b - 1, area, stride=2)
                            ]
                            if b == 0:
                                taken = jnp.where(edge, 0.0, taken)
                            at = (3 * a + b) * channels + piece * lanes
                            patch[
                                pl.ds(pl.multiple_of(image * area, area), area),
                                at:at + lanes,
                            ] = taken.astype(bf16)

        total = jnp.dot(patch[...], ws[...], preferred_element_type=f32) + b_space[...]
        active = total / (1.0 + jnp.exp(-total))
        spatial[pl.ds(pl.multiple_of((z + 1) * height, height), height)] = active.astype(bf16)

    def mix(z):
        base = (z + 1) * height
        mixed = spatial[pl.ds(pl.multiple_of(base, step_rows), height)].astype(f32) + b_time[...]
        for lag in range(3):
            mixed = mixed + jnp.dot(
                spatial[pl.ds(pl.multiple_of(base - lag * step_rows, step_rows), height)],
                wt[lag],
                preferred_element_type=f32,
            )
        scale = lax.rsqrt(jnp.mean(mixed * mixed, axis=-1, keepdims=True) + 1e-06)
        value = (mixed * scale * gain[...]).astype(bf16)
        lat[pl.ds(2 * z, 2)] = value.reshape(2, frames, cap, area, value.shape[-1])

    def near_copy(f, j, source):
        return pltpu.make_async_remote_copy(
            src_ref=lat.at[low + j, f],
            dst_ref=near[f].at[pl.ds(source * cap, cap)],
            send_sem=send_n.at[f, j],
            recv_sem=recv_n.at[f, source],
            device_id={"tm": low + j},
        )

    def far_copy(f, j, source):
        return pltpu.make_async_remote_copy(
            src_ref=lat.at[first + j, f, pl.ds(0, BASE)],
            dst_ref=far[f].at[pl.ds(source * BASE, BASE)],
            send_sem=send_f.at[f, j],
            recv_sem=recv_f.at[f, source],
            device_id={"tm": first + j},
        )

    def relay_copy(f, j, source):
        return pltpu.make_async_remote_copy(
            src_ref=lat.at[first + j, f, pl.ds(BASE, BASE)],
            dst_ref=relay[f].at[source],
            send_sem=send_x.at[f, j],
            recv_sem=recv_x.at[f, source],
            device_id={"tm": low + j},
        )

    def forward(f):
        return pltpu.make_async_remote_copy(
            src_ref=forward_out.at[f],
            dst_ref=far[f].at[pl.ds(HALF * BASE, BASE)],
            send_sem=send_r.at[f],
            recv_sem=recv_f.at[f, HALF],
            device_id={"tm": first + mine},
        )

    pick_at = 2 * rows * bucket
    full_at = pick_at + group_tiles

    def send_near(f, place):
        for side_x in range(2):
            j = 2 * place + side_x

            @pl.when(j != mine)
            def _():
                near_copy(f, j, mine).start()

            @pl.when(j == mine)
            def _():
                near[f][pl.ds(mine * cap, cap)] = lat[slab, f]

    def send_far(f, place):
        for side_x in range(2):
            far_copy(f, 2 * place + side_x, mine).start()

    def send_relay(f, place):
        for side_x in range(2):
            j = 2 * place + side_x

            @pl.when(j != mine)
            def _():
                relay_copy(f, j, mine).start()

            @pl.when(j == mine)
            def _():
                relay[f][mine] = lat[first + mine, f, BASE:cap]

    def run_relay(f):
        for k in range(1, HALF):
            relay_copy(f, mine, lax.rem(mine + k, HALF)).wait_recv()
        forward_out[f] = relay[f][index[0, full_at]]
        forward(f).start()


    def tile_near(f, k):
        to = lax.rem(row + k, rows)
        return pltpu.make_async_remote_copy(
            src_ref=packed_n.at[f, pl.ds(to * bucket, bucket)],
            dst_ref=rec.at[f, pl.ds((half * rows + row) * bucket, bucket)],
            send_sem=send_yn.at[f, k - 1],
            recv_sem=recv_yn.at[f, k - 1],
            device_id={"tile": to},
        )

    def tile_far(f, k):
        to = lax.rem(row + k, rows)
        return pltpu.make_async_remote_copy(
            src_ref=packed_f.at[f, pl.ds(to * bucket, bucket)],
            dst_ref=rec.at[f, pl.ds(((1 - half) * rows + row) * bucket, bucket)],
            send_sem=send_yf.at[f, k - 1],
            recv_sem=recv_yf.at[f, k - 1],
            device_id={"tile": to},
        )

    def run_near(f):
        for k in range(1, HALF):
            near_copy(f, mine, lax.rem(mine + k, HALF)).wait_recv()

        @pl.loop(0, rows * bucket)
        def _(i):
            packed_n[f, i] = near[f][index[0, i]]

        for k in range(1, rows):
            tile_near(f, k).start()
        own = pl.ds(row * bucket, bucket)
        rec[f, pl.ds((half * rows + row) * bucket, bucket)] = packed_n[f, own]

    def run_far(f):
        for j in range(HALF):
            far_copy(f, mine, j).wait_recv()
        forward(f).wait_recv()

        @pl.loop(0, rows * bucket)
        def _(i):
            packed_f[f, i] = far[f][index[0, rows * bucket + i]]

        for k in range(1, rows):
            tile_far(f, k).start()
        own = pl.ds(row * bucket, bucket)
        rec[f, pl.ds(((1 - half) * rows + row) * bucket, bucket)] = packed_f[f, own]

    for copy in small:
        copy.wait()
    index_v[...] = index_row(tiles[...], rows, cap, bucket, group_tiles, row, half)
    index_copy = pltpu.make_async_copy(index_v, index, w_sem.at[6])
    index_copy.start()
    ws_copy.wait()
    conv(conv_at(0))
    index_copy.wait()
    wt_copy.wait()
    pl.semaphore_wait(barrier, slabs + rows - 2)

    @pl.loop(0, steps)
    def _(k):
        @pl.when(k < steps - 1)
        def _():
            conv(conv_at(k + 1))

        mix(mix_at(k))

        @pl.when(k == 0)
        def _():
            send_relay(0, 0)
            send_far(0, 0)

        @pl.when(k == 1)
        def _():
            send_relay(0, 1)
            send_far(0, 1)

        @pl.when(k == 2)
        def _():
            send_near(0, 0)
            send_near(1, 0)

        @pl.when(k == 3)
        def _():
            send_near(0, 1)
            send_near(1, 1)

    send_relay(1, 0)
    send_relay(1, 1)
    run_relay(0)
    send_far(1, 0)
    send_far(1, 1)
    run_near(0)
    run_far(0)
    run_relay(1)
    run_near(1)
    run_far(1)

    for k in range(1, rows):
        for f in range(frames):
            tile_near(f, k).wait_recv()
            tile_far(f, k).wait_recv()

    @pl.loop(0, group_tiles)
    def _(i):
        for f in range(frames):
            out[i, f] = rec[f, index[0, pick_at + i]]

    for k in range(1, HALF):
        for f in range(frames):
            near_copy(f, lax.rem(mine + k, HALF), mine).wait_send()
    for f in range(frames):
        for j in range(HALF):
            far_copy(f, j, mine).wait_send()
        for k in range(1, HALF):
            relay_copy(f, lax.rem(mine + k, HALF), mine).wait_send()
        forward(f).wait_send()
        for k in range(1, rows):
            tile_far(f, k).wait_send()
    for k in range(1, rows):
        for f in range(frames):
            tile_near(f, k).wait_send()


def body_two_blocks(rows, slabs, pixels, slot_tile, w_space, b_space, w_time, b_time, gain):
    cap, all_frames, pix_count, channels = pixels.shape
    features = w_space.shape[-1]
    frames = all_frames // slabs
    group_tiles = cap // 2 * slabs
    per_group = (cap + rows - 1) // rows
    bucket = per_group * 3
    area = pix_count // 4
    span = 2 * frames
    steps = slabs // 2
    height = span * cap * area
    vmem = pl.BlockSpec(memory_space=pltpu.VMEM)
    hbm = pl.BlockSpec(memory_space=pl.ANY)
    bf16, f32 = jnp.bfloat16, jnp.float32
    dma = pltpu.SemaphoreType.DMA
    arrivals = (HALF + 1) * BASE

    def held(*lead):
        return pltpu.VMEM(lead + (area, features), bf16)

    return pl.pallas_call(
        functools.partial(encode, rows, slabs, cap, bucket, group_tiles),
        out_shape=jax.ShapeDtypeStruct((group_tiles, frames, area, features), bf16),
        in_specs=[hbm] * 7,
        out_specs=vmem,
        scratch_shapes=[
            pltpu.VMEM((steps, cap, span, pix_count, channels), bf16),
            pltpu.VMEM((9 * channels, features), bf16),
            pltpu.VMEM((3, features, features), bf16),
            pltpu.VMEM((1, features), f32),
            pltpu.VMEM((1, features), f32),
            pltpu.VMEM((1, features), f32),
            pltpu.VMEM((1, slot_tile.shape[0]), jnp.int32),
            pltpu.VMEM((1, 128), jnp.int32),
            pltpu.SMEM((1, 128), jnp.int32),
            pltpu.VMEM((2, channels // 128, span * cap, 48, 128), f32),
            pltpu.VMEM((height, 9 * channels), bf16),
            pltpu.VMEM(((steps + 1) * height, features), bf16),
            held(slabs, frames, cap),
            held(HALF * cap), held(HALF * cap), held(arrivals), held(arrivals),
            held(HALF, BASE), held(HALF, BASE), held(frames, BASE),
            held(frames, rows * bucket), held(frames, rows * bucket),
            held(frames, 2 * rows * bucket),
            dma((steps,)), dma((7,)),
            dma((frames, HALF)), dma((frames, HALF)), dma((frames, HALF)), dma((frames, HALF + 1)),
            dma((frames, HALF)), dma((frames, HALF)), dma((frames,)),
            dma((frames, rows - 1)), dma((frames, rows - 1)), dma((frames, rows - 1)), dma((frames, rows - 1)),
        ],
        compiler_params=pltpu.CompilerParams(
            collective_id=1, has_side_effects=True, vmem_limit_bytes=62 << 20
        ),
    )(
        slot_tile[None], pixels, w_space.reshape(9 * channels, features),
        b_space[None], w_time, b_time[None], gain[None],
    )


def solution(mesh):
    rows, slabs = mesh.shape["tile"], mesh.shape["tm"]
    plan = body_two_blocks if slabs == 2 * HALF else body
    return jax.shard_map(
        functools.partial(plan, rows, slabs),
        mesh=mesh,
        in_specs=(P(("tile", "tm"), None, None, None), P(), P(), P(), P(), P(), P()),
        out_specs=P("tile", "tm", None, None),
        check_vma=False,
    )
```

```python
import functools

import jax
import jax.numpy as jnp
from jax import lax
from jax.experimental import pallas as pl
from jax.experimental.pallas import tpu as pltpu
from jax.sharding import PartitionSpec as P

TILE_SIDE = 8
HALF = 4
BASE = 3


def conv_space(raw_tiles, w_space, b_space):
    number, frames, pix_count, channels = raw_tiles.shape
    grid = raw_tiles.reshape(number * frames, TILE_SIDE, TILE_SIDE, channels)
    total = lax.conv_general_dilated(
        grid,
        w_space,
        (2, 2),
        ((1, 1), (1, 1)),
        dimension_numbers=("NHWC", "HWIO", "NHWC"),
        preferred_element_type=jnp.float32,
    )
    active = jax.nn.silu(total + b_space)
    half_side = TILE_SIDE // 2
    return active.astype(jnp.bfloat16).reshape(number, frames, half_side * half_side, -1)


def tables(slot_tile, rows, groups, bucket, group_tiles, my_row):
    table = slot_tile.reshape(rows, -1)
    width = table.shape[1]
    group_of = jnp.where(table >= 0, lax.div(table, group_tiles), groups)
    pos = jnp.arange(width, dtype=jnp.int32)
    earlier = pos[None, :] < pos[:, None]
    same = (group_of[:, :, None] == group_of[:, None, :]) & earlier[None]
    rank = jnp.sum(same.astype(jnp.int32), axis=2)
    target = group_of * bucket + rank
    own_target = lax.dynamic_index_in_dim(target, my_row, 0, keepdims=False)
    own_live = lax.dynamic_index_in_dim(table, my_row, 0, keepdims=False) >= 0
    own_target = jnp.where(own_live, own_target, -1)
    places = jnp.arange(groups * bucket, dtype=jnp.int32)
    send_idx = jnp.sum(
        jnp.where(own_target[None, :] == places[:, None], pos[None, :], 0), axis=1
    )
    wanted = my_row * group_tiles + jnp.arange(group_tiles, dtype=jnp.int32)
    arrived = jnp.arange(rows, dtype=jnp.int32)[:, None] * bucket + rank
    pick_idx = jnp.sum(
        jnp.where(
            table.reshape(-1)[None, :] == wanted[:, None], arrived.reshape(-1)[None, :], 0
        ),
        axis=1,
    )
    return send_idx, pick_idx


def kernel(
    rows, slabs, cap, bucket, group_tiles,
    send_idx, pick_idx, src, w_time, b_time, gain, out,
    got1a, got1b, out2, got2a, got2b, feats, halo, total,
    send1, recv1, send2, recv2, send3, recv3,
):
    frames = 2
    got1, got2 = (got1a, got1b), (got2a, got2b)
    row = lax.axis_index("tile")
    slab = lax.axis_index("tm")
    barrier = pltpu.get_barrier_semaphore()
    for k in range(1, slabs):
        pl.semaphore_signal(barrier, inc=1, device_id={"tm": lax.rem(slab + k, slabs)})
    for k in range(1, rows):
        pl.semaphore_signal(barrier, inc=1, device_id={"tile": lax.rem(row + k, rows)})
    pl.semaphore_wait(barrier, slabs + rows - 2)

    def copy1(f, k):
        to = lax.rem(slab + k, slabs)
        return pltpu.make_async_remote_copy(
            src_ref=src.at[:, to * frames + f],
            dst_ref=got1[f].at[pl.ds(slab * cap, cap)],
            send_sem=send1.at[f, k - 1],
            recv_sem=recv1.at[f, k - 1],
            device_id={"tm": to},
        )

    def copy2(f, k):
        to = lax.rem(row + k, rows)
        return pltpu.make_async_remote_copy(
            src_ref=out2.at[f, pl.ds(to * bucket, bucket)],
            dst_ref=got2[f].at[pl.ds(row * bucket, bucket)],
            send_sem=send2.at[f, k - 1],
            recv_sem=recv2.at[f, k - 1],
            device_id={"tile": to},
        )

    def copy3(f):
        return pltpu.make_async_remote_copy(
            src_ref=feats.at[f],
            dst_ref=halo.at[f],
            send_sem=send3.at[f],
            recv_sem=recv3.at[f],
            device_id={"tm": lax.rem(slab + 1, slabs)},
        )

    for f in range(frames):
        for k in range(1, slabs):
            copy1(f, k).start()
    for f in range(frames):
        got1[f][pl.ds(slab * cap, cap)] = src[:, slab * frames + f]
        for k in range(1, slabs):
            copy1(f, k).wait_recv()

        @pl.loop(0, rows * bucket)
        def _(i):
            out2[f, i] = got1[f][send_idx[i]]

        for k in range(1, rows):
            copy2(f, k).start()

        @pl.loop(0, bucket)
        def _(j):
            got2[f][row * bucket + j] = got1[f][send_idx[row * bucket + j]]

        for k in range(1, rows):
            copy2(f, k).wait_recv()

        @pl.loop(0, group_tiles)
        def _(i):
            feats[f, i] = got2[f][pick_idx[i]]

        @pl.when(slab < slabs - 1)
        def _():
            copy3(f).start()

    part = group_tiles // 2
    height = part * 16

    def flat(value):
        return value.reshape(height, value.shape[-1])

    @pl.loop(0, 2)
    def _(c):
        at = pl.ds(c * part, part)
        own = [flat(feats[0, at]), flat(feats[1, at])]
        for f in range(frames):
            mixed = own[f].astype(jnp.float32) + b_time[...]
            for lag in range(f + 1):
                mixed = mixed + jnp.dot(
                    own[f - lag], w_time[lag], preferred_element_type=jnp.float32
                )
            total[f, c] = mixed

    for f in range(frames):

        @pl.when(slab > 0)
        def _():
            copy3(f).wait_recv()

        @pl.when(slab == 0)
        def _():
            halo[f] = jnp.zeros(halo.shape[1:], halo.dtype)

    @pl.loop(0, 2)
    def _(c):
        at = pl.ds(c * part, part)
        before = [flat(halo[0, at]), flat(halo[1, at])]
        for f in range(frames):
            mixed = total[f, c]
            for lag in range(f + 1, 3):
                mixed = mixed + jnp.dot(
                    before[2 + f - lag], w_time[lag], preferred_element_type=jnp.float32
                )
            scale = lax.rsqrt(jnp.mean(mixed * mixed, axis=-1, keepdims=True) + 1e-06)
            value = (mixed * scale * gain[...]).astype(jnp.bfloat16)
            out[at, f] = value.reshape(part, 16, value.shape[-1])

    for f in range(frames):
        for k in range(1, slabs):
            copy1(f, k).wait_send()
        for k in range(1, rows):
            copy2(f, k).wait_send()

        @pl.when(slab < slabs - 1)
        def _():
            copy3(f).wait_send()


def body(rows, slabs, pixels, slot_tile, w_space, b_space, w_time, b_time, gain):
    cap, all_frames = pixels.shape[:2]
    channels = w_space.shape[-1]
    group_tiles = cap // 2 * slabs
    per_group = (cap + rows - 1) // rows
    bucket = per_group * 3 * (slabs // 4)
    frames = all_frames // slabs
    send_idx, pick_idx = tables(
        slot_tile, rows, rows, bucket, group_tiles, lax.axis_index("tile")
    )
    spatial = conv_space(pixels, w_space, b_space)
    vmem = pl.BlockSpec(memory_space=pltpu.VMEM)
    smem = pl.BlockSpec(memory_space=pltpu.SMEM)
    bf16 = jnp.bfloat16
    dma = pltpu.SemaphoreType.DMA
    return pl.pallas_call(
        functools.partial(kernel, rows, slabs, cap, bucket, group_tiles),
        out_shape=jax.ShapeDtypeStruct((group_tiles, frames, 16, channels), bf16),
        in_specs=[smem, smem, vmem, vmem, vmem, vmem],
        out_specs=vmem,
        scratch_shapes=[
            pltpu.VMEM((slabs * cap, 16, channels), bf16),
            pltpu.VMEM((slabs * cap, 16, channels), bf16),
            pltpu.VMEM((frames, rows * bucket, 16, channels), bf16),
            pltpu.VMEM((rows * bucket, 16, channels), bf16),
            pltpu.VMEM((rows * bucket, 16, channels), bf16),
            pltpu.VMEM((frames, group_tiles, 16, channels), bf16),
            pltpu.VMEM((frames, group_tiles, 16, channels), bf16),
            pltpu.VMEM((frames, 2, group_tiles * 8, channels), jnp.float32),
            dma((frames, slabs - 1)),
            dma((frames, slabs - 1)),
            dma((frames, rows - 1)),
            dma((frames, rows - 1)),
            dma((frames,)),
            dma((frames,)),
        ],
        compiler_params=pltpu.CompilerParams(collective_id=0, has_side_effects=True),
    )(send_idx, pick_idx, spatial, w_time, b_time[None], gain[None])


def index_row(tiles, rows, cap, bucket, group_tiles, row, half):
    slots = tiles.shape[1]
    width = HALF * cap
    shape = (slots, slots)
    along = lax.broadcasted_iota(jnp.int32, shape, 1)
    down = lax.broadcasted_iota(jnp.int32, shape, 0)
    spread = jnp.broadcast_to(tiles, shape)
    column = jnp.sum(jnp.where(along == down, spread, 0), axis=1, keepdims=True)

    def key_of(ids, tile):
        key = jnp.where(tile < 0, rows, 0)
        for k in range(1, rows):
            key = key + jnp.where(tile >= k * group_tiles, 1, 0)
        block = jnp.zeros_like(ids)
        for k in range(1, slots // width):
            block = block + jnp.where(ids >= k * width, 1, 0)
        return block, key

    ids = lax.broadcasted_iota(jnp.int32, (slots, 1), 0)
    block, group = key_of(ids, column)
    lane = lax.broadcasted_iota(jnp.int32, (1, slots), 1)
    block_r, group_r = key_of(lane, tiles)
    same = (block * (rows + 1) + group) == (block_r * (rows + 1) + group_r)
    rank = jnp.sum(jnp.where(same & (along < down), 1, 0), axis=1, keepdims=True)
    part = block % 2
    arrival = (part * rows + block // 2) * bucket + rank
    inside = ids - block * width
    dev = jnp.zeros_like(ids)
    for k in range(1, HALF):
        dev = dev + jnp.where(inside >= k * cap, 1, 0)
    pos = inside - dev * cap
    came = jnp.where(pos < BASE, dev * BASE + pos, HALF * BASE + pos - BASE)
    came = jnp.where(block == row * 2 + half, inside, came)
    mine = block == row * 2 + half
    other = block == row * 2 + 1 - half
    live = column >= 0
    places = rows * bucket
    target = jnp.where(
        live & (mine | other), group * bucket + rank + jnp.where(other, places, 0), -1
    )
    place = lax.broadcasted_iota(jnp.int32, (1, 128), 1)
    wanted = jnp.where(
        (place >= 2 * places) & (place < 2 * places + group_tiles),
        place - 2 * places + row * group_tiles,
        -2,
    )
    total = jnp.where(target == place, came, 0) + jnp.where(column == wanted, arrival, 0)
    full = mine & live & (pos == BASE)
    total = total + jnp.where(full & (place == 2 * places + group_tiles), dev, 0)
    limit = jnp.where(
        place < places,
        width,
        jnp.where(
            place < 2 * places,
            (HALF + 1) * BASE,
            jnp.where(place < 2 * places + group_tiles, 2 * places, HALF),
        ),
    )
    return jnp.minimum(jnp.sum(total, axis=0, keepdims=True), limit - 1)


def encode(
    rows, slabs, cap, bucket, group_tiles, pieces,
    slot_tile, pixels, w_space, b_space_h, w_time, b_time_h, gain_h,
    out,
    pix, ws, wt, b_space, b_time, gain, tiles, index_v, index, plane, spatial, lat,
    *landing,
):
    frames = 2
    near, far, relay = (landing[i * frames * pieces:(i + 1) * frames * pieces] for i in range(3))
    (
        forward_out, packed_n, packed_f, rec,
        in_sem, w_sem, send_n, recv_n, send_f, recv_f, send_x, recv_x,
        send_r, send_yn, recv_yn, send_yf, recv_yf,
    ) = landing[3 * frames * pieces:]
    parts = frames * pieces
    breadth = lat.shape[-1]
    f32, bf16 = jnp.float32, jnp.bfloat16
    row = lax.axis_index("tile")
    slab = lax.axis_index("tm")
    half = lax.div(slab, HALF)
    mine = lax.rem(slab, HALF)
    first = (1 - half) * HALF
    low = half * HALF
    barrier = pltpu.get_barrier_semaphore()
    for k in range(1, slabs):
        pl.semaphore_signal(barrier, inc=1, device_id={"tm": lax.rem(slab + k, slabs)})
    for k in range(1, rows):
        pl.semaphore_signal(barrier, inc=1, device_id={"tile": lax.rem(row + k, rows)})

    steps = slabs // 2
    span = 2 * frames
    origin = lax.div(first, 2)

    def load_frame(z, f):
        return pltpu.make_async_copy(
            pixels.at[:, z * span + f], pix.at[z, f], in_sem.at[z, f]
        )

    def load(z):
        for f in range(span):
            load_frame(z, f).start()

    def conv_at(c):
        return lax.rem(c + 1 - half, steps)

    def mix_at(k):
        return lax.rem(origin + k, steps)

    def conv_before(k):
        return jnp.minimum(k + 2 - half, steps)

    small = [
        pltpu.make_async_copy(source, target, w_sem.at[2 + i])
        for i, (source, target) in enumerate(
            ((slot_tile, tiles), (b_space_h, b_space), (b_time_h, b_time), (gain_h, gain))
        )
    ]
    for copy in small:
        copy.start()
    load(conv_at(0))
    ws_copy = pltpu.make_async_copy(w_space, ws, w_sem.at[0])
    ws_copy.start()
    load(conv_at(1))
    wt_copy = pltpu.make_async_copy(w_time, wt, w_sem.at[1])
    wt_copy.start()

    @pl.loop(2, steps)
    def _(c):
        load(conv_at(c))

    count = span * cap
    side = TILE_SIDE
    out_side = side // 2
    area = out_side * out_side
    height = count * area
    step_rows = height // span
    channels = pix.shape[-1]
    lanes = plane.shape[-1]
    for piece in range(channels // lanes):
        plane[1, piece, :, 8:16] = jnp.zeros((count, 8, lanes), f32)
    spatial[height - 2 * step_rows:height] = jnp.zeros((2 * step_rows, spatial.shape[1]), bf16)
    edge = lax.rem(lax.broadcasted_iota(jnp.int32, (count, area, lanes), 1), out_side) == 0

    def conv(z):
        for f in range(span):
            load_frame(z, f).wait()

        value = pix[z].astype(f32).reshape(count, out_side, 2, side, channels)
        for parity in range(2):
            rows_of = value[:, :, parity].reshape(count, out_side * side, channels)
            for piece in range(channels // lanes):
                plane[parity, piece, :, 16:48] = rows_of[:, :, piece * lanes:(piece + 1) * lanes]

        parts = []
        for a in range(3):
            parity, base = ((1, 8), (0, 16), (1, 16))[a]
            for b in range(3):
                for piece in range(channels // lanes):
                    taken = plane[parity, piece, :, pl.ds(base + b - 1, area, stride=2)]
                    if b == 0:
                        taken = jnp.where(edge, 0.0, taken)
                    parts.append(taken.reshape(height, lanes).astype(bf16))
        patch = jnp.concatenate(parts, axis=1)
        total = jnp.dot(patch, ws[...], preferred_element_type=f32) + b_space[...]
        active = total / (1.0 + jnp.exp(-total))
        spatial[pl.ds(pl.multiple_of((z + 1) * height, height), height)] = active.astype(bf16)

    def mix(z):
        base = (z + 1) * height
        mixed = spatial[pl.ds(pl.multiple_of(base, step_rows), height)].astype(f32) + b_time[...]
        for lag in range(3):
            mixed = mixed + jnp.dot(
                spatial[pl.ds(pl.multiple_of(base - lag * step_rows, step_rows), height)],
                wt[lag],
                preferred_element_type=f32,
            )
        scale = lax.rsqrt(jnp.mean(mixed * mixed, axis=-1, keepdims=True) + 1e-06)
        value = (mixed * scale * gain[...]).astype(bf16)
        for h in range(pieces):
            lat[h, pl.ds(2 * z, 2)] = value[:, h * breadth:(h + 1) * breadth].reshape(
                2, frames, cap, area, breadth
            )

    def near_copy(q, j, source):
        return pltpu.make_async_remote_copy(
            src_ref=lat.at[q % pieces, low + j, q // pieces],
            dst_ref=near[q].at[pl.ds(source * cap, cap)],
            send_sem=send_n.at[q, j],
            recv_sem=recv_n.at[q, source],
            device_id={"tm": low + j},
        )

    def far_copy(q, j, source):
        return pltpu.make_async_remote_copy(
            src_ref=lat.at[q % pieces, first + j, q // pieces, pl.ds(0, BASE)],
            dst_ref=far[q].at[pl.ds(source * BASE, BASE)],
            send_sem=send_f.at[q, j],
            recv_sem=recv_f.at[q, source],
            device_id={"tm": first + j},
        )

    def relay_copy(q, j, source):
        return pltpu.make_async_remote_copy(
            src_ref=lat.at[q % pieces, first + j, q // pieces, pl.ds(BASE, BASE)],
            dst_ref=relay[q].at[source],
            send_sem=send_x.at[q, j],
            recv_sem=recv_x.at[q, source],
            device_id={"tm": low + j},
        )

    def forward(q):
        return pltpu.make_async_remote_copy(
            src_ref=forward_out.at[q],
            dst_ref=far[q].at[pl.ds(HALF * BASE, BASE)],
            send_sem=send_r.at[q],
            recv_sem=recv_f.at[q, HALF],
            device_id={"tm": first + mine},
        )

    pick_at = 2 * rows * bucket
    full_at = pick_at + group_tiles

    def send_near(q, place):
        for side_x in range(2):
            j = 2 * place + side_x

            @pl.when(j != mine)
            def _():
                near_copy(q, j, mine).start()

            @pl.when(j == mine)
            def _():
                near[q][pl.ds(mine * cap, cap)] = lat[q % pieces, slab, q // pieces]

    def send_far(q, place):
        for side_x in range(2):
            far_copy(q, 2 * place + side_x, mine).start()

    def send_relay(q, place):
        for side_x in range(2):
            j = 2 * place + side_x

            @pl.when(j != mine)
            def _():
                relay_copy(q, j, mine).start()

            @pl.when(j == mine)
            def _():
                relay[q][mine] = lat[q % pieces, first + mine, q // pieces, BASE:cap]

    def run_relay(q):
        for k in range(1, HALF):
            relay_copy(q, mine, lax.rem(mine + k, HALF)).wait_recv()
        forward_out[q] = relay[q][index[0, full_at]]
        forward(q).start()


    def tile_near(q, k):
        to = lax.rem(row + k, rows)
        return pltpu.make_async_remote_copy(
            src_ref=packed_n.at[q, pl.ds(to * bucket, bucket)],
            dst_ref=rec.at[q, pl.ds((half * rows + row) * bucket, bucket)],
            send_sem=send_yn.at[q, k - 1],
            recv_sem=recv_yn.at[q, k - 1],
            device_id={"tile": to},
        )

    def tile_far(q, k):
        to = lax.rem(row + k, rows)
        return pltpu.make_async_remote_copy(
            src_ref=packed_f.at[q, pl.ds(to * bucket, bucket)],
            dst_ref=rec.at[q, pl.ds(((1 - half) * rows + row) * bucket, bucket)],
            send_sem=send_yf.at[q, k - 1],
            recv_sem=recv_yf.at[q, k - 1],
            device_id={"tile": to},
        )

    def run_near(q):
        for k in range(1, HALF):
            near_copy(q, mine, lax.rem(mine + k, HALF)).wait_recv()

        @pl.loop(0, rows * bucket)
        def _(i):
            packed_n[q, i] = near[q][index[0, i]]

        for k in range(1, rows):
            tile_near(q, k).start()
        own = pl.ds(row * bucket, bucket)
        rec[q, pl.ds((half * rows + row) * bucket, bucket)] = packed_n[q, own]

    def run_far(q):
        for j in range(HALF):
            far_copy(q, mine, j).wait_recv()
        forward(q).wait_recv()

        @pl.loop(0, rows * bucket)
        def _(i):
            packed_f[q, i] = far[q][index[0, rows * bucket + i]]

        for k in range(1, rows):
            tile_far(q, k).start()
        own = pl.ds(row * bucket, bucket)
        rec[q, pl.ds(((1 - half) * rows + row) * bucket, bucket)] = packed_f[q, own]

    for copy in small:
        copy.wait()
    index_v[...] = index_row(tiles[...], rows, cap, bucket, group_tiles, row, half)
    index_copy = pltpu.make_async_copy(index_v, index, w_sem.at[6])
    index_copy.start()
    ws_copy.wait()
    conv(conv_at(0))
    index_copy.wait()
    wt_copy.wait()
    pl.semaphore_wait(barrier, slabs + rows - 2)

    @pl.loop(0, steps)
    def _(k):
        @pl.loop(jnp.where(k == 0, 1, conv_before(k - 1)), conv_before(k))
        def _(c):
            conv(conv_at(c))

        mix(mix_at(k))

        @pl.when(k == 0)
        def _():
            send_relay(0, 0)
            send_relay(1, 0)
            send_far(0, 0)
            send_far(1, 0)

        @pl.when(k == 1)
        def _():
            send_relay(0, 1)
            send_relay(1, 1)
            send_far(0, 1)
            send_far(1, 1)

        @pl.when(k == 2)
        def _():
            send_near(0, 0)
            send_near(1, 0)

        @pl.when(k == 3)
        def _():
            send_near(0, 1)
            send_near(1, 1)
            run_relay(0)
            run_relay(1)

    send_near(2, 0)
    send_near(2, 1)
    send_relay(2, 0)
    send_relay(2, 1)
    send_far(2, 0)
    send_far(2, 1)
    send_near(3, 0)
    send_near(3, 1)
    send_relay(3, 0)
    send_relay(3, 1)
    send_far(3, 0)
    send_far(3, 1)
    run_near(0)
    run_near(1)
    run_far(0)
    run_far(1)
    run_near(2)
    run_relay(2)
    run_far(2)
    run_near(3)
    run_relay(3)
    run_far(3)

    for k in range(1, rows):
        for q in range(parts):
            tile_near(q, k).wait_recv()
            tile_far(q, k).wait_recv()

    @pl.loop(0, group_tiles)
    def _(i):
        for q in range(parts):
            h = q % pieces
            out[i, q // pieces, :, h * breadth:(h + 1) * breadth] = rec[q, index[0, pick_at + i]]

    for q in range(parts):
        for k in range(1, HALF):
            near_copy(q, lax.rem(mine + k, HALF), mine).wait_send()
            relay_copy(q, lax.rem(mine + k, HALF), mine).wait_send()
        for j in range(HALF):
            far_copy(q, j, mine).wait_send()
        forward(q).wait_send()
        for k in range(1, rows):
            tile_far(q, k).wait_send()
            tile_near(q, k).wait_send()


def body_two_blocks(rows, slabs, pixels, slot_tile, w_space, b_space, w_time, b_time, gain):
    cap, all_frames, pix_count, channels = pixels.shape
    features = w_space.shape[-1]
    frames = all_frames // slabs
    group_tiles = cap // 2 * slabs
    per_group = (cap + rows - 1) // rows
    bucket = per_group * 3
    area = pix_count // 4
    span = 2 * frames
    steps = slabs // 2
    height = span * cap * area
    vmem = pl.BlockSpec(memory_space=pltpu.VMEM)
    hbm = pl.BlockSpec(memory_space=pl.ANY)
    bf16, f32 = jnp.bfloat16, jnp.float32
    dma = pltpu.SemaphoreType.DMA
    arrivals = (HALF + 1) * BASE
    pieces = 2
    parts = frames * pieces

    def held(*lead):
        return pltpu.VMEM(lead + (area, features // pieces), bf16)

    return pl.pallas_call(
        functools.partial(encode, rows, slabs, cap, bucket, group_tiles, pieces),
        out_shape=jax.ShapeDtypeStruct((group_tiles, frames, area, features), bf16),
        in_specs=[hbm] * 7,
        out_specs=vmem,
        scratch_shapes=[
            pltpu.VMEM((steps, span, cap, pix_count, channels), bf16),
            pltpu.VMEM((9 * channels, features), bf16),
            pltpu.VMEM((3, features, features), bf16),
            pltpu.VMEM((1, features), f32),
            pltpu.VMEM((1, features), f32),
            pltpu.VMEM((1, features), f32),
            pltpu.VMEM((1, slot_tile.shape[0]), jnp.int32),
            pltpu.VMEM((1, 128), jnp.int32),
            pltpu.SMEM((1, 128), jnp.int32),
            pltpu.VMEM((2, channels // 128, span * cap, 48, 128), f32),
            pltpu.VMEM(((steps + 1) * height, features), bf16),
            held(pieces, slabs, frames, cap),
            *[held(HALF * cap)] * parts, *[held(arrivals)] * parts, *[held(HALF, BASE)] * parts,
            held(parts, BASE),
            held(parts, rows * bucket), held(parts, rows * bucket), held(parts, 2 * rows * bucket),
            dma((steps, span)), dma((7,)),
            dma((parts, HALF)), dma((parts, HALF)), dma((parts, HALF)), dma((parts, HALF + 1)),
            dma((parts, HALF)), dma((parts, HALF)), dma((parts,)),
            dma((parts, rows - 1)), dma((parts, rows - 1)), dma((parts, rows - 1)), dma((parts, rows - 1)),
        ],
        compiler_params=pltpu.CompilerParams(
            collective_id=1, has_side_effects=True, vmem_limit_bytes=62 << 20
        ),
    )(
        slot_tile[None], pixels, w_space.reshape(9 * channels, features),
        b_space[None], w_time, b_time[None], gain[None],
    )


def solution(mesh):
    rows, slabs = mesh.shape["tile"], mesh.shape["tm"]
    plan = body_two_blocks if slabs == 2 * HALF else body
    return jax.shard_map(
        functools.partial(plan, rows, slabs),
        mesh=mesh,
        in_specs=(P(("tile", "tm"), None, None, None), P(), P(), P(), P(), P(), P()),
        out_specs=P("tile", "tm", None, None),
        check_vma=False,
    )
```

```python
import functools

import jax
import jax.numpy as jnp
from jax import lax
from jax.experimental import pallas as pl
from jax.experimental.pallas import tpu as pltpu
from jax.sharding import PartitionSpec as P

TILE_SIDE = 8
HALF = 4
BASE = 3


def conv_space(raw_tiles, w_space, b_space):
    number, frames, pix_count, channels = raw_tiles.shape
    grid = raw_tiles.reshape(number * frames, TILE_SIDE, TILE_SIDE, channels)
    total = lax.conv_general_dilated(
        grid,
        w_space,
        (2, 2),
        ((1, 1), (1, 1)),
        dimension_numbers=("NHWC", "HWIO", "NHWC"),
        preferred_element_type=jnp.float32,
    )
    active = jax.nn.silu(total + b_space)
    half_side = TILE_SIDE // 2
    return active.astype(jnp.bfloat16).reshape(number, frames, half_side * half_side, -1)


def tables(slot_tile, rows, groups, bucket, group_tiles, my_row):
    table = slot_tile.reshape(rows, -1)
    width = table.shape[1]
    group_of = jnp.where(table >= 0, lax.div(table, group_tiles), groups)
    pos = jnp.arange(width, dtype=jnp.int32)
    earlier = pos[None, :] < pos[:, None]
    same = (group_of[:, :, None] == group_of[:, None, :]) & earlier[None]
    rank = jnp.sum(same.astype(jnp.int32), axis=2)
    target = group_of * bucket + rank
    own_target = lax.dynamic_index_in_dim(target, my_row, 0, keepdims=False)
    own_live = lax.dynamic_index_in_dim(table, my_row, 0, keepdims=False) >= 0
    own_target = jnp.where(own_live, own_target, -1)
    places = jnp.arange(groups * bucket, dtype=jnp.int32)
    send_idx = jnp.sum(
        jnp.where(own_target[None, :] == places[:, None], pos[None, :], 0), axis=1
    )
    wanted = my_row * group_tiles + jnp.arange(group_tiles, dtype=jnp.int32)
    arrived = jnp.arange(rows, dtype=jnp.int32)[:, None] * bucket + rank
    pick_idx = jnp.sum(
        jnp.where(
            table.reshape(-1)[None, :] == wanted[:, None], arrived.reshape(-1)[None, :], 0
        ),
        axis=1,
    )
    return send_idx, pick_idx


def kernel(
    rows, slabs, cap, bucket, group_tiles,
    send_idx, pick_idx, src, w_time, b_time, gain, out,
    got1a, got1b, out2, got2a, got2b, feats, halo, total,
    send1, recv1, send2, recv2, send3, recv3,
):
    frames = 2
    got1, got2 = (got1a, got1b), (got2a, got2b)
    row = lax.axis_index("tile")
    slab = lax.axis_index("tm")
    barrier = pltpu.get_barrier_semaphore()
    for k in range(1, slabs):
        pl.semaphore_signal(barrier, inc=1, device_id={"tm": lax.rem(slab + k, slabs)})
    for k in range(1, rows):
        pl.semaphore_signal(barrier, inc=1, device_id={"tile": lax.rem(row + k, rows)})
    pl.semaphore_wait(barrier, slabs + rows - 2)

    def copy1(f, k):
        to = lax.rem(slab + k, slabs)
        return pltpu.make_async_remote_copy(
            src_ref=src.at[:, to * frames + f],
            dst_ref=got1[f].at[pl.ds(slab * cap, cap)],
            send_sem=send1.at[f, k - 1],
            recv_sem=recv1.at[f, k - 1],
            device_id={"tm": to},
        )

    def copy2(f, k):
        to = lax.rem(row + k, rows)
        return pltpu.make_async_remote_copy(
            src_ref=out2.at[f, pl.ds(to * bucket, bucket)],
            dst_ref=got2[f].at[pl.ds(row * bucket, bucket)],
            send_sem=send2.at[f, k - 1],
            recv_sem=recv2.at[f, k - 1],
            device_id={"tile": to},
        )

    def copy3(f):
        return pltpu.make_async_remote_copy(
            src_ref=feats.at[f],
            dst_ref=halo.at[f],
            send_sem=send3.at[f],
            recv_sem=recv3.at[f],
            device_id={"tm": lax.rem(slab + 1, slabs)},
        )

    for f in range(frames):
        for k in range(1, slabs):
            copy1(f, k).start()
    for f in range(frames):
        got1[f][pl.ds(slab * cap, cap)] = src[:, slab * frames + f]
        for k in range(1, slabs):
            copy1(f, k).wait_recv()

        @pl.loop(0, rows * bucket, unroll=8)
        def _(i):
            out2[f, i] = got1[f][send_idx[i]]

        for k in range(1, rows):
            copy2(f, k).start()

        @pl.loop(0, bucket)
        def _(j):
            got2[f][row * bucket + j] = got1[f][send_idx[row * bucket + j]]

        for k in range(1, rows):
            copy2(f, k).wait_recv()

        @pl.loop(0, group_tiles, unroll=4)
        def _(i):
            feats[f, i] = got2[f][pick_idx[i]]

        @pl.when(slab < slabs - 1)
        def _():
            copy3(f).start()

    part = group_tiles // 2
    height = part * 16

    def flat(value):
        return value.reshape(height, value.shape[-1])

    @pl.loop(0, 2)
    def _(c):
        at = pl.ds(c * part, part)
        own = [flat(feats[0, at]), flat(feats[1, at])]
        for f in range(frames):
            mixed = own[f].astype(jnp.float32) + b_time[...]
            for lag in range(f + 1):
                mixed = mixed + jnp.dot(
                    own[f - lag], w_time[lag], preferred_element_type=jnp.float32
                )
            total[f, c] = mixed

    for f in range(frames):

        @pl.when(slab > 0)
        def _():
            copy3(f).wait_recv()

        @pl.when(slab == 0)
        def _():
            halo[f] = jnp.zeros(halo.shape[1:], halo.dtype)

    @pl.loop(0, 2)
    def _(c):
        at = pl.ds(c * part, part)
        before = [flat(halo[0, at]), flat(halo[1, at])]
        for f in range(frames):
            mixed = total[f, c]
            for lag in range(f + 1, 3):
                mixed = mixed + jnp.dot(
                    before[2 + f - lag], w_time[lag], preferred_element_type=jnp.float32
                )
            scale = lax.rsqrt(jnp.mean(mixed * mixed, axis=-1, keepdims=True) + 1e-06)
            value = (mixed * scale * gain[...]).astype(jnp.bfloat16)
            out[at, f] = value.reshape(part, 16, value.shape[-1])

    for f in range(frames):
        for k in range(1, slabs):
            copy1(f, k).wait_send()
        for k in range(1, rows):
            copy2(f, k).wait_send()

        @pl.when(slab < slabs - 1)
        def _():
            copy3(f).wait_send()


def body(rows, slabs, pixels, slot_tile, w_space, b_space, w_time, b_time, gain):
    cap, all_frames = pixels.shape[:2]
    channels = w_space.shape[-1]
    group_tiles = cap // 2 * slabs
    per_group = (cap + rows - 1) // rows
    bucket = per_group * 3 * (slabs // 4)
    frames = all_frames // slabs
    send_idx, pick_idx = tables(
        slot_tile, rows, rows, bucket, group_tiles, lax.axis_index("tile")
    )
    spatial = conv_space(pixels, w_space, b_space)
    vmem = pl.BlockSpec(memory_space=pltpu.VMEM)
    smem = pl.BlockSpec(memory_space=pltpu.SMEM)
    bf16 = jnp.bfloat16
    dma = pltpu.SemaphoreType.DMA
    return pl.pallas_call(
        functools.partial(kernel, rows, slabs, cap, bucket, group_tiles),
        out_shape=jax.ShapeDtypeStruct((group_tiles, frames, 16, channels), bf16),
        in_specs=[smem, smem, vmem, vmem, vmem, vmem],
        out_specs=vmem,
        scratch_shapes=[
            pltpu.VMEM((slabs * cap, 16, channels), bf16),
            pltpu.VMEM((slabs * cap, 16, channels), bf16),
            pltpu.VMEM((frames, rows * bucket, 16, channels), bf16),
            pltpu.VMEM((rows * bucket, 16, channels), bf16),
            pltpu.VMEM((rows * bucket, 16, channels), bf16),
            pltpu.VMEM((frames, group_tiles, 16, channels), bf16),
            pltpu.VMEM((frames, group_tiles, 16, channels), bf16),
            pltpu.VMEM((frames, 2, group_tiles * 8, channels), jnp.float32),
            dma((frames, slabs - 1)),
            dma((frames, slabs - 1)),
            dma((frames, rows - 1)),
            dma((frames, rows - 1)),
            dma((frames,)),
            dma((frames,)),
        ],
        compiler_params=pltpu.CompilerParams(collective_id=0, has_side_effects=True),
    )(send_idx, pick_idx, spatial, w_time, b_time[None], gain[None])


def index_row(tiles, rows, cap, bucket, group_tiles, row, half):
    slots = tiles.shape[1]
    width = HALF * cap
    shape = (slots, slots)
    along = lax.broadcasted_iota(jnp.int32, shape, 1)
    down = lax.broadcasted_iota(jnp.int32, shape, 0)
    spread = jnp.broadcast_to(tiles, shape)
    column = jnp.sum(jnp.where(along == down, spread, 0), axis=1, keepdims=True)

    def key_of(ids, tile):
        key = jnp.where(tile < 0, rows, 0)
        for k in range(1, rows):
            key = key + jnp.where(tile >= k * group_tiles, 1, 0)
        block = jnp.zeros_like(ids)
        for k in range(1, slots // width):
            block = block + jnp.where(ids >= k * width, 1, 0)
        return block, key

    ids = lax.broadcasted_iota(jnp.int32, (slots, 1), 0)
    block, group = key_of(ids, column)
    lane = lax.broadcasted_iota(jnp.int32, (1, slots), 1)
    block_r, group_r = key_of(lane, tiles)
    same = (block * (rows + 1) + group) == (block_r * (rows + 1) + group_r)
    rank = jnp.sum(jnp.where(same & (along < down), 1, 0), axis=1, keepdims=True)
    part = block % 2
    arrival = (part * rows + block // 2) * bucket + rank
    inside = ids - block * width
    dev = jnp.zeros_like(ids)
    for k in range(1, HALF):
        dev = dev + jnp.where(inside >= k * cap, 1, 0)
    pos = inside - dev * cap
    came = jnp.where(pos < BASE, dev * BASE + pos, HALF * BASE + pos - BASE)
    came = jnp.where(block == row * 2 + half, inside, came)
    mine = block == row * 2 + half
    other = block == row * 2 + 1 - half
    live = column >= 0
    places = rows * bucket
    target = jnp.where(
        live & (mine | other), group * bucket + rank + jnp.where(other, places, 0), -1
    )
    place = lax.broadcasted_iota(jnp.int32, (1, 128), 1)
    wanted = jnp.where(
        (place >= 2 * places) & (place < 2 * places + group_tiles),
        place - 2 * places + row * group_tiles,
        -2,
    )
    total = jnp.where(target == place, came, 0) + jnp.where(column == wanted, arrival, 0)
    full = mine & live & (pos == BASE)
    total = total + jnp.where(full & (place == 2 * places + group_tiles), dev, 0)
    limit = jnp.where(
        place < places,
        width,
        jnp.where(
            place < 2 * places,
            (HALF + 1) * BASE,
            jnp.where(place < 2 * places + group_tiles, 2 * places, HALF),
        ),
    )
    return jnp.minimum(jnp.sum(total, axis=0, keepdims=True), limit - 1)


def encode(
    rows, slabs, cap, bucket, group_tiles, pieces,
    slot_tile, pixels, w_space, b_space_h, w_time, b_time_h, gain_h,
    out,
    pix, ws, wt, b_space, b_time, gain, tiles, index_v, index, plane, spatial, lat,
    *landing,
):
    frames = 2
    near, far, relay, rec = (
        landing[i * frames * pieces:(i + 1) * frames * pieces] for i in range(4)
    )
    (
        forward_out, packed_n, packed_f,
        in_sem, w_sem, send_n, recv_n, send_f, recv_f, send_x, recv_x,
        send_r, send_yn, recv_yn, send_yf, recv_yf,
    ) = landing[4 * frames * pieces:]
    parts = frames * pieces
    breadth = lat.shape[-1]
    f32, bf16 = jnp.float32, jnp.bfloat16
    row = lax.axis_index("tile")
    slab = lax.axis_index("tm")
    half = lax.div(slab, HALF)
    mine = lax.rem(slab, HALF)
    first = (1 - half) * HALF
    low = half * HALF
    barrier = pltpu.get_barrier_semaphore()
    for k in range(1, slabs):
        pl.semaphore_signal(barrier, inc=1, device_id={"tm": lax.rem(slab + k, slabs)})
    for k in range(1, rows):
        pl.semaphore_signal(barrier, inc=1, device_id={"tile": lax.rem(row + k, rows)})

    steps = slabs // 2
    span = 2 * frames
    origin = lax.div(first, 2)

    def load_frame(z, f):
        return pltpu.make_async_copy(
            pixels.at[:, z * span + f], pix.at[z, f], in_sem.at[z, f]
        )

    def load(z):
        for f in range(span):
            load_frame(z, f).start()

    def conv_at(c):
        return lax.rem(c + 1 - half, steps)

    def mix_at(k):
        return lax.rem(origin + k, steps)

    def conv_before(k):
        return jnp.minimum(k + 2 - half, steps)

    small = [
        pltpu.make_async_copy(source, target, w_sem.at[2 + i])
        for i, (source, target) in enumerate(
            ((slot_tile, tiles), (b_space_h, b_space), (b_time_h, b_time), (gain_h, gain))
        )
    ]
    for copy in small:
        copy.start()
    load(conv_at(0))
    ws_copy = pltpu.make_async_copy(w_space, ws, w_sem.at[0])
    ws_copy.start()
    load(conv_at(1))
    wt_copy = pltpu.make_async_copy(w_time, wt, w_sem.at[1])
    wt_copy.start()

    @pl.loop(2, steps)
    def _(c):
        load(conv_at(c))

    count = span * cap
    side = TILE_SIDE
    out_side = side // 2
    area = out_side * out_side
    height = count * area
    step_rows = height // span
    channels = pix.shape[-1]
    lanes = plane.shape[-1]
    for piece in range(channels // lanes):
        plane[1, piece, :, 8:16] = jnp.zeros((count, 8, lanes), f32)
    spatial[height - 2 * step_rows:height] = jnp.zeros((2 * step_rows, spatial.shape[1]), bf16)
    edge = lax.rem(lax.broadcasted_iota(jnp.int32, (count, area, lanes), 1), out_side) == 0

    def conv(z):
        for f in range(span):
            load_frame(z, f).wait()

        value = pix[z].astype(f32).reshape(count, out_side, 2, side, channels)
        for parity in range(2):
            rows_of = value[:, :, parity].reshape(count, out_side * side, channels)
            for piece in range(channels // lanes):
                plane[parity, piece, :, 16:48] = rows_of[:, :, piece * lanes:(piece + 1) * lanes]

        parts = []
        for a in range(3):
            parity, base = ((1, 8), (0, 16), (1, 16))[a]
            for b in range(3):
                for piece in range(channels // lanes):
                    taken = plane[parity, piece, :, pl.ds(base + b - 1, area, stride=2)]
                    if b == 0:
                        taken = jnp.where(edge, 0.0, taken)
                    parts.append(taken.reshape(height, lanes).astype(bf16))
        patch = jnp.concatenate(parts, axis=1)
        total = jnp.dot(patch, ws[...], preferred_element_type=f32) + b_space[...]
        active = total / (1.0 + jnp.exp(-total))
        spatial[pl.ds(pl.multiple_of((z + 1) * height, height), height)] = active.astype(bf16)

    def mix(z):
        base = (z + 1) * height
        mixed = spatial[pl.ds(pl.multiple_of(base, step_rows), height)].astype(f32) + b_time[...]
        for lag in range(3):
            mixed = mixed + jnp.dot(
                spatial[pl.ds(pl.multiple_of(base - lag * step_rows, step_rows), height)],
                wt[lag],
                preferred_element_type=f32,
            )
        scale = lax.rsqrt(jnp.mean(mixed * mixed, axis=-1, keepdims=True) + 1e-06)
        value = (mixed * scale * gain[...]).astype(bf16)
        for h in range(pieces):
            lat[h, pl.ds(2 * z, 2)] = value[:, h * breadth:(h + 1) * breadth].reshape(
                2, frames, cap, area, breadth
            )

    def near_copy(q, j, source):
        return pltpu.make_async_remote_copy(
            src_ref=lat.at[q % pieces, low + j, q // pieces],
            dst_ref=near[q].at[pl.ds(source * cap, cap)],
            send_sem=send_n.at[q, j],
            recv_sem=recv_n.at[q, source],
            device_id={"tm": low + j},
        )

    def far_copy(q, j, source):
        return pltpu.make_async_remote_copy(
            src_ref=lat.at[q % pieces, first + j, q // pieces, pl.ds(0, BASE)],
            dst_ref=far[q].at[pl.ds(source * BASE, BASE)],
            send_sem=send_f.at[q, j],
            recv_sem=recv_f.at[q, source],
            device_id={"tm": first + j},
        )

    def relay_copy(q, j, source):
        return pltpu.make_async_remote_copy(
            src_ref=lat.at[q % pieces, first + j, q // pieces, pl.ds(BASE, BASE)],
            dst_ref=relay[q].at[source],
            send_sem=send_x.at[q, j],
            recv_sem=recv_x.at[q, source],
            device_id={"tm": low + j},
        )

    def forward(q):
        return pltpu.make_async_remote_copy(
            src_ref=forward_out.at[q],
            dst_ref=far[q].at[pl.ds(HALF * BASE, BASE)],
            send_sem=send_r.at[q],
            recv_sem=recv_f.at[q, HALF],
            device_id={"tm": first + mine},
        )

    pick_at = 2 * rows * bucket
    full_at = pick_at + group_tiles

    def send_near(q, place):
        for side_x in range(2):
            j = 2 * place + side_x

            @pl.when(j != mine)
            def _():
                near_copy(q, j, mine).start()

            @pl.when(j == mine)
            def _():
                near[q][pl.ds(mine * cap, cap)] = lat[q % pieces, slab, q // pieces]

    def send_far(q, place):
        for side_x in range(2):
            far_copy(q, 2 * place + side_x, mine).start()

    def send_relay(q, place):
        for side_x in range(2):
            j = 2 * place + side_x

            @pl.when(j != mine)
            def _():
                relay_copy(q, j, mine).start()

            @pl.when(j == mine)
            def _():
                relay[q][mine] = lat[q % pieces, first + mine, q // pieces, BASE:cap]

    def run_relay(q):
        for k in range(1, HALF):
            relay_copy(q, mine, lax.rem(mine + k, HALF)).wait_recv()
        forward_out[q] = relay[q][index[0, full_at]]
        forward(q).start()


    def tile_near(q, k):
        to = lax.rem(row + k, rows)
        return pltpu.make_async_remote_copy(
            src_ref=packed_n.at[q, pl.ds(to * bucket, bucket)],
            dst_ref=rec[q].at[pl.ds((half * rows + row) * bucket, bucket)],
            send_sem=send_yn.at[q, k - 1],
            recv_sem=recv_yn.at[q, k - 1],
            device_id={"tile": to},
        )

    def tile_far(q, k):
        to = lax.rem(row + k, rows)
        return pltpu.make_async_remote_copy(
            src_ref=packed_f.at[q, pl.ds(to * bucket, bucket)],
            dst_ref=rec[q].at[pl.ds(((1 - half) * rows + row) * bucket, bucket)],
            send_sem=send_yf.at[q, k - 1],
            recv_sem=recv_yf.at[q, k - 1],
            device_id={"tile": to},
        )

    tile_order = sorted(range(1, rows), key=lambda k: k % 2)

    def run_near(q):
        for k in range(1, HALF):
            near_copy(q, mine, lax.rem(mine + k, HALF)).wait_recv()

        @pl.loop(0, rows * bucket, unroll=8)
        def _(i):
            packed_n[q, i] = near[q][index[0, i]]

        for k in tile_order:
            tile_near(q, k).start()
        own = pl.ds(row * bucket, bucket)
        rec[q][pl.ds((half * rows + row) * bucket, bucket)] = packed_n[q, own]

    def run_far(q):
        for j in range(HALF):
            far_copy(q, mine, j).wait_recv()
        forward(q).wait_recv()

        @pl.loop(0, rows * bucket, unroll=8)
        def _(i):
            packed_f[q, i] = far[q][index[0, rows * bucket + i]]

        for k in tile_order:
            tile_far(q, k).start()
        own = pl.ds(row * bucket, bucket)
        rec[q][pl.ds(((1 - half) * rows + row) * bucket, bucket)] = packed_f[q, own]

    for copy in small:
        copy.wait()
    index_v[...] = index_row(tiles[...], rows, cap, bucket, group_tiles, row, half)
    index_copy = pltpu.make_async_copy(index_v, index, w_sem.at[6])
    index_copy.start()
    ws_copy.wait()
    conv(conv_at(0))
    index_copy.wait()
    wt_copy.wait()
    pl.semaphore_wait(barrier, slabs + rows - 2)

    @pl.loop(0, steps)
    def _(k):
        @pl.loop(jnp.where(k == 0, 1, conv_before(k - 1)), conv_before(k))
        def _(c):
            conv(conv_at(c))

        mix(mix_at(k))

        @pl.when(k == 0)
        def _():
            send_relay(0, 0)
            send_relay(1, 0)
            send_far(0, 0)
            send_far(1, 0)

        @pl.when(k == 1)
        def _():
            send_relay(0, 1)
            send_relay(1, 1)
            send_far(0, 1)
            send_far(1, 1)

        @pl.when(k == 2)
        def _():
            send_near(0, 0)
            send_near(1, 0)

        @pl.when(k == 3)
        def _():
            send_near(0, 1)
            send_near(1, 1)
            run_relay(0)
            run_relay(1)

    send_near(2, 0)
    send_near(2, 1)
    send_relay(2, 0)
    send_relay(2, 1)
    send_far(2, 0)
    send_far(2, 1)
    send_relay(3, 0)
    send_relay(3, 1)
    send_near(3, 0)
    send_near(3, 1)
    send_far(3, 0)
    send_far(3, 1)
    run_near(0)
    run_near(1)
    run_far(0)
    run_far(1)
    run_near(2)
    run_relay(2)
    run_far(2)
    run_relay(3)
    run_near(3)
    run_far(3)

    for q in range(parts):
        for k in range(1, rows):
            tile_near(q, k).wait_recv()
            tile_far(q, k).wait_recv()

        @pl.loop(0, group_tiles, unroll=4)
        def _(i):
            h = q % pieces
            out[i, q // pieces, :, h * breadth:(h + 1) * breadth] = rec[q][index[0, pick_at + i]]

    for q in range(parts):
        for k in range(1, HALF):
            near_copy(q, lax.rem(mine + k, HALF), mine).wait_send()
            relay_copy(q, lax.rem(mine + k, HALF), mine).wait_send()
        for j in range(HALF):
            far_copy(q, j, mine).wait_send()
        forward(q).wait_send()
        for k in range(1, rows):
            tile_far(q, k).wait_send()
            tile_near(q, k).wait_send()


def body_two_blocks(rows, slabs, pixels, slot_tile, w_space, b_space, w_time, b_time, gain):
    cap, all_frames, pix_count, channels = pixels.shape
    features = w_space.shape[-1]
    frames = all_frames // slabs
    group_tiles = cap // 2 * slabs
    per_group = (cap + rows - 1) // rows
    bucket = per_group * 3
    area = pix_count // 4
    span = 2 * frames
    steps = slabs // 2
    height = span * cap * area
    vmem = pl.BlockSpec(memory_space=pltpu.VMEM)
    hbm = pl.BlockSpec(memory_space=pl.ANY)
    bf16, f32 = jnp.bfloat16, jnp.float32
    dma = pltpu.SemaphoreType.DMA
    arrivals = (HALF + 1) * BASE
    pieces = 2
    parts = frames * pieces

    def held(*lead):
        return pltpu.VMEM(lead + (area, features // pieces), bf16)

    return pl.pallas_call(
        functools.partial(encode, rows, slabs, cap, bucket, group_tiles, pieces),
        out_shape=jax.ShapeDtypeStruct((group_tiles, frames, area, features), bf16),
        in_specs=[hbm] * 7,
        out_specs=vmem,
        scratch_shapes=[
            pltpu.VMEM((steps, span, cap, pix_count, channels), bf16),
            pltpu.VMEM((9 * channels, features), bf16),
            pltpu.VMEM((3, features, features), bf16),
            pltpu.VMEM((1, features), f32),
            pltpu.VMEM((1, features), f32),
            pltpu.VMEM((1, features), f32),
            pltpu.VMEM((1, slot_tile.shape[0]), jnp.int32),
            pltpu.VMEM((1, 128), jnp.int32),
            pltpu.SMEM((1, 128), jnp.int32),
            pltpu.VMEM((2, channels // 128, span * cap, 48, 128), f32),
            pltpu.VMEM(((steps + 1) * height, features), bf16),
            held(pieces, slabs, frames, cap),
            *[held(HALF * cap)] * parts, *[held(arrivals)] * parts, *[held(HALF, BASE)] * parts,
            *[held(2 * rows * bucket)] * parts,
            held(parts, BASE),
            held(parts, rows * bucket), held(parts, rows * bucket),
            dma((steps, span)), dma((7,)),
            dma((parts, HALF)), dma((parts, HALF)), dma((parts, HALF)), dma((parts, HALF + 1)),
            dma((parts, HALF)), dma((parts, HALF)), dma((parts,)),
            dma((parts, rows - 1)), dma((parts, rows - 1)), dma((parts, rows - 1)), dma((parts, rows - 1)),
        ],
        compiler_params=pltpu.CompilerParams(
            collective_id=1, has_side_effects=True, vmem_limit_bytes=62 << 20
        ),
    )(
        slot_tile[None], pixels, w_space.reshape(9 * channels, features),
        b_space[None], w_time, b_time[None], gain[None],
    )


def solution(mesh):
    rows, slabs = mesh.shape["tile"], mesh.shape["tm"]
    plan = body_two_blocks if slabs == 2 * HALF else body
    return jax.shard_map(
        functools.partial(plan, rows, slabs),
        mesh=mesh,
        in_specs=(P(("tile", "tm"), None, None, None), P(), P(), P(), P(), P(), P()),
        out_specs=P("tile", "tm", None, None),
        check_vma=False,
    )
```

```python
import functools

import jax
import jax.numpy as jnp
from jax import lax
from jax.experimental import pallas as pl
from jax.experimental.pallas import tpu as pltpu
from jax.sharding import PartitionSpec as P

TILE_SIDE = 8
HALF = 4
BASE = 3


def conv_space(raw_tiles, w_space, b_space):
    number, frames, pix_count, channels = raw_tiles.shape
    grid = raw_tiles.reshape(number * frames, TILE_SIDE, TILE_SIDE, channels)
    total = lax.conv_general_dilated(
        grid,
        w_space,
        (2, 2),
        ((1, 1), (1, 1)),
        dimension_numbers=("NHWC", "HWIO", "NHWC"),
        preferred_element_type=jnp.float32,
    )
    active = jax.nn.silu(total + b_space)
    half_side = TILE_SIDE // 2
    return active.astype(jnp.bfloat16).reshape(number, frames, half_side * half_side, -1)


def tables(slot_tile, rows, groups, bucket, group_tiles, my_row):
    table = slot_tile.reshape(rows, -1)
    width = table.shape[1]
    group_of = jnp.where(table >= 0, lax.div(table, group_tiles), groups)
    pos = jnp.arange(width, dtype=jnp.int32)
    earlier = pos[None, :] < pos[:, None]
    same = (group_of[:, :, None] == group_of[:, None, :]) & earlier[None]
    rank = jnp.sum(same.astype(jnp.int32), axis=2)
    target = group_of * bucket + rank
    own_target = lax.dynamic_index_in_dim(target, my_row, 0, keepdims=False)
    own_live = lax.dynamic_index_in_dim(table, my_row, 0, keepdims=False) >= 0
    own_target = jnp.where(own_live, own_target, -1)
    places = jnp.arange(groups * bucket, dtype=jnp.int32)
    send_idx = jnp.sum(
        jnp.where(own_target[None, :] == places[:, None], pos[None, :], 0), axis=1
    )
    wanted = my_row * group_tiles + jnp.arange(group_tiles, dtype=jnp.int32)
    arrived = jnp.arange(rows, dtype=jnp.int32)[:, None] * bucket + rank
    pick_idx = jnp.sum(
        jnp.where(
            table.reshape(-1)[None, :] == wanted[:, None], arrived.reshape(-1)[None, :], 0
        ),
        axis=1,
    )
    return send_idx, pick_idx


def kernel(
    rows, slabs, cap, bucket, group_tiles,
    send_idx, pick_idx, src, w_time, b_time, gain, out,
    got1a, got1b, out2, got2a, got2b, feats, halo, total,
    send1, recv1, send2, recv2, send3, recv3,
):
    frames = 2
    got1, got2 = (got1a, got1b), (got2a, got2b)
    row = lax.axis_index("tile")
    slab = lax.axis_index("tm")
    barrier = pltpu.get_barrier_semaphore()
    for k in range(1, slabs):
        pl.semaphore_signal(barrier, inc=1, device_id={"tm": lax.rem(slab + k, slabs)})
    for k in range(1, rows):
        pl.semaphore_signal(barrier, inc=1, device_id={"tile": lax.rem(row + k, rows)})
    pl.semaphore_wait(barrier, slabs + rows - 2)

    def copy1(f, k):
        to = lax.rem(slab + k, slabs)
        return pltpu.make_async_remote_copy(
            src_ref=src.at[:, to * frames + f],
            dst_ref=got1[f].at[pl.ds(slab * cap, cap)],
            send_sem=send1.at[f, k - 1],
            recv_sem=recv1.at[f, k - 1],
            device_id={"tm": to},
        )

    def copy2(f, k):
        to = lax.rem(row + k, rows)
        return pltpu.make_async_remote_copy(
            src_ref=out2.at[f, pl.ds(to * bucket, bucket)],
            dst_ref=got2[f].at[pl.ds(row * bucket, bucket)],
            send_sem=send2.at[f, k - 1],
            recv_sem=recv2.at[f, k - 1],
            device_id={"tile": to},
        )

    def copy3(f):
        return pltpu.make_async_remote_copy(
            src_ref=feats.at[f],
            dst_ref=halo.at[f],
            send_sem=send3.at[f],
            recv_sem=recv3.at[f],
            device_id={"tm": lax.rem(slab + 1, slabs)},
        )

    for f in range(frames):
        for k in range(1, slabs):
            copy1(f, k).start()
    for f in range(frames):
        got1[f][pl.ds(slab * cap, cap)] = src[:, slab * frames + f]
        for k in range(1, slabs):
            copy1(f, k).wait_recv()

        @pl.loop(0, rows * bucket, unroll=8)
        def _(i):
            out2[f, i] = got1[f][send_idx[i]]

        for k in range(1, rows):
            copy2(f, k).start()

        @pl.loop(0, bucket)
        def _(j):
            got2[f][row * bucket + j] = got1[f][send_idx[row * bucket + j]]

        for k in range(1, rows):
            copy2(f, k).wait_recv()

        @pl.loop(0, group_tiles, unroll=4)
        def _(i):
            feats[f, i] = got2[f][pick_idx[i]]

        @pl.when(slab < slabs - 1)
        def _():
            copy3(f).start()

    part = group_tiles // 2
    height = part * 16

    def flat(value):
        return value.reshape(height, value.shape[-1])

    @pl.loop(0, 2)
    def _(c):
        at = pl.ds(c * part, part)
        own = [flat(feats[0, at]), flat(feats[1, at])]
        for f in range(frames):
            mixed = own[f].astype(jnp.float32) + b_time[...]
            for lag in range(f + 1):
                mixed = mixed + jnp.dot(
                    own[f - lag], w_time[lag], preferred_element_type=jnp.float32
                )
            total[f, c] = mixed

    for f in range(frames):

        @pl.when(slab > 0)
        def _():
            copy3(f).wait_recv()

        @pl.when(slab == 0)
        def _():
            halo[f] = jnp.zeros(halo.shape[1:], halo.dtype)

    @pl.loop(0, 2)
    def _(c):
        at = pl.ds(c * part, part)
        before = [flat(halo[0, at]), flat(halo[1, at])]
        for f in range(frames):
            mixed = total[f, c]
            for lag in range(f + 1, 3):
                mixed = mixed + jnp.dot(
                    before[2 + f - lag], w_time[lag], preferred_element_type=jnp.float32
                )
            scale = lax.rsqrt(jnp.mean(mixed * mixed, axis=-1, keepdims=True) + 1e-06)
            value = (mixed * scale * gain[...]).astype(jnp.bfloat16)
            out[at, f] = value.reshape(part, 16, value.shape[-1])

    for f in range(frames):
        for k in range(1, slabs):
            copy1(f, k).wait_send()
        for k in range(1, rows):
            copy2(f, k).wait_send()

        @pl.when(slab < slabs - 1)
        def _():
            copy3(f).wait_send()


def body(rows, slabs, pixels, slot_tile, w_space, b_space, w_time, b_time, gain):
    cap, all_frames = pixels.shape[:2]
    channels = w_space.shape[-1]
    group_tiles = cap // 2 * slabs
    per_group = (cap + rows - 1) // rows
    bucket = per_group * 3 * (slabs // 4)
    frames = all_frames // slabs
    send_idx, pick_idx = tables(
        slot_tile, rows, rows, bucket, group_tiles, lax.axis_index("tile")
    )
    spatial = conv_space(pixels, w_space, b_space)
    vmem = pl.BlockSpec(memory_space=pltpu.VMEM)
    smem = pl.BlockSpec(memory_space=pltpu.SMEM)
    bf16 = jnp.bfloat16
    dma = pltpu.SemaphoreType.DMA
    return pl.pallas_call(
        functools.partial(kernel, rows, slabs, cap, bucket, group_tiles),
        out_shape=jax.ShapeDtypeStruct((group_tiles, frames, 16, channels), bf16),
        in_specs=[smem, smem, vmem, vmem, vmem, vmem],
        out_specs=vmem,
        scratch_shapes=[
            pltpu.VMEM((slabs * cap, 16, channels), bf16),
            pltpu.VMEM((slabs * cap, 16, channels), bf16),
            pltpu.VMEM((frames, rows * bucket, 16, channels), bf16),
            pltpu.VMEM((rows * bucket, 16, channels), bf16),
            pltpu.VMEM((rows * bucket, 16, channels), bf16),
            pltpu.VMEM((frames, group_tiles, 16, channels), bf16),
            pltpu.VMEM((frames, group_tiles, 16, channels), bf16),
            pltpu.VMEM((frames, 2, group_tiles * 8, channels), jnp.float32),
            dma((frames, slabs - 1)),
            dma((frames, slabs - 1)),
            dma((frames, rows - 1)),
            dma((frames, rows - 1)),
            dma((frames,)),
            dma((frames,)),
        ],
        compiler_params=pltpu.CompilerParams(collective_id=0, has_side_effects=True),
    )(send_idx, pick_idx, spatial, w_time, b_time[None], gain[None])


def index_row(tiles, rows, cap, bucket, group_tiles, row, half):
    slots = tiles.shape[1]
    width = HALF * cap
    shape = (slots, slots)
    along = lax.broadcasted_iota(jnp.int32, shape, 1)
    down = lax.broadcasted_iota(jnp.int32, shape, 0)
    spread = jnp.broadcast_to(tiles, shape)
    column = jnp.sum(jnp.where(along == down, spread, 0), axis=1, keepdims=True)

    def key_of(ids, tile):
        key = jnp.where(tile < 0, rows, 0)
        for k in range(1, rows):
            key = key + jnp.where(tile >= k * group_tiles, 1, 0)
        block = jnp.zeros_like(ids)
        for k in range(1, slots // width):
            block = block + jnp.where(ids >= k * width, 1, 0)
        return block, key

    ids = lax.broadcasted_iota(jnp.int32, (slots, 1), 0)
    block, group = key_of(ids, column)
    lane = lax.broadcasted_iota(jnp.int32, (1, slots), 1)
    block_r, group_r = key_of(lane, tiles)
    same = (block * (rows + 1) + group) == (block_r * (rows + 1) + group_r)
    rank = jnp.sum(jnp.where(same & (along < down), 1, 0), axis=1, keepdims=True)
    part = block % 2
    arrival = (part * rows + block // 2) * bucket + rank
    inside = ids - block * width
    dev = jnp.zeros_like(ids)
    for k in range(1, HALF):
        dev = dev + jnp.where(inside >= k * cap, 1, 0)
    pos = inside - dev * cap
    came = jnp.where(pos < BASE, dev * BASE + pos, HALF * BASE + pos - BASE)
    came = jnp.where(block == row * 2 + half, inside, came)
    mine = block == row * 2 + half
    other = block == row * 2 + 1 - half
    live = column >= 0
    places = rows * bucket
    target = jnp.where(
        live & (mine | other), group * bucket + rank + jnp.where(other, places, 0), -1
    )
    place = lax.broadcasted_iota(jnp.int32, (1, 128), 1)
    wanted = jnp.where(
        (place >= 2 * places) & (place < 2 * places + group_tiles),
        place - 2 * places + row * group_tiles,
        -2,
    )
    total = jnp.where(target == place, came, 0) + jnp.where(column == wanted, arrival, 0)
    full = mine & live & (pos == BASE)
    total = total + jnp.where(full & (place == 2 * places + group_tiles), dev, 0)
    limit = jnp.where(
        place < places,
        width,
        jnp.where(
            place < 2 * places,
            (HALF + 1) * BASE,
            jnp.where(place < 2 * places + group_tiles, 2 * places, HALF),
        ),
    )
    return jnp.minimum(jnp.sum(total, axis=0, keepdims=True), limit - 1)


def encode(
    rows, slabs, cap, bucket, group_tiles, pieces,
    slot_tile, pixels, w_space, b_space_h, w_time, b_time_h, gain_h,
    out,
    pix, ws, wt, b_space, b_time, gain, tiles, index_v, index, plane, spatial, lat,
    *landing,
):
    frames = 2
    near, far, relay, rec = (
        landing[i * frames * pieces:(i + 1) * frames * pieces] for i in range(4)
    )
    (
        forward_out, packed_n, packed_f,
        in_sem, w_sem, send_n, recv_n, send_f, recv_f, send_x, recv_x,
        send_r, send_yn, recv_yn, send_yf, recv_yf, picked, send_out,
    ) = landing[4 * frames * pieces:]
    parts = frames * pieces
    breadth = lat.shape[-1]
    f32, bf16 = jnp.float32, jnp.bfloat16
    row = lax.axis_index("tile")
    slab = lax.axis_index("tm")
    half = lax.div(slab, HALF)
    mine = lax.rem(slab, HALF)
    first = (1 - half) * HALF
    low = half * HALF
    barrier = pltpu.get_barrier_semaphore()
    for k in range(1, slabs):
        pl.semaphore_signal(barrier, inc=1, device_id={"tm": lax.rem(slab + k, slabs)})
    for k in range(1, rows):
        pl.semaphore_signal(barrier, inc=1, device_id={"tile": lax.rem(row + k, rows)})

    steps = slabs // 2
    span = 2 * frames
    origin = lax.div(first, 2)

    def load_frame(z, f):
        return pltpu.make_async_copy(
            pixels.at[:, z * span + f], pix.at[z, f], in_sem.at[z, f]
        )

    def load(z):
        for f in range(span):
            load_frame(z, f).start()

    def conv_at(c):
        return lax.rem(c + 1 - half, steps)

    def mix_at(k):
        return lax.rem(origin + k, steps)

    def conv_before(k):
        return jnp.minimum(k + 2 - half, steps)

    small = [
        pltpu.make_async_copy(source, target, w_sem.at[2 + i])
        for i, (source, target) in enumerate(
            ((slot_tile, tiles), (b_space_h, b_space), (b_time_h, b_time), (gain_h, gain))
        )
    ]
    for copy in small:
        copy.start()
    load(conv_at(0))
    ws_copy = pltpu.make_async_copy(w_space, ws, w_sem.at[0])
    ws_copy.start()
    load(conv_at(1))
    wt_copy = pltpu.make_async_copy(w_time, wt, w_sem.at[1])
    wt_copy.start()

    @pl.loop(2, steps)
    def _(c):
        load(conv_at(c))

    count = span * cap
    side = TILE_SIDE
    out_side = side // 2
    area = out_side * out_side
    height = count * area
    step_rows = height // span
    channels = pix.shape[-1]
    lanes = plane.shape[-1]
    for piece in range(channels // lanes):
        plane[1, piece, :, 8:16] = jnp.zeros((count, 8, lanes), f32)
    spatial[height - 2 * step_rows:height] = jnp.zeros((2 * step_rows, spatial.shape[1]), bf16)
    edge = lax.rem(lax.broadcasted_iota(jnp.int32, (count, area, lanes), 1), out_side) == 0

    def conv(z):
        for f in range(span):
            load_frame(z, f).wait()

        value = pix[z].astype(f32).reshape(count, out_side, 2, side, channels)
        for parity in range(2):
            rows_of = value[:, :, parity].reshape(count, out_side * side, channels)
            for piece in range(channels // lanes):
                plane[parity, piece, :, 16:48] = rows_of[:, :, piece * lanes:(piece + 1) * lanes]

        parts = []
        for a in range(3):
            parity, base = ((1, 8), (0, 16), (1, 16))[a]
            for b in range(3):
                for piece in range(channels // lanes):
                    taken = plane[parity, piece, :, pl.ds(base + b - 1, area, stride=2)]
                    if b == 0:
                        taken = jnp.where(edge, 0.0, taken)
                    parts.append(taken.reshape(height, lanes).astype(bf16))
        patch = jnp.concatenate(parts, axis=1)
        total = jnp.dot(patch, ws[...], preferred_element_type=f32) + b_space[...]
        active = total / (1.0 + jnp.exp(-total))
        spatial[pl.ds(pl.multiple_of((z + 1) * height, height), height)] = active.astype(bf16)

    def mix(z):
        base = (z + 1) * height
        mixed = spatial[pl.ds(pl.multiple_of(base, step_rows), height)].astype(f32) + b_time[...]
        for lag in range(3):
            mixed = mixed + jnp.dot(
                spatial[pl.ds(pl.multiple_of(base - lag * step_rows, step_rows), height)],
                wt[lag],
                preferred_element_type=f32,
            )
        scale = lax.rsqrt(jnp.mean(mixed * mixed, axis=-1, keepdims=True) + 1e-06)
        value = (mixed * scale * gain[...]).astype(bf16)
        for h in range(pieces):
            lat[h, pl.ds(2 * z, 2)] = value[:, h * breadth:(h + 1) * breadth].reshape(
                2, frames, cap, area, breadth
            )

    def store(q):
        h = q % pieces
        return pltpu.make_async_copy(
            picked.at[q],
            out.at[:, q // pieces, :, pl.ds(h * breadth, breadth)],
            send_out.at[q],
        )

    def near_copy(q, j, source):
        return pltpu.make_async_remote_copy(
            src_ref=lat.at[q % pieces, low + j, q // pieces],
            dst_ref=near[q].at[pl.ds(source * cap, cap)],
            send_sem=send_n.at[q, j],
            recv_sem=recv_n.at[q, source],
            device_id={"tm": low + j},
        )

    def far_copy(q, j, source):
        return pltpu.make_async_remote_copy(
            src_ref=lat.at[q % pieces, first + j, q // pieces, pl.ds(0, BASE)],
            dst_ref=far[q].at[pl.ds(source * BASE, BASE)],
            send_sem=send_f.at[q, j],
            recv_sem=recv_f.at[q, source],
            device_id={"tm": first + j},
        )

    def relay_copy(q, j, source):
        return pltpu.make_async_remote_copy(
            src_ref=lat.at[q % pieces, first + j, q // pieces, pl.ds(BASE, BASE)],
            dst_ref=relay[q].at[source],
            send_sem=send_x.at[q, j],
            recv_sem=recv_x.at[q, source],
            device_id={"tm": low + j},
        )

    def forward(q):
        return pltpu.make_async_remote_copy(
            src_ref=forward_out.at[q],
            dst_ref=far[q].at[pl.ds(HALF * BASE, BASE)],
            send_sem=send_r.at[q],
            recv_sem=recv_f.at[q, HALF],
            device_id={"tm": first + mine},
        )

    pick_at = 2 * rows * bucket
    full_at = pick_at + group_tiles

    def send_near(q, place):
        for side_x in range(2):
            j = 2 * place + side_x

            @pl.when(j != mine)
            def _():
                near_copy(q, j, mine).start()

            @pl.when(j == mine)
            def _():
                near[q][pl.ds(mine * cap, cap)] = lat[q % pieces, slab, q // pieces]

    def send_far(q, place):
        for side_x in range(2):
            far_copy(q, 2 * place + side_x, mine).start()

    def send_relay(q, place):
        for side_x in range(2):
            j = 2 * place + side_x

            @pl.when(j != mine)
            def _():
                relay_copy(q, j, mine).start()

            @pl.when(j == mine)
            def _():
                relay[q][mine] = lat[q % pieces, first + mine, q // pieces, BASE:cap]

    def run_relay(q):
        for k in range(1, HALF):
            relay_copy(q, mine, lax.rem(mine + k, HALF)).wait_recv()
        forward_out[q] = relay[q][index[0, full_at]]
        forward(q).start()


    def tile_near(q, k):
        to = lax.rem(row + k, rows)
        return pltpu.make_async_remote_copy(
            src_ref=packed_n.at[q, pl.ds(to * bucket, bucket)],
            dst_ref=rec[q].at[pl.ds((half * rows + row) * bucket, bucket)],
            send_sem=send_yn.at[q, k - 1],
            recv_sem=recv_yn.at[q, k - 1],
            device_id={"tile": to},
        )

    def tile_far(q, k):
        to = lax.rem(row + k, rows)
        return pltpu.make_async_remote_copy(
            src_ref=packed_f.at[q, pl.ds(to * bucket, bucket)],
            dst_ref=rec[q].at[pl.ds(((1 - half) * rows + row) * bucket, bucket)],
            send_sem=send_yf.at[q, k - 1],
            recv_sem=recv_yf.at[q, k - 1],
            device_id={"tile": to},
        )

    tile_order = sorted(range(1, rows), key=lambda k: k % 2)

    def run_near(q):
        for k in range(1, HALF):
            near_copy(q, mine, lax.rem(mine + k, HALF)).wait_recv()

        @pl.loop(0, rows * bucket, unroll=8)
        def _(i):
            packed_n[q, i] = near[q][index[0, i]]

        for k in tile_order:
            tile_near(q, k).start()
        own = pl.ds(row * bucket, bucket)
        rec[q][pl.ds((half * rows + row) * bucket, bucket)] = packed_n[q, own]

    def run_far(q):
        for j in range(HALF):
            far_copy(q, mine, j).wait_recv()
        forward(q).wait_recv()

        @pl.loop(0, rows * bucket, unroll=8)
        def _(i):
            packed_f[q, i] = far[q][index[0, rows * bucket + i]]

        for k in tile_order:
            tile_far(q, k).start()
        own = pl.ds(row * bucket, bucket)
        rec[q][pl.ds(((1 - half) * rows + row) * bucket, bucket)] = packed_f[q, own]

    for copy in small:
        copy.wait()
    index_v[...] = index_row(tiles[...], rows, cap, bucket, group_tiles, row, half)
    index_copy = pltpu.make_async_copy(index_v, index, w_sem.at[6])
    index_copy.start()
    ws_copy.wait()
    conv(conv_at(0))
    index_copy.wait()
    wt_copy.wait()
    pl.semaphore_wait(barrier, slabs + rows - 2)

    @pl.loop(0, steps)
    def _(k):
        @pl.loop(jnp.where(k == 0, 1, conv_before(k - 1)), conv_before(k))
        def _(c):
            conv(conv_at(c))

        mix(mix_at(k))

        @pl.when(k == 0)
        def _():
            send_relay(0, 0)
            send_far(0, 0)
            send_far(1, 0)

        @pl.when(k == 1)
        def _():
            send_relay(0, 1)
            send_far(0, 1)
            send_far(1, 1)
            send_relay(1, 0)
            send_relay(1, 1)

        @pl.when(k == 2)
        def _():
            send_near(0, 0)
            send_near(1, 0)

        @pl.when(k == 3)
        def _():
            send_near(0, 1)
            send_near(1, 1)
            run_relay(0)
            run_relay(1)

    send_near(2, 0)
    send_near(2, 1)
    send_relay(2, 0)
    send_relay(2, 1)
    send_far(2, 0)
    send_far(2, 1)
    send_relay(3, 0)
    send_relay(3, 1)
    send_near(3, 0)
    send_near(3, 1)
    send_far(3, 0)
    send_far(3, 1)
    run_near(0)
    run_near(1)
    run_far(0)
    run_far(1)
    run_near(2)
    run_relay(2)
    run_far(2)
    run_relay(3)
    run_near(3)
    run_far(3)

    for q in range(parts):
        for k in range(1, rows):
            tile_near(q, k).wait_recv()
            tile_far(q, k).wait_recv()

        @pl.loop(0, group_tiles, unroll=4)
        def _(i):
            picked[q, i] = rec[q][index[0, pick_at + i]]

        store(q).start()

    for q in range(parts):
        for k in range(1, HALF):
            near_copy(q, lax.rem(mine + k, HALF), mine).wait_send()
            relay_copy(q, lax.rem(mine + k, HALF), mine).wait_send()
        for j in range(HALF):
            far_copy(q, j, mine).wait_send()
        forward(q).wait_send()
        store(q).wait()
        for k in range(1, rows):
            tile_far(q, k).wait_send()
            tile_near(q, k).wait_send()


def body_two_blocks(rows, slabs, pixels, slot_tile, w_space, b_space, w_time, b_time, gain):
    cap, all_frames, pix_count, channels = pixels.shape
    features = w_space.shape[-1]
    frames = all_frames // slabs
    group_tiles = cap // 2 * slabs
    per_group = (cap + rows - 1) // rows
    bucket = per_group * 3
    area = pix_count // 4
    span = 2 * frames
    steps = slabs // 2
    height = span * cap * area
    vmem = pl.BlockSpec(memory_space=pltpu.VMEM)
    hbm = pl.BlockSpec(memory_space=pl.ANY)
    bf16, f32 = jnp.bfloat16, jnp.float32
    dma = pltpu.SemaphoreType.DMA
    arrivals = (HALF + 1) * BASE
    pieces = 2
    parts = frames * pieces

    def held(*lead):
        return pltpu.VMEM(lead + (area, features // pieces), bf16)

    return pl.pallas_call(
        functools.partial(encode, rows, slabs, cap, bucket, group_tiles, pieces),
        out_shape=jax.ShapeDtypeStruct((group_tiles, frames, area, features), bf16),
        in_specs=[hbm] * 7,
        out_specs=hbm,
        scratch_shapes=[
            pltpu.VMEM((steps, span, cap, pix_count, channels), bf16),
            pltpu.VMEM((9 * channels, features), bf16),
            pltpu.VMEM((3, features, features), bf16),
            pltpu.VMEM((1, features), f32),
            pltpu.VMEM((1, features), f32),
            pltpu.VMEM((1, features), f32),
            pltpu.VMEM((1, slot_tile.shape[0]), jnp.int32),
            pltpu.VMEM((1, 128), jnp.int32),
            pltpu.SMEM((1, 128), jnp.int32),
            pltpu.VMEM((2, channels // 128, span * cap, 48, 128), f32),
            pltpu.VMEM(((steps + 1) * height, features), bf16),
            held(pieces, slabs, frames, cap),
            *[held(HALF * cap)] * parts, *[held(arrivals)] * parts, *[held(HALF, BASE)] * parts,
            *[held(2 * rows * bucket)] * parts,
            held(parts, BASE),
            held(parts, rows * bucket), held(parts, rows * bucket),
            dma((steps, span)), dma((7,)),
            dma((parts, HALF)), dma((parts, HALF)), dma((parts, HALF)), dma((parts, HALF + 1)),
            dma((parts, HALF)), dma((parts, HALF)), dma((parts,)),
            dma((parts, rows - 1)), dma((parts, rows - 1)), dma((parts, rows - 1)), dma((parts, rows - 1)),
            held(parts, group_tiles), dma((parts,)),
        ],
        compiler_params=pltpu.CompilerParams(
            collective_id=1, has_side_effects=True, vmem_limit_bytes=62 << 20
        ),
    )(
        slot_tile[None], pixels, w_space.reshape(9 * channels, features),
        b_space[None], w_time, b_time[None], gain[None],
    )


def solution(mesh):
    rows, slabs = mesh.shape["tile"], mesh.shape["tm"]
    plan = body_two_blocks if slabs == 2 * HALF else body
    return jax.shard_map(
        functools.partial(plan, rows, slabs),
        mesh=mesh,
        in_specs=(P(("tile", "tm"), None, None, None), P(), P(), P(), P(), P(), P()),
        out_specs=P("tile", "tm", None, None),
        check_vma=False,
    )
```

```python
import functools

import jax
import jax.numpy as jnp
from jax import lax
from jax.experimental import pallas as pl
from jax.experimental.pallas import tpu as pltpu
from jax.sharding import PartitionSpec as P

TILE_SIDE = 8
HALF = 4
BASE = 3


def conv_space(raw_tiles, w_space, b_space):
    number, frames, pix_count, channels = raw_tiles.shape
    grid = raw_tiles.reshape(number * frames, TILE_SIDE, TILE_SIDE, channels)
    total = lax.conv_general_dilated(
        grid,
        w_space,
        (2, 2),
        ((1, 1), (1, 1)),
        dimension_numbers=("NHWC", "HWIO", "NHWC"),
        preferred_element_type=jnp.float32,
    )
    active = jax.nn.silu(total + b_space)
    half_side = TILE_SIDE // 2
    return active.astype(jnp.bfloat16).reshape(number, frames, half_side * half_side, -1)


def tables(slot_tile, rows, groups, bucket, group_tiles, my_row):
    table = slot_tile.reshape(rows, -1)
    width = table.shape[1]
    group_of = jnp.where(table >= 0, lax.div(table, group_tiles), groups)
    pos = jnp.arange(width, dtype=jnp.int32)
    earlier = pos[None, :] < pos[:, None]
    same = (group_of[:, :, None] == group_of[:, None, :]) & earlier[None]
    rank = jnp.sum(same.astype(jnp.int32), axis=2)
    target = group_of * bucket + rank
    own_target = lax.dynamic_index_in_dim(target, my_row, 0, keepdims=False)
    own_live = lax.dynamic_index_in_dim(table, my_row, 0, keepdims=False) >= 0
    own_target = jnp.where(own_live, own_target, -1)
    places = jnp.arange(groups * bucket, dtype=jnp.int32)
    send_idx = jnp.sum(
        jnp.where(own_target[None, :] == places[:, None], pos[None, :], 0), axis=1
    )
    wanted = my_row * group_tiles + jnp.arange(group_tiles, dtype=jnp.int32)
    arrived = jnp.arange(rows, dtype=jnp.int32)[:, None] * bucket + rank
    pick_idx = jnp.sum(
        jnp.where(
            table.reshape(-1)[None, :] == wanted[:, None], arrived.reshape(-1)[None, :], 0
        ),
        axis=1,
    )
    return send_idx, pick_idx


def kernel(
    rows, slabs, cap, bucket, group_tiles,
    send_idx, pick_idx, src, w_time, b_time, gain, out,
    got1a, got1b, out2, got2a, got2b, feats, halo, total,
    send1, recv1, send2, recv2, send3, recv3,
):
    frames = 2
    got1, got2 = (got1a, got1b), (got2a, got2b)
    row = lax.axis_index("tile")
    slab = lax.axis_index("tm")
    barrier = pltpu.get_barrier_semaphore()
    for k in range(1, slabs):
        pl.semaphore_signal(barrier, inc=1, device_id={"tm": lax.rem(slab + k, slabs)})
    for k in range(1, rows):
        pl.semaphore_signal(barrier, inc=1, device_id={"tile": lax.rem(row + k, rows)})
    pl.semaphore_wait(barrier, slabs + rows - 2)

    def copy1(f, k):
        to = lax.rem(slab + k, slabs)
        return pltpu.make_async_remote_copy(
            src_ref=src.at[:, to * frames + f],
            dst_ref=got1[f].at[pl.ds(slab * cap, cap)],
            send_sem=send1.at[f, k - 1],
            recv_sem=recv1.at[f, k - 1],
            device_id={"tm": to},
        )

    def copy2(f, k):
        to = lax.rem(row + k, rows)
        return pltpu.make_async_remote_copy(
            src_ref=out2.at[f, pl.ds(to * bucket, bucket)],
            dst_ref=got2[f].at[pl.ds(row * bucket, bucket)],
            send_sem=send2.at[f, k - 1],
            recv_sem=recv2.at[f, k - 1],
            device_id={"tile": to},
        )

    def copy3(f):
        return pltpu.make_async_remote_copy(
            src_ref=feats.at[f],
            dst_ref=halo.at[f],
            send_sem=send3.at[f],
            recv_sem=recv3.at[f],
            device_id={"tm": lax.rem(slab + 1, slabs)},
        )

    for f in range(frames):
        for k in range(1, slabs):
            copy1(f, k).start()
    for f in range(frames):
        got1[f][pl.ds(slab * cap, cap)] = src[:, slab * frames + f]
        for k in range(1, slabs):
            copy1(f, k).wait_recv()

        @pl.loop(0, rows * bucket, unroll=8)
        def _(i):
            out2[f, i] = got1[f][send_idx[i]]

        for k in range(1, rows):
            copy2(f, k).start()

        @pl.loop(0, bucket)
        def _(j):
            got2[f][row * bucket + j] = got1[f][send_idx[row * bucket + j]]

        for k in range(1, rows):
            copy2(f, k).wait_recv()

        @pl.loop(0, group_tiles, unroll=4)
        def _(i):
            feats[f, i] = got2[f][pick_idx[i]]

        @pl.when(slab < slabs - 1)
        def _():
            copy3(f).start()

    part = group_tiles // 2
    height = part * 16

    def flat(value):
        return value.reshape(height, value.shape[-1])

    @pl.loop(0, 2)
    def _(c):
        at = pl.ds(c * part, part)
        own = [flat(feats[0, at]), flat(feats[1, at])]
        for f in range(frames):
            mixed = own[f].astype(jnp.float32) + b_time[...]
            for lag in range(f + 1):
                mixed = mixed + jnp.dot(
                    own[f - lag], w_time[lag], preferred_element_type=jnp.float32
                )
            total[f, c] = mixed

    for f in range(frames):

        @pl.when(slab > 0)
        def _():
            copy3(f).wait_recv()

        @pl.when(slab == 0)
        def _():
            halo[f] = jnp.zeros(halo.shape[1:], halo.dtype)

    @pl.loop(0, 2)
    def _(c):
        at = pl.ds(c * part, part)
        before = [flat(halo[0, at]), flat(halo[1, at])]
        for f in range(frames):
            mixed = total[f, c]
            for lag in range(f + 1, 3):
                mixed = mixed + jnp.dot(
                    before[2 + f - lag], w_time[lag], preferred_element_type=jnp.float32
                )
            scale = lax.rsqrt(jnp.mean(mixed * mixed, axis=-1, keepdims=True) + 1e-06)
            value = (mixed * scale * gain[...]).astype(jnp.bfloat16)
            out[at, f] = value.reshape(part, 16, value.shape[-1])

    for f in range(frames):
        for k in range(1, slabs):
            copy1(f, k).wait_send()
        for k in range(1, rows):
            copy2(f, k).wait_send()

        @pl.when(slab < slabs - 1)
        def _():
            copy3(f).wait_send()


def body(rows, slabs, pixels, slot_tile, w_space, b_space, w_time, b_time, gain):
    cap, all_frames = pixels.shape[:2]
    channels = w_space.shape[-1]
    group_tiles = cap // 2 * slabs
    per_group = (cap + rows - 1) // rows
    bucket = per_group * 3 * (slabs // 4)
    frames = all_frames // slabs
    send_idx, pick_idx = tables(
        slot_tile, rows, rows, bucket, group_tiles, lax.axis_index("tile")
    )
    spatial = conv_space(pixels, w_space, b_space)
    vmem = pl.BlockSpec(memory_space=pltpu.VMEM)
    smem = pl.BlockSpec(memory_space=pltpu.SMEM)
    bf16 = jnp.bfloat16
    dma = pltpu.SemaphoreType.DMA
    return pl.pallas_call(
        functools.partial(kernel, rows, slabs, cap, bucket, group_tiles),
        out_shape=jax.ShapeDtypeStruct((group_tiles, frames, 16, channels), bf16),
        in_specs=[smem, smem, vmem, vmem, vmem, vmem],
        out_specs=vmem,
        scratch_shapes=[
            pltpu.VMEM((slabs * cap, 16, channels), bf16),
            pltpu.VMEM((slabs * cap, 16, channels), bf16),
            pltpu.VMEM((frames, rows * bucket, 16, channels), bf16),
            pltpu.VMEM((rows * bucket, 16, channels), bf16),
            pltpu.VMEM((rows * bucket, 16, channels), bf16),
            pltpu.VMEM((frames, group_tiles, 16, channels), bf16),
            pltpu.VMEM((frames, group_tiles, 16, channels), bf16),
            pltpu.VMEM((frames, 2, group_tiles * 8, channels), jnp.float32),
            dma((frames, slabs - 1)),
            dma((frames, slabs - 1)),
            dma((frames, rows - 1)),
            dma((frames, rows - 1)),
            dma((frames,)),
            dma((frames,)),
        ],
        compiler_params=pltpu.CompilerParams(collective_id=0, has_side_effects=True),
    )(send_idx, pick_idx, spatial, w_time, b_time[None], gain[None])


def index_row(tiles, rows, cap, bucket, group_tiles, row, half):
    slots = tiles.shape[1]
    width = HALF * cap
    shape = (slots, slots)
    along = lax.broadcasted_iota(jnp.int32, shape, 1)
    down = lax.broadcasted_iota(jnp.int32, shape, 0)
    spread = jnp.broadcast_to(tiles, shape)
    column = jnp.sum(jnp.where(along == down, spread, 0), axis=1, keepdims=True)

    def key_of(ids, tile):
        key = jnp.where(tile < 0, rows, 0)
        for k in range(1, rows):
            key = key + jnp.where(tile >= k * group_tiles, 1, 0)
        block = jnp.zeros_like(ids)
        for k in range(1, slots // width):
            block = block + jnp.where(ids >= k * width, 1, 0)
        return block, key

    ids = lax.broadcasted_iota(jnp.int32, (slots, 1), 0)
    block, group = key_of(ids, column)
    lane = lax.broadcasted_iota(jnp.int32, (1, slots), 1)
    block_r, group_r = key_of(lane, tiles)
    same = (block * (rows + 1) + group) == (block_r * (rows + 1) + group_r)
    rank = jnp.sum(jnp.where(same & (along < down), 1, 0), axis=1, keepdims=True)
    part = block % 2
    arrival = (part * rows + block // 2) * bucket + rank
    inside = ids - block * width
    dev = jnp.zeros_like(ids)
    for k in range(1, HALF):
        dev = dev + jnp.where(inside >= k * cap, 1, 0)
    pos = inside - dev * cap
    came = jnp.where(pos < BASE, dev * BASE + pos, HALF * BASE + pos - BASE)
    came = jnp.where(block == row * 2 + half, inside, came)
    mine = block == row * 2 + half
    other = block == row * 2 + 1 - half
    live = column >= 0
    places = rows * bucket
    target = jnp.where(
        live & (mine | other), group * bucket + rank + jnp.where(other, places, 0), -1
    )
    place = lax.broadcasted_iota(jnp.int32, (1, 128), 1)
    wanted = jnp.where(
        (place >= 2 * places) & (place < 2 * places + group_tiles),
        place - 2 * places + row * group_tiles,
        -2,
    )
    total = jnp.where(target == place, came, 0) + jnp.where(column == wanted, arrival, 0)
    full = mine & live & (pos == BASE)
    total = total + jnp.where(full & (place == 2 * places + group_tiles), dev, 0)
    limit = jnp.where(
        place < places,
        width,
        jnp.where(
            place < 2 * places,
            (HALF + 1) * BASE,
            jnp.where(place < 2 * places + group_tiles, 2 * places, HALF),
        ),
    )
    return jnp.minimum(jnp.sum(total, axis=0, keepdims=True), limit - 1)


def encode(
    rows, slabs, cap, bucket, group_tiles, pieces,
    slot_tile, pixels, w_space, b_space_h, w_time, b_time_h, gain_h,
    out,
    pix, ws, wt, b_space, b_time, gain, tiles, index_v, index, plane, spatial, lat,
    *landing,
):
    frames = 2
    near, far, relay, rec = (
        landing[i * frames * pieces:(i + 1) * frames * pieces] for i in range(4)
    )
    (
        forward_out, packed_n, packed_f,
        in_sem, w_sem, send_n, recv_n, send_f, recv_f, send_x, recv_x,
        send_r, send_yn, recv_yn, send_yf, recv_yf, picked, send_out,
    ) = landing[4 * frames * pieces:]
    parts = frames * pieces
    breadth = lat.shape[-1]
    f32, bf16 = jnp.float32, jnp.bfloat16
    row = lax.axis_index("tile")
    slab = lax.axis_index("tm")
    half = lax.div(slab, HALF)
    mine = lax.rem(slab, HALF)
    first = (1 - half) * HALF
    low = half * HALF
    barrier = pltpu.get_barrier_semaphore()
    for k in range(1, slabs):
        pl.semaphore_signal(barrier, inc=1, device_id={"tm": lax.rem(slab + k, slabs)})
    for k in range(1, rows):
        pl.semaphore_signal(barrier, inc=1, device_id={"tile": lax.rem(row + k, rows)})

    steps = slabs // 2
    span = 2 * frames
    origin = lax.div(first, 2)

    def load_frame(z, f):
        return pltpu.make_async_copy(
            pixels.at[:, z * span + f], pix.at[z, f], in_sem.at[z, f]
        )

    def load(z):
        for f in range(span):
            load_frame(z, f).start()

    def conv_at(c):
        return lax.rem(c + 1 - half, steps)

    def mix_at(k):
        return lax.rem(origin + k, steps)

    def conv_before(k):
        return jnp.minimum(k + 2 - half, steps)

    small = [
        pltpu.make_async_copy(source, target, w_sem.at[2 + i])
        for i, (source, target) in enumerate(
            ((slot_tile, tiles), (b_space_h, b_space), (b_time_h, b_time), (gain_h, gain))
        )
    ]
    for copy in small:
        copy.start()
    load(conv_at(0))
    ws_copy = pltpu.make_async_copy(w_space, ws, w_sem.at[0])
    ws_copy.start()
    load(conv_at(1))
    wt_copy = pltpu.make_async_copy(w_time, wt, w_sem.at[1])
    wt_copy.start()

    @pl.loop(2, steps)
    def _(c):
        load(conv_at(c))

    count = span * cap
    side = TILE_SIDE
    out_side = side // 2
    area = out_side * out_side
    height = count * area
    step_rows = height // span
    channels = pix.shape[-1]
    lanes = plane.shape[-1]
    for piece in range(channels // lanes):
        plane[1, piece, :, 8:16] = jnp.zeros((count, 8, lanes), f32)
    spatial[height - 2 * step_rows:height] = jnp.zeros((2 * step_rows, spatial.shape[1]), bf16)
    edge = lax.rem(lax.broadcasted_iota(jnp.int32, (count, area, lanes), 1), out_side) == 0

    def conv(z):
        for f in range(span):
            load_frame(z, f).wait()

        value = pix[z].astype(f32).reshape(count, out_side, 2, side, channels)
        for parity in range(2):
            rows_of = value[:, :, parity].reshape(count, out_side * side, channels)
            for piece in range(channels // lanes):
                plane[parity, piece, :, 16:48] = rows_of[:, :, piece * lanes:(piece + 1) * lanes]

        parts = []
        for a in range(3):
            parity, base = ((1, 8), (0, 16), (1, 16))[a]
            for b in range(3):
                for piece in range(channels // lanes):
                    taken = plane[parity, piece, :, pl.ds(base + b - 1, area, stride=2)]
                    if b == 0:
                        taken = jnp.where(edge, 0.0, taken)
                    parts.append(taken.reshape(height, lanes).astype(bf16))
        patch = jnp.concatenate(parts, axis=1)
        total = jnp.dot(patch, ws[...], preferred_element_type=f32) + b_space[...]
        active = total / (1.0 + jnp.exp(-total))
        spatial[pl.ds(pl.multiple_of((z + 1) * height, height), height)] = active.astype(bf16)

    def mix(z):
        base = (z + 1) * height
        mixed = spatial[pl.ds(pl.multiple_of(base, step_rows), height)].astype(f32) + b_time[...]
        for lag in range(3):
            mixed = mixed + jnp.dot(
                spatial[pl.ds(pl.multiple_of(base - lag * step_rows, step_rows), height)],
                wt[lag],
                preferred_element_type=f32,
            )
        scale = lax.rsqrt(jnp.mean(mixed * mixed, axis=-1, keepdims=True) + 1e-06)
        value = (mixed * scale * gain[...]).astype(bf16)
        for h in range(pieces):
            lat[h, pl.ds(2 * z, 2)] = value[:, h * breadth:(h + 1) * breadth].reshape(
                2, frames, cap, area, breadth
            )

    def store(q):
        h = q % pieces
        return pltpu.make_async_copy(
            picked.at[q],
            out.at[:, q // pieces, :, pl.ds(h * breadth, breadth)],
            send_out.at[q],
        )

    def near_copy(q, j, source):
        return pltpu.make_async_remote_copy(
            src_ref=lat.at[q % pieces, low + j, q // pieces],
            dst_ref=near[q].at[pl.ds(source * cap, cap)],
            send_sem=send_n.at[q, j],
            recv_sem=recv_n.at[q, source],
            device_id={"tm": low + j},
        )

    def far_copy(q, j, source):
        return pltpu.make_async_remote_copy(
            src_ref=lat.at[q % pieces, first + j, q // pieces, pl.ds(0, BASE)],
            dst_ref=far[q].at[pl.ds(source * BASE, BASE)],
            send_sem=send_f.at[q, j],
            recv_sem=recv_f.at[q, source],
            device_id={"tm": first + j},
        )

    def relay_copy(q, j, source):
        return pltpu.make_async_remote_copy(
            src_ref=lat.at[q % pieces, first + j, q // pieces, pl.ds(BASE, BASE)],
            dst_ref=relay[q].at[source],
            send_sem=send_x.at[q, j],
            recv_sem=recv_x.at[q, source],
            device_id={"tm": low + j},
        )

    def forward(q):
        return pltpu.make_async_remote_copy(
            src_ref=forward_out.at[q],
            dst_ref=far[q].at[pl.ds(HALF * BASE, BASE)],
            send_sem=send_r.at[q],
            recv_sem=recv_f.at[q, HALF],
            device_id={"tm": first + mine},
        )

    pick_at = 2 * rows * bucket
    full_at = pick_at + group_tiles

    def send_near(q, place):
        for side_x in range(2):
            j = 2 * place + side_x

            @pl.when(j != mine)
            def _():
                near_copy(q, j, mine).start()

            @pl.when(j == mine)
            def _():
                near[q][pl.ds(mine * cap, cap)] = lat[q % pieces, slab, q // pieces]

    def send_far(q, place):
        for side_x in range(2):
            far_copy(q, 2 * place + side_x, mine).start()

    def send_relay(q, place):
        for side_x in range(2):
            j = 2 * place + side_x

            @pl.when(j != mine)
            def _():
                relay_copy(q, j, mine).start()

            @pl.when(j == mine)
            def _():
                relay[q][mine] = lat[q % pieces, first + mine, q // pieces, BASE:cap]

    def run_relay(q):
        for k in range(1, HALF):
            relay_copy(q, mine, lax.rem(mine + k, HALF)).wait_recv()
        forward_out[q] = relay[q][index[0, full_at]]
        forward(q).start()


    def tile_near(q, k):
        to = lax.rem(row + k, rows)
        return pltpu.make_async_remote_copy(
            src_ref=packed_n.at[q, pl.ds(to * bucket, bucket)],
            dst_ref=rec[q].at[pl.ds((half * rows + row) * bucket, bucket)],
            send_sem=send_yn.at[q, k - 1],
            recv_sem=recv_yn.at[q, k - 1],
            device_id={"tile": to},
        )

    def tile_far(q, k):
        to = lax.rem(row + k, rows)
        return pltpu.make_async_remote_copy(
            src_ref=packed_f.at[q, pl.ds(to * bucket, bucket)],
            dst_ref=rec[q].at[pl.ds(((1 - half) * rows + row) * bucket, bucket)],
            send_sem=send_yf.at[q, k - 1],
            recv_sem=recv_yf.at[q, k - 1],
            device_id={"tile": to},
        )

    tile_order = sorted(range(1, rows), key=lambda k: k % 2)

    def run_near(q):
        for k in range(1, HALF):
            near_copy(q, mine, lax.rem(mine + k, HALF)).wait_recv()

        @pl.loop(0, rows * bucket, unroll=8)
        def _(i):
            packed_n[q, i] = near[q][index[0, i]]

        for k in tile_order:
            tile_near(q, k).start()
        own = pl.ds(row * bucket, bucket)
        rec[q][pl.ds((half * rows + row) * bucket, bucket)] = packed_n[q, own]

    def run_far(q):
        for j in range(HALF):
            far_copy(q, mine, j).wait_recv()
        forward(q).wait_recv()

        @pl.loop(0, rows * bucket, unroll=8)
        def _(i):
            packed_f[q, i] = far[q][index[0, rows * bucket + i]]

        for k in tile_order:
            tile_far(q, k).start()
        own = pl.ds(row * bucket, bucket)
        rec[q][pl.ds(((1 - half) * rows + row) * bucket, bucket)] = packed_f[q, own]

    for copy in small:
        copy.wait()
    index_v[...] = index_row(tiles[...], rows, cap, bucket, group_tiles, row, half)
    index_copy = pltpu.make_async_copy(index_v, index, w_sem.at[6])
    index_copy.start()
    ws_copy.wait()
    conv(conv_at(0))
    index_copy.wait()
    wt_copy.wait()
    pl.semaphore_wait(barrier, slabs + rows - 2)

    @pl.loop(0, steps)
    def _(k):
        @pl.loop(jnp.where(k == 0, 1, conv_before(k - 1)), conv_before(k))
        def _(c):
            conv(conv_at(c))

        mix(mix_at(k))

        @pl.when(k == 0)
        def _():
            send_relay(0, 0)
            send_far(0, 0)
            send_far(1, 0)

        @pl.when(k == 1)
        def _():
            send_relay(0, 1)
            send_far(0, 1)
            send_far(1, 1)
            send_relay(1, 0)
            send_relay(1, 1)

        @pl.when(k == 2)
        def _():
            send_near(0, 0)

        @pl.when(k == 3)
        def _():
            send_near(0, 1)
            run_relay(0)

    send_near(1, 0)
    send_near(1, 1)
    run_relay(1)
    send_near(2, 0)
    send_near(2, 1)
    send_relay(2, 0)
    send_relay(2, 1)
    send_far(2, 0)
    send_far(2, 1)
    send_relay(3, 0)
    send_relay(3, 1)
    send_near(3, 0)
    send_near(3, 1)
    send_far(3, 0)
    send_far(3, 1)
    run_near(0)
    run_near(1)
    run_far(0)
    run_far(1)
    run_near(2)
    run_relay(2)
    run_far(2)
    run_relay(3)
    run_near(3)
    run_far(3)

    for q in range(parts):
        for k in range(1, rows):
            tile_near(q, k).wait_recv()
            tile_far(q, k).wait_recv()

        @pl.loop(0, group_tiles, unroll=4)
        def _(i):
            picked[q, i] = rec[q][index[0, pick_at + i]]

        store(q).start()

    for q in range(parts):
        for k in range(1, HALF):
            near_copy(q, lax.rem(mine + k, HALF), mine).wait_send()
            relay_copy(q, lax.rem(mine + k, HALF), mine).wait_send()
        for j in range(HALF):
            far_copy(q, j, mine).wait_send()
        forward(q).wait_send()
        store(q).wait()
        for k in range(1, rows):
            tile_far(q, k).wait_send()
            tile_near(q, k).wait_send()


def body_two_blocks(rows, slabs, pixels, slot_tile, w_space, b_space, w_time, b_time, gain):
    cap, all_frames, pix_count, channels = pixels.shape
    features = w_space.shape[-1]
    frames = all_frames // slabs
    group_tiles = cap // 2 * slabs
    per_group = (cap + rows - 1) // rows
    bucket = per_group * 3
    area = pix_count // 4
    span = 2 * frames
    steps = slabs // 2
    height = span * cap * area
    vmem = pl.BlockSpec(memory_space=pltpu.VMEM)
    hbm = pl.BlockSpec(memory_space=pl.ANY)
    bf16, f32 = jnp.bfloat16, jnp.float32
    dma = pltpu.SemaphoreType.DMA
    arrivals = (HALF + 1) * BASE
    pieces = 2
    parts = frames * pieces

    def held(*lead):
        return pltpu.VMEM(lead + (area, features // pieces), bf16)

    return pl.pallas_call(
        functools.partial(encode, rows, slabs, cap, bucket, group_tiles, pieces),
        out_shape=jax.ShapeDtypeStruct((group_tiles, frames, area, features), bf16),
        in_specs=[hbm] * 7,
        out_specs=hbm,
        scratch_shapes=[
            pltpu.VMEM((steps, span, cap, pix_count, channels), bf16),
            pltpu.VMEM((9 * channels, features), bf16),
            pltpu.VMEM((3, features, features), bf16),
            pltpu.VMEM((1, features), f32),
            pltpu.VMEM((1, features), f32),
            pltpu.VMEM((1, features), f32),
            pltpu.VMEM((1, slot_tile.shape[0]), jnp.int32),
            pltpu.VMEM((1, 128), jnp.int32),
            pltpu.SMEM((1, 128), jnp.int32),
            pltpu.VMEM((2, channels // 128, span * cap, 48, 128), f32),
            pltpu.VMEM(((steps + 1) * height, features), bf16),
            held(pieces, slabs, frames, cap),
            *[held(HALF * cap)] * parts, *[held(arrivals)] * parts, *[held(HALF, BASE)] * parts,
            *[held(2 * rows * bucket)] * parts,
            held(parts, BASE),
            held(parts, rows * bucket), held(parts, rows * bucket),
            dma((steps, span)), dma((7,)),
            dma((parts, HALF)), dma((parts, HALF)), dma((parts, HALF)), dma((parts, HALF + 1)),
            dma((parts, HALF)), dma((parts, HALF)), dma((parts,)),
            dma((parts, rows - 1)), dma((parts, rows - 1)), dma((parts, rows - 1)), dma((parts, rows - 1)),
            held(parts, group_tiles), dma((parts,)),
        ],
        compiler_params=pltpu.CompilerParams(
            collective_id=1, has_side_effects=True, vmem_limit_bytes=62 << 20
        ),
    )(
        slot_tile[None], pixels, w_space.reshape(9 * channels, features),
        b_space[None], w_time, b_time[None], gain[None],
    )


def solution(mesh):
    rows, slabs = mesh.shape["tile"], mesh.shape["tm"]
    plan = body_two_blocks if slabs == 2 * HALF else body
    return jax.shard_map(
        functools.partial(plan, rows, slabs),
        mesh=mesh,
        in_specs=(P(("tile", "tm"), None, None, None), P(), P(), P(), P(), P(), P()),
        out_specs=P("tile", "tm", None, None),
        check_vma=False,
    )
```
